32 devices in a mesh: dp: 16 (over z, x, core), seq: 2 (over y).
Axes of the slice: x: 2, y: 2, z: 4, core: 2. Of those that a mesh axis runs over, the one named last changes fastest.
Arguments:
- frames_in: bfloat16 [16, 1500, 768], P('dp', 'seq'), may hold values from -6 to 6
- ln1_gain: bfloat16 [768], P('dp'), may hold values from 0.25 to 1.75
- ln1_bias: bfloat16 [768], P('dp'), may hold values from -1.75 to 1.75
- w_qkv: bfloat16 [768, 2304], P('dp'), may hold values from -2 to 2
- b_qv: bfloat16 [1536], P('dp'), may hold values from -1.25 to 1.25
- w_o: bfloat16 [768, 768], P('dp'), may hold values from -0.875 to 0.875
- b_o: bfloat16 [768], P('dp'), may hold values from -1.75 to 1.75
- ln2_gain: bfloat16 [768], P('dp'), may hold values from 0.25 to 1.75
- ln2_bias: bfloat16 [768], P('dp'), may hold values from -1.75 to 1.75
- w_fc1: bfloat16 [768, 3072], P('dp'), may hold values from -0.21875 to 0.21875
- b_fc1: bfloat16 [3072], P('dp'), may hold values from -3 to 3
- w_fc2: bfloat16 [3072, 768], P('dp'), may hold values from -0.109375 to 0.109375
- b_fc2: bfloat16 [768], P('dp'), may hold values from -1.75 to 1.75
- cotangent: bfloat16 [16, 1500, 768], P('dp', 'seq'), may hold values from -6 to 6
Outputs:
- frames_out: bfloat16 [16, 1500, 768], P('dp', 'seq')
- grad_frames: float32 [16, 1500, 768], P('dp', 'seq')
- grad_ln1_gain: float32 [768], P('dp')
- grad_ln1_bias: float32 [768], P('dp')
- grad_w_qkv: float32 [768, 2304], P('dp')
- grad_b_qv: float32 [1536], P('dp')
- grad_w_o: float32 [768, 768], P('dp')
- grad_b_o: float32 [768], P('dp')
- grad_ln2_gain: float32 [768], P('dp')
- grad_ln2_bias: float32 [768], P('dp')
- grad_w_fc1: float32 [768, 3072], P('dp')
- grad_b_fc1: float32 [3072], P('dp')
- grad_w_fc2: float32 [3072, 768], P('dp')
- grad_b_fc2: float32 [768], P('dp')
The draws below stay inside these ranges and needn't reach their ends.
All inputs are finite; a program needn't handle non-finite values.
Results may differ from the reference program's by a relative error of at most 0.0095.
Values may be sent and summed in bfloat16 or wider, within the bound.
No kernel may reach another device: no remote copies, remote signals or barrier semaphores. Data moves between devices by JAX's collectives and lax.ppermute only.
A program may use at most 192 MiB of HBM per device.

```python
import math
import jax
import jax.numpy as jnp
from jax import lax

D = 768
HEADS = 12
FF = 3072
FRAMES = 1500
CLIPS = 16


def draw_w_qkv(key, part):
    base = jax.random.truncated_normal(key, -2.5, 2.5, (D, 3 * D), jnp.float32) * (1.0 / math.sqrt(D))
    return base.astype(jnp.bfloat16)


def block_levels(own_key, extent, cuts, smallest, largest):
    level, own = 1.0, jax.random.fold_in(own_key, 6)
    for position, parts in cuts:
        steps = jnp.exp(jax.random.uniform(jax.random.fold_in(own, position), (parts,), jnp.float32, smallest / len(cuts), largest / len(cuts)))
        level = level * jnp.repeat(steps, extent[position] // parts).reshape([-1 if axis == position else 1 for axis in range(len(extent))])
    return level


def gaussian(stream_key, dims, spread, most, shards=(), kind=jnp.bfloat16):
    entries = spread * jax.random.normal(stream_key, dims, jnp.float32)
    if shards:
        entries = entries * block_levels(stream_key, dims, shards, -0.22, 0.18)
    return jnp.clip(entries, -most, most).astype(kind)


def setup_inputs(seed: int = 0) -> dict:
    keys = jax.random.split(jax.random.key(seed), 15)
    frames_in = gaussian(keys[0], (CLIPS, FRAMES, D), 1.0, 6.0, ((0, 16), (1, 2)))
    ln1_gain = jnp.clip(1.0 + 0.15 * jax.random.normal(keys[1], (D,), jnp.float32), 0.25, 1.75).astype(jnp.bfloat16)
    ln1_bias = gaussian(keys[2], (D,), 0.3, 1.75, ((0, 16),))
    w_qkv = draw_w_qkv(jax.random.fold_in(keys[14], 71), 0)
    b_qv = gaussian(keys[4], (2 * D,), 0.2, 1.25, ((0, 16),))
    w_o = gaussian(keys[5], (D, D), (D // 16) ** -0.5, 0.875, ((0, 16),))
    b_o = gaussian(keys[6], (D,), 0.3, 1.75, ((0, 16),))
    ln2_gain = jnp.clip(1.0 + 0.15 * jax.random.normal(keys[7], (D,), jnp.float32), 0.25, 1.75).astype(jnp.bfloat16)
    ln2_bias = gaussian(keys[8], (D,), 0.3, 1.75, ((0, 16),))
    w_fc1 = gaussian(keys[9], (D, FF), D ** -0.5, 0.21875, ((0, 16),))
    b_fc1 = gaussian(keys[10], (FF,), 0.5, 3.0, ((0, 16),))
    w_fc2 = gaussian(keys[11], (FF, D), FF ** -0.5, 0.109375, ((0, 16),))
    b_fc2 = gaussian(keys[12], (D,), 0.3, 1.75, ((0, 16),))
    cotangent = gaussian(keys[13], (CLIPS, FRAMES, D), 1.0, 6.0, ((0, 16), (1, 2)))
    return dict(frames_in=frames_in, ln1_gain=ln1_gain, ln1_bias=ln1_bias, w_qkv=w_qkv, b_qv=b_qv, w_o=w_o, b_o=b_o, ln2_gain=ln2_gain, ln2_bias=ln2_bias, w_fc1=w_fc1, b_fc1=b_fc1, w_fc2=w_fc2, b_fc2=b_fc2, cotangent=cotangent)


EPSILON = 1e-05

def normalize(values, gain, shift):
    center = lax.optimization_barrier(jnp.mean(values, axis=-1, keepdims=True))
    centered = values - center
    variance = lax.optimization_barrier(jnp.mean(centered * centered, axis=-1, keepdims=True))
    inverse = lax.rsqrt(variance + EPSILON)
    normed = centered * inverse
    return (normed, inverse, normed * gain + shift)

def norm_back(grad_out, normed, inverse, gain):
    weighted = grad_out * gain
    first = lax.optimization_barrier(jnp.mean(weighted, axis=-1, keepdims=True))
    second = lax.optimization_barrier(jnp.mean(weighted * normed, axis=-1, keepdims=True))
    return inverse * (weighted - first - normed * second)

def gelu_cdf(values):
    return 0.5 * (1.0 + lax.erf(values * (1.0 / math.sqrt(2.0))))

def gelu_slope(values):
    density = jnp.exp(-0.5 * values * values) * (1.0 / math.sqrt(2.0 * math.pi))
    return gelu_cdf(values) + values * density

def head_forward(operands):
    query, key_rows, value_rows = operands
    factor = 1.0 / math.sqrt(query.shape[-1])
    scores = jnp.dot(query, key_rows.T, preferred_element_type=jnp.float32) * factor
    row_peak = lax.optimization_barrier(jnp.max(scores, axis=-1, keepdims=True))
    row_total = lax.optimization_barrier(jnp.sum(jnp.exp(scores - row_peak), axis=-1, keepdims=True))
    logsum = row_peak + jnp.log(row_total)
    weights_low = jnp.exp(scores - logsum).astype(jnp.bfloat16)
    context = jnp.dot(weights_low, value_rows, preferred_element_type=jnp.float32).astype(jnp.bfloat16)
    return (context, logsum[:, 0])

def head_backward(operands):
    query, key_rows, value_rows, context, grad_context, logsum = operands
    factor = 1.0 / math.sqrt(query.shape[-1])
    scores = jnp.dot(query, key_rows.T, preferred_element_type=jnp.float32) * factor
    weights_full = jnp.exp(scores - logsum[:, None])
    weights_low = weights_full.astype(jnp.bfloat16)
    grad_values = jnp.dot(weights_low.T, grad_context, preferred_element_type=jnp.float32).astype(jnp.bfloat16)
    grad_weights = jnp.dot(grad_context, value_rows.T, preferred_element_type=jnp.float32)
    delta = lax.optimization_barrier(jnp.sum(grad_context.astype(jnp.float32) * context.astype(jnp.float32), axis=-1, keepdims=True))
    grad_scores = (weights_full * (grad_weights - delta)).astype(jnp.bfloat16)
    grad_query = (jnp.dot(grad_scores, key_rows, preferred_element_type=jnp.float32) * factor).astype(jnp.bfloat16)
    grad_keys = (jnp.dot(grad_scores.T, query, preferred_element_type=jnp.float32) * factor).astype(jnp.bfloat16)
    return (grad_query, grad_keys, grad_values)

def reference(frames_in, ln1_gain, ln1_bias, w_qkv, b_qv, w_o, b_o, ln2_gain, ln2_bias, w_fc1, b_fc1, w_fc2, b_fc2, cotangent):
    head_size = D // HEADS
    gain_one = ln1_gain.astype(jnp.float32)
    shift_one = ln1_bias.astype(jnp.float32)
    gain_two = ln2_gain.astype(jnp.float32)
    shift_two = ln2_bias.astype(jnp.float32)
    bias_wide = b_qv.astype(jnp.float32)
    bias_out = b_o.astype(jnp.float32)
    bias_fc1 = b_fc1.astype(jnp.float32)
    bias_fc2 = b_fc2.astype(jnp.float32)

    def split_heads(block):
        return block.reshape(FRAMES, HEADS, head_size).transpose(1, 0, 2)

    def join_heads(block):
        return block.transpose(1, 0, 2).reshape(FRAMES, D)

    def one_clip(totals, operands):
        clip_in, clip_grad = operands
        inputs = clip_in.astype(jnp.float32)
        normed_one, inverse_one, hidden_one = normalize(inputs, gain_one, shift_one)
        hidden_one = hidden_one.astype(jnp.bfloat16)
        projected = jnp.dot(hidden_one, w_qkv, preferred_element_type=jnp.float32)
        query = (projected[:, :D] + bias_wide[:D]).astype(jnp.bfloat16)
        key_rows = projected[:, D:2 * D].astype(jnp.bfloat16)
        value_rows = (projected[:, 2 * D:] + bias_wide[D:]).astype(jnp.bfloat16)
        query_heads = split_heads(query)
        key_heads = split_heads(key_rows)
        value_heads = split_heads(value_rows)
        context_heads, logsum = lax.map(head_forward, (query_heads, key_heads, value_heads))
        context_heads = lax.optimization_barrier(context_heads)
        context = join_heads(context_heads)
        residual = inputs + jnp.dot(context, w_o, preferred_element_type=jnp.float32) + bias_out
        normed_two, inverse_two, hidden_two = normalize(residual, gain_two, shift_two)
        hidden_two = hidden_two.astype(jnp.bfloat16)
        pre_act = jnp.dot(hidden_two, w_fc1, preferred_element_type=jnp.float32) + bias_fc1
        activated = (pre_act * gelu_cdf(pre_act)).astype(jnp.bfloat16)
        output = residual + jnp.dot(activated, w_fc2, preferred_element_type=jnp.float32) + bias_fc2
        clip_out = output.astype(jnp.bfloat16)
        grad_full = clip_grad.astype(jnp.float32)
        grad_bias_fc2 = lax.optimization_barrier(jnp.sum(grad_full, axis=0))
        grad_weight_fc2 = jnp.dot(activated.T, clip_grad, preferred_element_type=jnp.float32)
        grad_pre = jnp.dot(clip_grad, w_fc2.T, preferred_element_type=jnp.float32) * gelu_slope(pre_act)
        grad_bias_fc1 = lax.optimization_barrier(jnp.sum(grad_pre, axis=0))
        grad_pre_low = grad_pre.astype(jnp.bfloat16)
        grad_weight_fc1 = jnp.dot(hidden_two.T, grad_pre_low, preferred_element_type=jnp.float32)
        grad_hidden_two = jnp.dot(grad_pre_low, w_fc1.T, preferred_element_type=jnp.float32)
        grad_gain_two = lax.optimization_barrier(jnp.sum(grad_hidden_two * normed_two, axis=0))
        grad_shift_two = lax.optimization_barrier(jnp.sum(grad_hidden_two, axis=0))
        grad_residual = grad_full + norm_back(grad_hidden_two, normed_two, inverse_two, gain_two)
        grad_bias_out = lax.optimization_barrier(jnp.sum(grad_residual, axis=0))
        grad_residual_low = grad_residual.astype(jnp.bfloat16)
        grad_weight_out = jnp.dot(context.T, grad_residual_low, preferred_element_type=jnp.float32)
        grad_context = jnp.dot(grad_residual_low, w_o.T, preferred_element_type=jnp.float32).astype(jnp.bfloat16)
        grad_context = lax.optimization_barrier(grad_context)
        back_heads = lax.map(head_backward, (query_heads, key_heads, value_heads, context_heads, split_heads(grad_context), logsum))
        back_heads = lax.optimization_barrier(back_heads)
        grad_query = join_heads(back_heads[0])
        grad_keys = join_heads(back_heads[1])
        grad_values = join_heads(back_heads[2])
        grad_bias_qv = jnp.concatenate([lax.optimization_barrier(jnp.sum(grad_query.astype(jnp.float32), axis=0)), lax.optimization_barrier(jnp.sum(grad_values.astype(jnp.float32), axis=0))])
        grad_projected = jnp.concatenate([grad_query, grad_keys, grad_values], axis=1)
        grad_weight_qkv = jnp.dot(hidden_one.T, grad_projected, preferred_element_type=jnp.float32)
        grad_hidden_one = jnp.dot(grad_projected, w_qkv.T, preferred_element_type=jnp.float32)
        grad_gain_one = lax.optimization_barrier(jnp.sum(grad_hidden_one * normed_one, axis=0))
        grad_shift_one = lax.optimization_barrier(jnp.sum(grad_hidden_one, axis=0))
        grad_input = grad_residual + norm_back(grad_hidden_one, normed_one, inverse_one, gain_one)
        terms = (grad_gain_one, grad_shift_one, grad_weight_qkv, grad_bias_qv, grad_weight_out, grad_bias_out, grad_gain_two, grad_shift_two, grad_weight_fc1, grad_bias_fc1, grad_weight_fc2, grad_bias_fc2)
        return (jax.tree.map(jnp.add, totals, terms), (clip_out, grad_input))
    zeros = (jnp.zeros((D,), jnp.float32), jnp.zeros((D,), jnp.float32), jnp.zeros((D, 3 * D), jnp.float32), jnp.zeros((2 * D,), jnp.float32), jnp.zeros((D, D), jnp.float32), jnp.zeros((D,), jnp.float32), jnp.zeros((D,), jnp.float32), jnp.zeros((D,), jnp.float32), jnp.zeros((D, FF), jnp.float32), jnp.zeros((FF,), jnp.float32), jnp.zeros((FF, D), jnp.float32), jnp.zeros((D,), jnp.float32))
    totals, outputs = lax.scan(one_clip, zeros, (frames_in, cotangent))
    frames_out, grad_frames = outputs
    return (frames_out, grad_frames, totals[0], totals[1], totals[2], totals[3], totals[4], totals[5], totals[6], totals[7], totals[8], totals[9], totals[10], totals[11])
```

```python
import functools
import math

import jax
import jax.numpy as jnp
from jax import lax
from jax.experimental import pallas as pl
from jax.experimental.pallas import tpu as pltpu
from jax.sharding import PartitionSpec as P

HEADS = 12
EPSILON = 1e-05
BF = jnp.bfloat16
F32 = jnp.float32
MASKED = -1e30


def dot(a, b, ca=1, cb=0):
    return lax.dot_general(a, b, (((ca,), (cb,)), ((), ())), preferred_element_type=F32)


def split3(x):
    high = x.astype(BF).astype(F32)
    rest = x - high
    mid = rest.astype(BF).astype(F32)
    return high, mid, (rest - mid).astype(BF).astype(F32)


def forward_kernel(half, valid, q_ref, k_ref, v_ref, o_ref, lse_ref, kx_ref, vt_ref):
    rows = k_ref.shape[0]
    wide = q_ref.shape[0]

    @pl.when(pl.program_id(1) == 0)
    def _():
        kx_ref[:, :128] = k_ref[...]
        row = lax.broadcasted_iota(jnp.int32, (rows, 128), 0)
        lane = lax.broadcasted_iota(jnp.int32, (rows, 128), 1)
        padded = (lax.rem(row, half) >= valid) & (lane == 0)
        kx_ref[:, 128:] = jnp.where(padded, MASKED, 0.0).astype(BF)
        vt = v_ref[...].T
        vt_ref[0:64, :] = vt[0:64, :]
        vt_ref[64:80, :] = jnp.ones((16, rows), BF)
        vt_ref[80:144, :] = vt[64:128, :]
        vt_ref[144:160, :] = jnp.ones((16, rows), BF)

    lane = lax.broadcasted_iota(jnp.int32, (wide, 128), 1)
    q = q_ref[...] * jnp.asarray(0.125, BF)
    one = jnp.where(lane == 0, 1.0, 0.0).astype(BF)
    outs, sums = [], []
    for h in range(2):
        mine = (lane < 64) if h == 0 else (lane >= 64)
        qx = jnp.concatenate([jnp.where(mine, q, jnp.zeros_like(q)), one], axis=1)
        s = dot(kx_ref[...], qx, 1, 1)
        peak = jnp.max(s, axis=0, keepdims=True)
        p = jnp.exp(s - peak).astype(BF)
        o = dot(vt_ref[80 * h : 80 * h + 80, :], p)
        total = o[64:65, :]
        outs.append(o[0:64, :] / total)
        sums.append(peak + jnp.log(total))
    o_ref[...] = jnp.concatenate(outs, axis=0).T.astype(BF)
    lse_ref[...] = jnp.concatenate(sums + [jnp.zeros((6, wide), F32)], axis=0)[None]


def attention_forward(qkv, half, valid, wide):
    rows, width = qkv.shape
    pairs = width // 3 // 128
    return pl.pallas_call(
        functools.partial(forward_kernel, half, valid),
        grid=(pairs, rows // wide),
        in_specs=[
            pl.BlockSpec((wide, 128), lambda p, i: (i, p)),
            pl.BlockSpec((rows, 128), lambda p, i: (0, pairs + p)),
            pl.BlockSpec((rows, 128), lambda p, i: (0, 2 * pairs + p)),
        ],
        out_specs=[
            pl.BlockSpec((wide, 128), lambda p, i: (i, p)),
            pl.BlockSpec((1, 8, wide), lambda p, i: (p, 0, i)),
        ],
        out_shape=[
            jax.ShapeDtypeStruct((rows, pairs * 128), BF),
            jax.ShapeDtypeStruct((pairs, 8, rows), F32),
        ],
        scratch_shapes=[pltpu.VMEM((rows, 256), BF), pltpu.VMEM((160, rows), BF)],
        cost_estimate=pl.CostEstimate(
            flops=pairs * 2 * 4 * rows * rows * 256,
            bytes_accessed=rows * width * 2 + rows * width,
            transcendentals=pairs * 2 * rows * rows,
        ),
        name="attention_forward",
    )(qkv, qkv, qkv)


def backward_kernel(
    half, valid, q_ref, k_ref, v_ref, o_ref, do_ref, lse_ref,
    dq_ref, dk_ref, dv_ref, kt_ref, vt_ref, dkt_ref, dvt_ref,
):
    rows = k_ref.shape[0]
    wide = q_ref.shape[0]

    @pl.when(pl.program_id(1) == 0)
    def _():
        kt_ref[0:128, :] = k_ref[...].T
        vt_ref[0:128, :] = v_ref[...].T
        row = lax.broadcasted_iota(jnp.int32, (128, rows), 0)
        key = lax.broadcasted_iota(jnp.int32, (128, rows), 1)
        bias = jnp.where(lax.rem(key, half) >= valid, MASKED, 0.0)
        ones = jnp.where((row >= 1) & (row < 4), 1.0, 0.0)
        kt_ref[128:256, :] = jnp.where(row == 0, bias, ones).astype(BF)
        vt_ref[128:256, :] = ones.astype(BF)
        dkt_ref[...] = jnp.zeros_like(dkt_ref)
        dvt_ref[...] = jnp.zeros_like(dvt_ref)

    lane = lax.broadcasted_iota(jnp.int32, (wide, 128), 1)
    q = q_ref[...] * jnp.asarray(0.125, BF)
    do = do_ref[...]
    product = do.astype(F32) * o_ref[...].astype(F32)
    lse = lse_ref[0].T
    qt, dot_t = q.T, do.T

    def extra(x, first):
        a, b, c = split3(-x)
        tail = jnp.where(lane == 2, b, jnp.where(lane == 3, c, 0.0))
        return jnp.where(lane == 0, first, jnp.where(lane == 1, a, tail)).astype(BF)

    dq = []
    for h in range(2):
        mine = (lane < 64) if h == 0 else (lane >= 64)
        delta = jnp.sum(jnp.where(mine, product, 0.0), axis=1, keepdims=True)
        qx = jnp.concatenate(
            [jnp.where(mine, q, jnp.zeros_like(q)), extra(lse[:, h : h + 1], 1.0)], axis=1
        )
        dx = jnp.concatenate([jnp.where(mine, do, jnp.zeros_like(do)), extra(delta, 0.0)], axis=1)
        p = jnp.exp(dot(qx, kt_ref[...]))
        low = p.astype(BF)
        ds = (p * dot(dx, vt_ref[...])).astype(BF)
        dq.append(dot(ds, k_ref[...]))
        part = slice(64 * h, 64 * h + 64)
        dkt_ref[part, :] += dot(qt[part, :], ds)
        dvt_ref[part, :] += dot(dot_t[part, :], low)
    dq_ref[...] = (jnp.where(lane < 64, dq[0], dq[1]) * 0.125).astype(BF)

    @pl.when(pl.program_id(1) == pl.num_programs(1) - 1)
    def _():
        dk_ref[...] = dkt_ref[...].T.astype(BF)
        dv_ref[...] = dvt_ref[...].T.astype(BF)


def attention_backward(qkv, o, do, lse, half, valid, wide):
    rows, width = qkv.shape
    pairs = width // 3 // 128

    def whole(part):
        return pl.BlockSpec((rows, 128), lambda p, i: (0, part * pairs + p))

    block = pl.BlockSpec((wide, 128), lambda p, i: (i, p))
    return pl.pallas_call(
        functools.partial(backward_kernel, half, valid),
        grid=(pairs, rows // wide),
        in_specs=[
            block, whole(1), whole(2), block, block,
            pl.BlockSpec((1, 8, wide), lambda p, i: (p, 0, i)),
        ],
        out_specs=[block, whole(0), whole(0)],
        out_shape=[jax.ShapeDtypeStruct((rows, pairs * 128), BF)] * 3,
        scratch_shapes=[
            pltpu.VMEM((256, rows), BF),
            pltpu.VMEM((256, rows), BF),
            pltpu.VMEM((128, rows), F32),
            pltpu.VMEM((128, rows), F32),
        ],
        cost_estimate=pl.CostEstimate(
            flops=pairs * 2 * 8 * rows * rows * 256,
            bytes_accessed=rows * width * 4,
            transcendentals=pairs * 2 * rows * rows,
        ),
        name="attention_backward",
    )(qkv, qkv, qkv, o, do, lse)


def swap(x, axis, size, bit):
    return lax.ppermute(x, axis, [(i, i ^ bit) for i in range(size)])


def bits_of(size):
    top = size // 4
    return top, [1 << b for b in range(top.bit_length() - 2, -1, -1)]


def gather_blocks(x, size):
    me = lax.axis_index("dp")
    top, bits = bits_of(size)
    held = jnp.stack([x] + [swap(x, "dp", size, j * top) for j in (1, 2, 3)])
    where = [j * top for j in range(4)]
    for bit in bits:
        held = jnp.concatenate([held, swap(held, "dp", size, bit)])
        where = where + [w ^ bit for w in where]
    place = [0] * size
    for i, w in enumerate(where):
        place[w] = i
    return jnp.take(held, jnp.asarray(place)[me ^ jnp.arange(size)], axis=0, mode="clip")


def scatter_blocks(x, size):
    me = lax.axis_index("dp")
    top, bits = bits_of(size)
    x = x.reshape(4, *[2] * len(bits), *x.shape[1:])
    for bit in reversed(bits):
        axis = 1 + bits.index(bit)
        mine = lax.rem(me // bit, 2)
        keep = lax.dynamic_index_in_dim(x, mine, axis, keepdims=False)
        give = lax.dynamic_index_in_dim(x, 1 - mine, axis, keepdims=False)
        got = swap(give.astype(BF), "dp", size, bit)
        x = keep.astype(F32) + got.astype(F32)
    mine = me // top
    total = lax.dynamic_index_in_dim(x, mine, 0, keepdims=False)
    for j in (1, 2, 3):
        give = lax.dynamic_index_in_dim(x, mine ^ j, 0, keepdims=False)
        total = total + swap(give.astype(BF), "dp", size, j * top).astype(F32)
    return total


def normalize(values):
    center = jnp.mean(values, axis=-1, keepdims=True)
    centered = values - center
    variance = jnp.mean(centered * centered, axis=-1, keepdims=True)
    inverse = lax.rsqrt(variance + EPSILON)
    return centered * inverse, inverse


def norm_back(grad_out, normed, inverse, gain):
    weighted = grad_out * gain
    first = jnp.mean(weighted, axis=-1, keepdims=True)
    second = jnp.mean(weighted * normed, axis=-1, keepdims=True)
    return inverse * (weighted - first - normed * second)


def gelu_cdf(values):
    return 0.5 * (1.0 + lax.erf(values * (1.0 / math.sqrt(2.0))))


def gelu_slope(values):
    density = jnp.exp(-0.5 * values * values) * (1.0 / math.sqrt(2.0 * math.pi))
    return gelu_cdf(values) + values * density


def shards(
    size, frames_in, ln1_gain, ln1_bias, w_qkv, b_qv, w_o, b_o,
    ln2_gain, ln2_bias, w_fc1, b_fc1, w_fc2, b_fc2, cotangent,
):
    clips, valid, wide = frames_in.shape
    assert clips == 1
    ff = w_fc1.shape[1]
    part = w_qkv.shape[0]
    group = wide // 2
    half = -(-valid // 256) * 256
    here = lax.axis_index("seq")

    def pad(block):
        return jnp.pad(block[0], ((0, half - valid), (0, 0)))

    def other(x):
        return swap(x, "seq", 2, 1)

    def pick(x, axis, index):
        return lax.dynamic_index_in_dim(x, index, axis, keepdims=False)

    vectors = jnp.concatenate([ln1_gain, ln1_bias, b_qv, b_o, ln2_gain, ln2_bias, b_fc1, b_fc2])
    count = vectors.shape[0] // part
    columns = jnp.pad(vectors.reshape(count, part).T, ((0, 0), (0, 128 - count)))
    w_mine = pick(w_qkv.reshape(part, 3, 2, group), 2, here).reshape(part, 3 * group)
    first = gather_blocks(jnp.concatenate([w_mine, columns], axis=1), size)
    qkv_full = first[:, :, : 3 * group].reshape(wide, 3 * group)
    table = first[:, :, 3 * group : 3 * group + count].transpose(2, 0, 1).astype(F32)

    def vector(start, stop):
        return table[start:stop].transpose(1, 0, 2).reshape(-1)

    per = ff // wide
    gain_one, shift_one = vector(0, 1), vector(1, 2)
    bias_qv, bias_out = vector(2, 4), vector(4, 5)
    gain_two, shift_two = vector(5, 6), vector(6, 7)
    bias_fc1, bias_fc2 = vector(7, 7 + per), vector(7 + per, 8 + per)
    second = lax.all_gather(jnp.concatenate([w_o, w_fc1], axis=1), "dp", axis=0, tiled=True)
    out_full, fc1_full = second[:, :wide], second[:, wide:]
    fc2_full = lax.all_gather(w_fc2, "dp", axis=0, tiled=True)

    own = pad(frames_in)
    both = jnp.concatenate([own, other(own)], axis=0).astype(F32)
    normed_both, inverse_both = normalize(both)
    hidden_one = (normed_both * gain_one + shift_one).astype(BF)
    bias_mine = pick(bias_qv.reshape(2, 2, group), 1, here)
    bias_row = jnp.concatenate([bias_mine[0], jnp.zeros((group,), F32), bias_mine[1]])
    qkv = (dot(hidden_one, qkv_full) + bias_row).astype(BF)
    o, lse = attention_forward(qkv, half, valid, 512)
    o_got = other(o[half:])
    o_own = o[:half]
    context = jnp.where(
        here == 0,
        jnp.concatenate([o_own, o_got], axis=1),
        jnp.concatenate([o_got, o_own], axis=1),
    )
    residual = both[:half] + dot(context, out_full) + bias_out

    normed_two, inverse_two = normalize(residual)
    hidden_two = (normed_two * gain_two + shift_two).astype(BF)
    pre_act = dot(hidden_two, fc1_full) + bias_fc1
    activated = (pre_act * gelu_cdf(pre_act)).astype(BF)
    output = residual + dot(activated, fc2_full) + bias_fc2
    frames_out = output.astype(BF)[:valid][None]
    grad_low = pad(cotangent)
    grad_full = grad_low.astype(F32)
    grad_bias_fc2 = jnp.sum(grad_full, axis=0)
    grad_fc2 = dot(activated, grad_low, 0, 0).astype(BF)
    grad_pre = dot(grad_low, fc2_full, 1, 1) * gelu_slope(pre_act)
    grad_bias_fc1 = jnp.sum(grad_pre, axis=0)
    grad_pre_low = grad_pre.astype(BF)
    grad_fc1 = dot(hidden_two, grad_pre_low, 0, 0).astype(BF)
    grad_hidden_two = dot(grad_pre_low, fc1_full, 1, 1)
    grad_gain_two = jnp.sum(grad_hidden_two * normed_two, axis=0)
    grad_shift_two = jnp.sum(grad_hidden_two, axis=0)
    grad_residual = grad_full + norm_back(grad_hidden_two, normed_two, inverse_two, gain_two)
    grad_bias_out = jnp.sum(grad_residual, axis=0)
    grad_residual_low = grad_residual.astype(BF)
    grad_out = dot(context, grad_residual_low, 0, 0).astype(BF)
    grad_context = dot(grad_residual_low, out_full, 1, 1).astype(BF)
    grad_second = lax.psum_scatter(
        jnp.concatenate([grad_out, grad_fc1], axis=1), "dp", scatter_dimension=0, tiled=True
    )
    grad_fc2 = lax.psum_scatter(grad_fc2, "dp", scatter_dimension=0, tiled=True)

    left, right = grad_context[:, :group], grad_context[:, group:]
    do_got = other(jnp.where(here == 0, right, left))
    do = jnp.concatenate([jnp.where(here == 0, left, right), do_got], axis=0)
    dqkv = jnp.concatenate(attention_backward(qkv, o, do, lse, half, valid, 512), axis=1)
    grad_hidden_other = dot(dqkv[half:], qkv_full, 1, 1)
    grad_got = other(grad_hidden_other.astype(BF))
    grad_hidden_mine = dot(dqkv[:half], qkv_full, 1, 1)
    grad_qkv = dot(hidden_one, dqkv, 0, 0)
    sums = jnp.sum(dqkv.astype(F32), axis=0).reshape(3, group)
    grad_bias_mine = jnp.stack([sums[0], sums[2]])
    zero = jnp.zeros_like(grad_bias_mine)
    grad_bias_qv = jnp.where(
        here == 0,
        jnp.concatenate([grad_bias_mine, zero], axis=1),
        jnp.concatenate([zero, grad_bias_mine], axis=1),
    ).reshape(-1)
    grad_both = jnp.concatenate([grad_hidden_mine, grad_hidden_other], axis=0)
    grad_gain_one = jnp.sum(grad_both * normed_both, axis=0)
    grad_shift_one = jnp.sum(grad_both, axis=0)
    grad_hidden_one = grad_hidden_mine + grad_got.astype(F32)
    grad_input = grad_residual + norm_back(
        grad_hidden_one, normed_both[:half], inverse_both[:half], gain_one
    )

    grad_vectors = [
        grad_gain_one, grad_shift_one, grad_bias_qv, grad_bias_out,
        grad_gain_two, grad_shift_two, grad_bias_fc1, grad_bias_fc2,
    ]
    rows = jnp.concatenate([v.reshape(size, -1, part) for v in grad_vectors], axis=1)
    columns = jnp.pad(rows.transpose(0, 2, 1), ((0, 0), (0, 0), (0, 128 - count)))
    mine = scatter_blocks(
        jnp.concatenate([grad_qkv.reshape(size, part, 3 * group), columns], axis=2), size
    ).astype(BF)
    theirs = other(mine)
    low = jnp.where(here == 0, mine, theirs)[:, : 3 * group].reshape(part, 3, 1, group)
    high = jnp.where(here == 0, theirs, mine)[:, : 3 * group].reshape(part, 3, 1, group)
    grad_w_qkv = jnp.concatenate([low, high], axis=2).reshape(part, 6 * group).astype(F32)
    small = mine[:, 3 * group :].astype(F32) + theirs[:, 3 * group :].astype(F32)
    small = small[:, :count].T

    def piece(start, stop):
        return small[start:stop].reshape(-1)

    second_sum = grad_second.astype(F32) + other(grad_second).astype(F32)
    fc2_sum = grad_fc2.astype(F32) + other(grad_fc2).astype(F32)
    return (
        frames_out,
        grad_input[:valid][None],
        piece(0, 1),
        piece(1, 2),
        grad_w_qkv,
        piece(2, 4),
        second_sum[:, :wide],
        piece(4, 5),
        piece(5, 6),
        piece(6, 7),
        second_sum[:, wide:],
        piece(7, 7 + per),
        fc2_sum,
        piece(7 + per, 8 + per),
    )


def solution(mesh):
    frames, rows, vector = P("dp", "seq", None), P("dp", None), P("dp")
    in_specs = (
        frames, vector, vector, rows, vector, rows, vector,
        vector, vector, rows, vector, rows, vector, frames,
    )
    out_specs = (
        frames, frames, vector, vector, rows, vector, rows, vector,
        vector, vector, rows, vector, rows, vector,
    )
    return jax.shard_map(
        functools.partial(shards, mesh.shape["dp"]),
        mesh=mesh, in_specs=in_specs, out_specs=out_specs, check_vma=False,
    )
```

```python
import functools
import math

import jax
import jax.numpy as jnp
from jax import lax
from jax.experimental import pallas as pl
from jax.experimental.pallas import tpu as pltpu
from jax.sharding import PartitionSpec as P


EPSILON = 1e-05
BF = jnp.bfloat16
F32 = jnp.float32
MASKED = -1e30


def dot(a, b, ca=1, cb=0):
    return lax.dot_general(a, b, (((ca,), (cb,)), ((), ())), preferred_element_type=F32)


def split3(x):
    high = x.astype(BF).astype(F32)
    rest = x - high
    mid = rest.astype(BF).astype(F32)
    return high, mid, (rest - mid).astype(BF).astype(F32)


def forward_kernel(half, valid, q_ref, k_ref, v_ref, mine_ref, sent_ref, lse_ref, kx_ref, vt_ref):
    rows = k_ref.shape[0]
    wide = q_ref.shape[0]

    kx_ref[:, :128] = k_ref[...]
    row = lax.broadcasted_iota(jnp.int32, (rows, 128), 0)
    lane = lax.broadcasted_iota(jnp.int32, (rows, 128), 1)
    padded = (lax.rem(row, half) >= valid) & (lane == 0)
    kx_ref[:, 128:] = jnp.where(padded, MASKED, 0.0).astype(BF)
    vt = v_ref[...].T
    vt_ref[0:64, :] = vt[0:64, :]
    vt_ref[64:80, :] = jnp.ones((16, rows), BF)
    vt_ref[80:144, :] = vt[64:128, :]
    vt_ref[144:160, :] = jnp.ones((16, rows), BF)

    lane = lax.broadcasted_iota(jnp.int32, (wide, 128), 1)
    q = q_ref[...] * jnp.asarray(0.125, BF)
    one = jnp.where(lane == 0, 1.0, 0.0).astype(BF)
    outs, sums = [], []
    for h in range(2):
        mine = (lane < 64) if h == 0 else (lane >= 64)
        qx = jnp.concatenate([jnp.where(mine, q, jnp.zeros_like(q)), one], axis=1)
        s = dot(kx_ref[...], qx, 1, 1)
        peak = jnp.max(s, axis=0, keepdims=True)
        p = jnp.exp(s - peak).astype(BF)
        o = dot(vt_ref[80 * h : 80 * h + 80, :], p)
        total = o[64:65, :]
        outs.append(o[0:64, :] / total)
        sums.append(peak + jnp.log(total))
    o = jnp.concatenate(outs, axis=0).T.astype(BF)
    mine_ref[...] = o[:half]
    sent_ref[...] = o[half:]
    lse_ref[...] = jnp.concatenate(sums + [jnp.zeros((6, wide), F32)], axis=0)[None]


def attention_forward(qkv, half, valid):
    rows, width = qkv.shape
    pairs = width // 3 // 128
    block = pl.BlockSpec((half, 128), lambda p: (0, p))
    return pl.pallas_call(
        functools.partial(forward_kernel, half, valid),
        grid=(pairs,),
        in_specs=[
            pl.BlockSpec((rows, 128), lambda p: (0, p)),
            pl.BlockSpec((rows, 128), lambda p: (0, pairs + p)),
            pl.BlockSpec((rows, 128), lambda p: (0, 2 * pairs + p)),
        ],
        out_specs=[block, block, pl.BlockSpec((1, 8, rows), lambda p: (p, 0, 0))],
        out_shape=[
            jax.ShapeDtypeStruct((half, pairs * 128), BF),
            jax.ShapeDtypeStruct((half, pairs * 128), BF),
            jax.ShapeDtypeStruct((pairs, 8, rows), F32),
        ],
        scratch_shapes=[pltpu.VMEM((rows, 256), BF), pltpu.VMEM((160, rows), BF)],
        cost_estimate=pl.CostEstimate(
            flops=pairs * 2 * 4 * rows * rows * 256,
            bytes_accessed=rows * width * 2 + rows * width,
            transcendentals=pairs * 2 * rows * rows,
        ),
        name="attention_forward",
    )(qkv, qkv, qkv)


def backward_kernel(
    half, valid, q_ref, k_ref, v_ref, o_mine_ref, o_sent_ref, mine_ref, got_ref, lse_ref, token_ref,
    d_ref, kt_ref, vt_ref, dkt_ref, dvt_ref,
):
    rows = k_ref.shape[0]
    step = pl.program_id(1)

    @pl.when(step == 0)
    def _():
        kt_ref[0:128, :] = k_ref[...].T
        vt_ref[0:128, :] = v_ref[...].T
        row = lax.broadcasted_iota(jnp.int32, (128, rows), 0)
        key = lax.broadcasted_iota(jnp.int32, (128, rows), 1)
        bias = jnp.where(lax.rem(key, half) >= valid, MASKED, 0.0)
        ones = jnp.where((row >= 1) & (row < 4), 1.0, 0.0)
        kt_ref[128:256, :] = jnp.where(row == 0, bias, ones).astype(BF)
        vt_ref[128:256, :] = ones.astype(BF)
        dkt_ref[...] = jnp.zeros_like(dkt_ref)
        dvt_ref[...] = jnp.zeros_like(dvt_ref)

    lane = lax.broadcasted_iota(jnp.int32, (half, 128), 1)
    q = q_ref[...] * jnp.asarray(0.125, BF)
    do = jnp.where(step == 0, mine_ref[...], got_ref[...])
    o = jnp.where(step == 0, o_mine_ref[...], o_sent_ref[...])
    product = do.astype(F32) * o.astype(F32)
    lse = lse_ref[0].T
    qt, dot_t = q.T, do.T

    def extra(x, first):
        a, b, c = split3(-x)
        tail = jnp.where(lane == 2, b, jnp.where(lane == 3, c, 0.0))
        return jnp.where(lane == 0, first, jnp.where(lane == 1, a, tail)).astype(BF)

    dq = []
    for h in range(2):
        mine = (lane < 64) if h == 0 else (lane >= 64)
        delta = jnp.sum(jnp.where(mine, product, 0.0), axis=1, keepdims=True)
        qx = jnp.concatenate(
            [jnp.where(mine, q, jnp.zeros_like(q)), extra(lse[:, h : h + 1], 1.0)], axis=1
        )
        dx = jnp.concatenate([jnp.where(mine, do, jnp.zeros_like(do)), extra(delta, 0.0)], axis=1)
        p = jnp.exp(dot(qx, kt_ref[...]))
        low = p.astype(BF)
        ds = (p * dot(dx, vt_ref[...])).astype(BF)
        dq.append(dot(ds, k_ref[...]))
        part = slice(64 * h, 64 * h + 64)
        dkt_ref[part, :] += dot(qt[part, :], ds)
        dvt_ref[part, :] += dot(dot_t[part, :], low)
    dq = (jnp.where(lane < 64, dq[0], dq[1]) * 0.125).astype(BF)
    d_ref[0, pl.ds(pl.multiple_of(step * half, 128), half), :] = dq

    @pl.when(step == 1)
    def _():
        d_ref[1] = dkt_ref[...].T.astype(BF)
        d_ref[2] = dvt_ref[...].T.astype(BF)


def attention_backward(qkv, o_mine, o_sent, do_mine, do_got, lse, token, half, valid, start, count):
    rows, width = qkv.shape
    pairs = width // 3 // 128

    def whole(part):
        return pl.BlockSpec((rows, 128), lambda p, i: (0, part * pairs + start + p))

    block = pl.BlockSpec((half, 128), lambda p, i: (i, start + p))
    fixed = pl.BlockSpec((half, 128), lambda p, i: (0, start + p))
    return pl.pallas_call(
        functools.partial(backward_kernel, half, valid),
        grid=(count, 2),
        in_specs=[
            block, whole(1), whole(2), fixed, fixed, fixed, fixed,
            pl.BlockSpec((1, 8, half), lambda p, i: (start + p, 0, i)),
            pl.BlockSpec(memory_space=pl.ANY),
        ],
        out_specs=pl.BlockSpec((3, rows, 128), lambda p, i: (0, 0, p)),
        out_shape=jax.ShapeDtypeStruct((3, rows, count * 128), BF),
        scratch_shapes=[
            pltpu.VMEM((256, rows), BF),
            pltpu.VMEM((256, rows), BF),
            pltpu.VMEM((128, rows), F32),
            pltpu.VMEM((128, rows), F32),
        ],
        cost_estimate=pl.CostEstimate(
            flops=count * 2 * 8 * rows * rows * 256,
            bytes_accessed=count * rows * 128 * 16,
            transcendentals=count * 2 * rows * rows,
        ),
        name="attention_backward",
    )(qkv, qkv, qkv, o_mine, o_sent, do_mine, do_got, lse, token)


def prepare_kernel(x_ref, *refs):
    normed_ref, flipped_ref, inverse_ref = refs[-3:]
    valid = x_ref.shape[1]
    x = x_ref[0].astype(F32)
    centered = x - jnp.mean(x, axis=-1, keepdims=True)
    inverse = lax.rsqrt(jnp.mean(centered * centered, axis=-1, keepdims=True) + EPSILON)
    rest = (normed_ref.shape[0] - valid // 8 * 8, normed_ref.shape[1])
    normed_ref[valid // 8 * 8 :, :] = jnp.zeros(rest, F32)
    normed_ref[:valid, :] = centered * inverse
    inverse_ref[...] = jnp.zeros(inverse_ref.shape, F32)
    inverse_ref[:valid, :] = inverse
    wide = normed_ref.shape[1]
    flipped_ref[:wide, :] = normed_ref[...].T.astype(BF)
    flipped_ref[wide:, :] = jnp.ones((16, normed_ref.shape[0]), BF)


def prepare(frames, half, block, filled=()):
    _, valid, wide = frames.shape
    return pl.pallas_call(
        prepare_kernel,
        grid=(1,),
        in_specs=[pl.BlockSpec((1, valid, wide), lambda i: (0, 0, 0))]
        + [pl.BlockSpec(memory_space=pl.ANY)] * len(filled),
        out_specs=[
            pl.BlockSpec((half, wide), lambda i: (block, 0)),
            pl.BlockSpec((wide + 16, half), lambda i: (0, block)),
            pl.BlockSpec((half, 1), lambda i: (0, 0)),
        ],
        out_shape=[
            jax.ShapeDtypeStruct((2 * half, wide), F32),
            jax.ShapeDtypeStruct((wide + 16, 2 * half), BF),
            jax.ShapeDtypeStruct((half, 1), F32),
        ],
        input_output_aliases={1: 0, 2: 1} if filled else {},
        cost_estimate=pl.CostEstimate(
            flops=half * wide * 16, bytes_accessed=half * wide * 8, transcendentals=half
        ),
        name="prepare",
    )(frames, *filled)


def projection_kernel(
    part, group, place_ref, held_ref, x_ref, qkv_ref, w_ref, wt_ref, rows_ref, columns_ref,
    gain_ref, bias_ref,
):
    wide, width = w_ref.shape

    @pl.when(pl.program_id(0) == 0)
    def _():
        blocks, extent, _ = held_ref.shape
        for d in range(blocks):
            block = held_ref[place_ref[d]]
            w_ref[d * extent : (d + 1) * extent, :] = block[:, :width]
            columns_ref[d * extent : (d + 1) * extent, :] = block[:, width:].astype(F32)
        wt_ref[...] = w_ref[...].T
        table = columns_ref[...].T[:16, :]
        rows_ref[...] = table
        gain_ref[...] = table[:8]
        here = place_ref[blocks]
        lane = lax.broadcasted_iota(jnp.int32, (wide, group), 0)
        entry = lax.broadcasted_iota(jnp.int32, (wide, group), 1)
        base = lane + part * (lane // part) - group * here
        low = table.astype(BF)
        for v in range(2):
            total = jnp.zeros((16, group), F32)
            for j in range(2):
                chosen = entry == base + part * j - wide * v
                picked = dot(low, jnp.where(chosen, 1.0, 0.0).astype(BF))
                total = total + picked[2 + j : 3 + j, :]
            bias_ref[:, 2 * v * group : (2 * v + 1) * group] = total[:8]
        bias_ref[:, group : 2 * group] = jnp.zeros((8, group), F32)

    h = (x_ref[...] * gain_ref[0:1, :] + gain_ref[1:2, :]).astype(BF)
    qkv_ref[...] = (dot(h, w_ref[...]) + bias_ref[0:1, :]).astype(BF)


def projection(held, place, normed, part):
    blocks, extent, across = held.shape
    width = across - 128
    rows, wide = normed.shape
    tile = 512

    def fixed(*shape):
        return pl.BlockSpec(shape, lambda i, p: tuple(0 for _ in shape))

    return pl.pallas_call(
        functools.partial(projection_kernel, part, width // 3),
        grid_spec=pltpu.PrefetchScalarGridSpec(
            num_scalar_prefetch=1,
            grid=(rows // tile,),
            in_specs=[fixed(blocks, extent, across), pl.BlockSpec((tile, wide), lambda i, p: (i, 0))],
            out_specs=[
                pl.BlockSpec((tile, width), lambda i, p: (i, 0)),
                fixed(wide, width), fixed(width, wide), fixed(16, wide), fixed(wide, 128),
            ],
            scratch_shapes=[pltpu.VMEM((8, wide), F32), pltpu.VMEM((8, width), F32)],
        ),
        out_shape=[
            jax.ShapeDtypeStruct((rows, width), BF),
            jax.ShapeDtypeStruct((wide, width), BF),
            jax.ShapeDtypeStruct((width, wide), BF),
            jax.ShapeDtypeStruct((16, wide), F32),
            jax.ShapeDtypeStruct((wide, 128), F32),
        ],
        cost_estimate=pl.CostEstimate(
            flops=2 * rows * wide * width, bytes_accessed=rows * wide * 8, transcendentals=0
        ),
        name="projection",
    )(place, held, normed)


def weight_kernel(pieces, xt_ref, w_ref, scale_ref, *refs):
    d_refs, (g_ref, c_ref, s_ref) = refs[:pieces], refs[pieces:]
    d = jnp.concatenate([r[0] for r in d_refs], axis=1)
    m = dot(xt_ref[...], d)
    s = m[w_ref.shape[0] :][:8]
    m = m[: w_ref.shape[0]]
    s_ref[...] = s
    gain, shift = scale_ref[:, 0:1], scale_ref[:, 1:2]
    total = s[0:1, :]
    g_ref[...] = (gain * m + shift * total).astype(BF)
    w = w_ref[...].astype(F32)
    lane = lax.broadcasted_iota(jnp.int32, c_ref.shape, 1)
    first = jnp.sum(w * m, axis=1, keepdims=True)
    second = jnp.sum(w * total, axis=1, keepdims=True)
    now = jnp.where(lane == 0, first, jnp.where(lane == 1, second, 0.0))
    before = jnp.where(pl.program_id(0) == 0, jnp.zeros_like(now), c_ref[...])
    c_ref[...] = before + now


def projection_weight_gradient(xt, w, scale, ds):
    tall, rows = xt.shape
    wide = w.shape[0]
    group = sum(d.shape[2] for d in ds)
    return pl.pallas_call(
        functools.partial(weight_kernel, len(ds)),
        grid=(3,),
        in_specs=[
            pl.BlockSpec((tall, rows), lambda j: (0, 0)),
            pl.BlockSpec((wide, group), lambda j: (0, j)),
            pl.BlockSpec((wide, 128), lambda j: (0, 0)),
        ]
        + [pl.BlockSpec((1, *d.shape[1:]), lambda j: (j, 0, 0)) for d in ds],
        out_specs=[
            pl.BlockSpec((wide, group), lambda j: (0, j)),
            pl.BlockSpec((wide, 128), lambda j: (0, 0)),
            pl.BlockSpec((8, group), lambda j: (0, j)),
        ],
        out_shape=[
            jax.ShapeDtypeStruct((wide, 3 * group), BF),
            jax.ShapeDtypeStruct((wide, 128), F32),
            jax.ShapeDtypeStruct((8, 3 * group), F32),
        ],
        cost_estimate=pl.CostEstimate(
            flops=2 * rows * wide * 3 * group, bytes_accessed=rows * wide * 4, transcendentals=0
        ),
        name="projection_weight_gradient",
    )(xt, w, scale, *ds)


def spread_kernel(
    part, pieces, per, place_ref, token_ref, xt_ref, w_ref, scale_ref, *refs
):
    d_refs, (b_ref, v_ref, keep_ref, give_ref, c_ref, s_ref) = refs[:pieces], refs[pieces:]
    step = pl.program_id(0)
    wide, group = w_ref.shape
    d = jnp.concatenate([r[0] for r in d_refs], axis=1)
    m = dot(xt_ref[...], d)
    s = m[wide : wide + 8]
    m = m[:wide]
    s_ref[step] = s
    gain, shift = scale_ref[:, 0:1], scale_ref[:, 1:2]
    total = s[0:1, :]
    g = (gain * m + shift * total).astype(BF)
    w = w_ref[...].astype(F32)
    lane = lax.broadcasted_iota(jnp.int32, c_ref.shape, 1)
    first = jnp.sum(w * m, axis=1, keepdims=True)
    second = jnp.sum(w * total, axis=1, keepdims=True)
    now = jnp.where(lane == 0, first, jnp.where(lane == 1, second, 0.0))

    @pl.when(step == 0)
    def _():
        c_ref[...] = now

    @pl.when(step > 0)
    def _():
        c_ref[...] += now

    def store(value, columns):
        value = value.reshape(keep_ref.shape[0], 2, part, value.shape[1])

        @pl.when(place_ref[0] == 0)
        def _():
            keep_ref[:, :, columns] = value[:, 0]
            give_ref[:, :, columns] = value[:, 1]

        @pl.when(place_ref[0] == 1)
        def _():
            keep_ref[:, :, columns] = value[:, 1]
            give_ref[:, :, columns] = value[:, 0]

    store(g, pl.ds(pl.multiple_of(step * group, 128), group))

    @pl.when(step == 2)
    def _():
        columns = c_ref[...]
        small = v_ref[...].T
        for i, name in enumerate((4, 5, 6, 7 + per)):
            columns = jnp.where(lane == name, small[:, i : i + 1], columns)
        v = jnp.broadcast_to(b_ref[...], (8, b_ref.shape[1])).T[:, 0:1]
        for j in range(per):
            column = jnp.concatenate(
                [v[(d * per + j) * part :][:part] for d in range(wide // part)], axis=0
            )
            columns = jnp.where(lane == 7 + j, column, columns)
        c_ref[...] = columns
        half = group // 2
        low = lane[:half]
        for side in (0, 2):
            v = s_ref[side].T[:, 0:1]
            at = pl.ds(pl.multiple_of(place_ref[1] * half + side * wide // 4, 64), half)
            block = c_ref[at, :]
            for j in range(2):
                column = jnp.concatenate(
                    [v[(2 * d + j) * part :][:part] for d in range(half // part)], axis=0
                )
                block = jnp.where(low == 2 + j, column, block)
            c_ref[at, :] = block
        store(c_ref[...].astype(BF), pl.ds(3 * group, 128))


def spread_weight_gradient(place, token, xt, w, scale, ds, bias, sums, part):
    _, rows = xt.shape
    wide = w.shape[0]
    group = sum(d.shape[2] for d in ds)
    size = wide // part
    out = pl.BlockSpec((size // 2, part, 3 * group + 128), lambda j, p: (0, 0, 0))

    def fixed(x):
        return pl.BlockSpec(x.shape, lambda j, p: (0, 0))

    return pl.pallas_call(
        functools.partial(spread_kernel, part, len(ds), bias.shape[1] // wide),
        grid_spec=pltpu.PrefetchScalarGridSpec(
            num_scalar_prefetch=1,
            grid=(3,),
            in_specs=[
                pl.BlockSpec(memory_space=pl.ANY),
                fixed(xt),
                pl.BlockSpec((wide, group), lambda j, p: (0, j)),
                fixed(scale),
            ]
            + [pl.BlockSpec((1, *d.shape[1:]), lambda j, p: (j, 0, 0)) for d in ds]
            + [fixed(bias), fixed(sums)],
            out_specs=[out, out],
            scratch_shapes=[pltpu.VMEM((wide, 128), F32), pltpu.VMEM((3, 8, group), F32)],
        ),
        out_shape=[jax.ShapeDtypeStruct((size // 2, part, 3 * group + 128), BF)] * 2,
        cost_estimate=pl.CostEstimate(
            flops=2 * rows * wide * 3 * group, bytes_accessed=rows * wide * 4, transcendentals=0
        ),
        name="spread_weight_gradient",
    )(place, token, xt, w, scale, *ds, bias, sums)


def input_kernel(pieces, token_ref, wt_ref, *refs):
    d_refs, (other_ref, mine_ref) = refs[:pieces], refs[pieces:]
    d = jnp.concatenate([r[j] for j in range(3) for r in d_refs], axis=1)
    value = dot(d, wt_ref[...])
    half = pl.num_programs(0) // 2

    @pl.when(pl.program_id(0) < half)
    def _():
        other_ref[...] = value.astype(BF)

    @pl.when(pl.program_id(0) >= half)
    def _():
        mine_ref[...] = value


def projection_input_gradient(wt, ds, token, half):
    wide = wt.shape[1]
    tile = 384
    tiles = half // tile
    return pl.pallas_call(
        functools.partial(input_kernel, len(ds)),
        grid=(2 * tiles,),
        in_specs=[pl.BlockSpec(memory_space=pl.ANY), pl.BlockSpec(wt.shape, lambda i: (0, 0))]
        + [
            pl.BlockSpec((3, tile, d.shape[2]), lambda i: (0, lax.rem(i + tiles, 2 * tiles), 0))
            for d in ds
        ],
        out_specs=[
            pl.BlockSpec((tile, wide), lambda i: (jnp.minimum(i, tiles - 1), 0)),
            pl.BlockSpec((tile, wide), lambda i: (jnp.maximum(i - tiles, 0), 0)),
        ],
        out_shape=[
            jax.ShapeDtypeStruct((half, wide), BF),
            jax.ShapeDtypeStruct((half, wide), F32),
        ],
        cost_estimate=pl.CostEstimate(
            flops=4 * half * wt.size, bytes_accessed=half * wt.shape[0] * 8, transcendentals=0
        ),
        name="projection_input_gradient",
    )(token, wt, *ds)


def second_kernel(place_ref, token_ref, mine_ref, got_ref, drb_ref, h_ref, du_ref, out_ref, ht_ref):
    group = mine_ref.shape[1]
    step = pl.program_id(0)

    @pl.when(step == 0)
    def _():
        ht_ref[...] = h_ref[...].T
        here = place_ref[0]
        first = pl.multiple_of(here * group, 128)
        other = pl.multiple_of(group - here * group, 128)
        out_ref[pl.ds(first, group), :] = dot(mine_ref[...], drb_ref[...], 0, 0).astype(BF)
        out_ref[pl.ds(other, group), :] = dot(got_ref[...], drb_ref[...], 0, 0).astype(BF)

    @pl.when(step > 0)
    def _():
        out_ref[...] = dot(ht_ref[...], du_ref[...]).astype(BF)


def second_gradient(here, token, o_mine, o_got, drb, hidden, du):
    rows, wide = hidden.shape
    ff = du.shape[1]

    def fixed(x):
        return pl.BlockSpec(x.shape, lambda i, p: (0, 0))

    return pl.pallas_call(
        second_kernel,
        grid_spec=pltpu.PrefetchScalarGridSpec(
            num_scalar_prefetch=1,
            grid=(1 + ff // wide,),
            in_specs=[
                pl.BlockSpec(memory_space=pl.ANY), fixed(o_mine), fixed(o_got), fixed(drb), fixed(hidden),
                pl.BlockSpec((rows, wide), lambda i, p: (0, jnp.maximum(i - 1, 0))),
            ],
            out_specs=pl.BlockSpec((wide, wide), lambda i, p: (0, i)),
            scratch_shapes=[pltpu.VMEM((wide, rows), BF)],
        ),
        out_shape=jax.ShapeDtypeStruct((wide, wide + ff), BF),
        cost_estimate=pl.CostEstimate(
            flops=2 * rows * wide * (wide + ff), bytes_accessed=rows * ff * 4, transcendentals=0
        ),
        name="second_gradient",
    )(here, token, o_mine, o_got, drb, hidden, du)


def fill_rows(ref, x):
    valid = x.shape[0]
    start = valid // 16 * 16
    ref[start:, :] = jnp.zeros((ref.shape[0] - start, ref.shape[1]), ref.dtype)
    ref[:valid, :] = x


def third_kernel(place_ref, z_ref, cot_ref, token_ref, keep_ref, give_ref, padded_ref):
    @pl.when(pl.program_id(0) == 0)
    def _():
        fill_rows(padded_ref, cot_ref[0])

    value = dot(z_ref[...], padded_ref[...], 0, 0).astype(BF)
    owners, extent, wide = keep_ref.shape
    value = value.reshape(owners, 2, extent, wide)

    @pl.when(place_ref[0] == 0)
    def _():
        keep_ref[...] = value[:, 0]
        give_ref[...] = value[:, 1]

    @pl.when(place_ref[0] == 1)
    def _():
        keep_ref[...] = value[:, 1]
        give_ref[...] = value[:, 0]


def third_gradient(parity, activated, cotangent, size, token):
    _, valid, wide = cotangent.shape
    rows, ff = activated.shape
    extent = ff // size
    owners = wide // extent // 2
    out = pl.BlockSpec((owners, extent, wide), lambda i, p: (i, 0, 0))
    return pl.pallas_call(
        third_kernel,
        grid_spec=pltpu.PrefetchScalarGridSpec(
            num_scalar_prefetch=1,
            grid=(ff // wide,),
            in_specs=[
                pl.BlockSpec((rows, wide), lambda i, p: (0, i)),
                pl.BlockSpec((1, valid, wide), lambda i, p: (0, 0, 0)),
                pl.BlockSpec(memory_space=pl.ANY),
            ],
            out_specs=[out, out],
            scratch_shapes=[pltpu.VMEM((rows, wide), BF)],
        ),
        out_shape=[jax.ShapeDtypeStruct((size // 2, extent, wide), BF)] * 2,
        cost_estimate=pl.CostEstimate(
            flops=2 * rows * wide * ff, bytes_accessed=rows * ff * 4, transcendentals=0
        ),
        name="third_gradient",
    )(parity, activated, cotangent, token)


def feed_back_kernel(
    part, place_ref, fc2_ref, fc1_ref, out_ref, slope_ref, cot_ref, residual_ref, gain_ref,
    du_ref, flat_ref, grad_ref, low_ref, mine_ref, sent_ref, bias_ref, sums_ref,
    total_ref, padded_ref,
):
    step = pl.program_id(0)
    rows, wide = total_ref.shape
    group = mine_ref.shape[1]
    per = fc2_ref.shape[1] // wide

    @pl.when(step == 0)
    def _():
        fill_rows(padded_ref, cot_ref[0])
        total_ref[...] = jnp.zeros_like(total_ref)

    if part:
        for d in range(fc2_ref.shape[0] // part):
            for j in range(per):
                block = fc2_ref[d * part : (d + 1) * part, j * wide : (j + 1) * wide]
                flat_ref[(d * per + j) * part : (d * per + j + 1) * part, :] = block
    else:
        flat_ref[...] = fc2_ref[...]
    du = dot(padded_ref[...], flat_ref[...], 1, 1) * slope_ref[...].astype(F32)
    bias_ref[...] = jnp.sum(du, axis=0, keepdims=True)
    du = du.astype(BF)
    du_ref[...] = du
    total_ref[...] += dot(du, fc1_ref[...], 1, 1)

    @pl.when(step == pl.num_programs(0) - 1)
    def _():
        tile = 64

        def body(i, sums):
            at = pl.ds(pl.multiple_of(i * tile, tile), tile)
            r = residual_ref[at, :]
            centered = r - jnp.mean(r, axis=-1, keepdims=True)
            inverse = lax.rsqrt(jnp.mean(centered * centered, axis=-1, keepdims=True) + EPSILON)
            normed = centered * inverse
            dh = total_ref[at, :]
            weighted = dh * gain_ref[...]
            first = jnp.mean(weighted, axis=-1, keepdims=True)
            second = jnp.mean(weighted * normed, axis=-1, keepdims=True)
            g = padded_ref[at, :].astype(F32)
            grad = g + inverse * (weighted - first - normed * second)
            grad_ref[at, :] = grad
            low_ref[at, :] = grad.astype(BF)
            parts = (grad, dh * normed, dh, g)
            return tuple(s + jnp.sum(p, axis=0, keepdims=True) for s, p in zip(sums, parts, strict=True))

        zero = jnp.zeros((1, wide), F32)
        sums = lax.fori_loop(0, rows // tile, body, (zero,) * 4)
        sums_ref[...] = jnp.concatenate(sums + (jnp.zeros((4, wide), F32),), axis=0)
        here = place_ref[0]
        mine = out_ref[pl.ds(pl.multiple_of(here * group, 128), group), :]
        other = out_ref[pl.ds(pl.multiple_of(group - here * group, 128), group), :]
        sent_ref[...] = dot(low_ref[...], other, 1, 1).astype(BF)
        mine_ref[...] = dot(low_ref[...], mine, 1, 1).astype(BF)


def feed_back(here, weights, slope, cotangent, residual, gain, part):
    rows, ff = slope.shape
    _, valid, wide = cotangent.shape
    group = wide // 2
    per = ff // wide
    if part % 16:
        part = 0
        fc2, fc1, out = weights
        fc2_spec = pl.BlockSpec((wide, wide), lambda i, p: (i, 0))
        fc1_spec = pl.BlockSpec((wide, wide), lambda i, p: (0, i))
        out_spec = pl.BlockSpec((wide, wide), lambda i, p: (0, 0))
    else:
        fc2 = fc1 = out = weights
        fc2_spec = pl.BlockSpec((wide // per, ff), lambda i, p: (i, 0))
        fc1_spec = pl.BlockSpec((wide, wide), lambda i, p: (0, per + 1 + i))
        out_spec = pl.BlockSpec((wide, wide), lambda i, p: (0, per))

    def fixed(*shape):
        return pl.BlockSpec(shape, lambda i, p: tuple(0 for _ in shape))

    block = pl.BlockSpec((rows, wide), lambda i, p: (0, i))
    return pl.pallas_call(
        functools.partial(feed_back_kernel, part),
        grid_spec=pltpu.PrefetchScalarGridSpec(
            num_scalar_prefetch=1,
            grid=(per,),
            in_specs=[
                fc2_spec, fc1_spec, out_spec, block, fixed(1, valid, wide), fixed(rows, wide),
                fixed(1, wide),
            ],
            out_specs=[
                block, pl.BlockSpec((wide, wide), lambda i, p: (i, 0)), fixed(rows, wide),
                fixed(rows, wide), fixed(rows, group), fixed(rows, group),
                pl.BlockSpec((1, wide), lambda i, p: (0, i)), fixed(8, wide),
            ],
            scratch_shapes=[pltpu.VMEM((rows, wide), F32), pltpu.VMEM((rows, wide), BF)],
        ),
        out_shape=[
            jax.ShapeDtypeStruct((rows, ff), BF),
            jax.ShapeDtypeStruct((ff, wide), BF),
            jax.ShapeDtypeStruct((rows, wide), F32),
            jax.ShapeDtypeStruct((rows, wide), BF),
            jax.ShapeDtypeStruct((rows, group), BF),
            jax.ShapeDtypeStruct((rows, group), BF),
            jax.ShapeDtypeStruct((1, ff), F32),
            jax.ShapeDtypeStruct((8, wide), F32),
        ],
        cost_estimate=pl.CostEstimate(
            flops=4 * rows * wide * ff, bytes_accessed=ff * wide * 10, transcendentals=rows
        ),
        name="feed_back",
    )(here, fc2, fc1, out, slope, cotangent, residual, gain)


def finish_kernel(spans, place_ref, mine_ref, theirs_ref, w_ref, *refs):
    here = place_ref[0]
    group = w_ref.shape[1] // 6
    mine, theirs = mine_ref[...].astype(F32), theirs_ref[...].astype(F32)
    for j in range(3):
        part = slice(j * group, (j + 1) * group)
        at = (2 * j * group) + here * group
        w_ref[:, pl.ds(pl.multiple_of(at, 128), group)] = mine[:, part]
        at = (2 * j + 1) * group - here * group
        w_ref[:, pl.ds(pl.multiple_of(at, 128), group)] = theirs[:, part]
    rows = (mine[:, 3 * group :] + theirs[:, 3 * group :]).T
    for (start, stop), ref in zip(spans, refs, strict=True):
        ref[...] = jnp.concatenate([rows[i : i + 1] for i in range(start, stop)], axis=1)


def finish(here, mine, theirs, spans):
    part, across = mine.shape
    width = 2 * (across - 128)

    def fixed(*shape):
        return pl.BlockSpec(shape, lambda i, p: (0, 0))

    sizes = [(1, (stop - start) * part) for start, stop in spans]
    return pl.pallas_call(
        functools.partial(finish_kernel, spans),
        grid_spec=pltpu.PrefetchScalarGridSpec(
            num_scalar_prefetch=1,
            grid=(1,),
            in_specs=[fixed(part, across)] * 2,
            out_specs=[fixed(part, width)] + [fixed(*shape) for shape in sizes],
        ),
        out_shape=[jax.ShapeDtypeStruct((part, width), F32)]
        + [jax.ShapeDtypeStruct(shape, F32) for shape in sizes],
        name="finish",
    )(here, mine, theirs)


def join_kernel(mine_ref, theirs_ref, out_ref, first_ref):
    wide = out_ref.shape[1]
    mine, theirs = mine_ref[...].astype(F32), theirs_ref[...].astype(F32)
    out_ref[...] = mine[:, :wide] + theirs[:, :wide]
    first_ref[...] = mine[:, wide:] + theirs[:, wide:]


def join_second(mine, theirs, wide):
    part, across = mine.shape
    return pl.pallas_call(
        join_kernel,
        out_shape=[
            jax.ShapeDtypeStruct((part, wide), F32),
            jax.ShapeDtypeStruct((part, across - wide), F32),
        ],
        name="join_second",
    )(mine, theirs)


def input_end_kernel(mine_ref, got_ref, residual_ref, normed_ref, gain_ref, inverse_ref, out_ref):
    normed = normed_ref[...]
    weighted = (mine_ref[...] + got_ref[...].astype(F32)) * gain_ref[...]
    first = jnp.mean(weighted, axis=-1, keepdims=True)
    second = jnp.mean(weighted * normed, axis=-1, keepdims=True)
    out_ref[:, 0, :] = residual_ref[...] + inverse_ref[...] * (weighted - first - normed * second)


def input_end(mine, got, residual, normed, gain, inverse, valid):
    half, wide = mine.shape
    tile = 128
    block = pl.BlockSpec((tile, wide), lambda i: (i, 0))
    return pl.pallas_call(
        input_end_kernel,
        grid=(half // tile,),
        in_specs=[
            block, block, block, block, pl.BlockSpec((1, wide), lambda i: (0, 0)),
            pl.BlockSpec((tile, 1), lambda i: (i, 0)),
        ],
        out_specs=pl.BlockSpec((tile, 1, wide), lambda i: (i, 0, 0)),
        out_shape=jax.ShapeDtypeStruct((valid, 1, wide), F32),
        cost_estimate=pl.CostEstimate(
            flops=half * wide * 10, bytes_accessed=half * wide * 18, transcendentals=0
        ),
        name="input_end",
    )(mine, got, residual, normed, gain, inverse)


def swap(x, axis, size, bit):
    return lax.ppermute(x, axis, [(i, i ^ bit) for i in range(size)])


def bits_of(size):
    top = size // 4
    return top, [1 << b for b in range(top.bit_length() - 2, -1, -1)]


def gather_blocks(x, size):
    me = lax.axis_index("dp")
    top, bits = bits_of(size)
    held = jnp.stack([x] + [swap(x, "dp", size, j * top) for j in (1, 2, 3)])
    where = [j * top for j in range(4)]
    for bit in bits:
        held = jnp.concatenate([held, swap(held, "dp", size, bit)])
        where = where + [w ^ bit for w in where]
    place = [0] * size
    for i, w in enumerate(where):
        place[w] = i
    return held, jnp.asarray(place, jnp.int32)[me ^ jnp.arange(size)]


def halve(x, axis, bit):
    mine = lax.rem(lax.axis_index("dp") // bit, 2)
    keep = lax.dynamic_index_in_dim(x, mine, axis, keepdims=False)
    give = lax.dynamic_index_in_dim(x, 1 - mine, axis, keepdims=False)
    return keep, give.astype(BF)


def scatter_split(x, size):
    top, _ = bits_of(size)
    mine = lax.axis_index("dp") // top
    gives = [
        lax.dynamic_index_in_dim(x, mine ^ j, 0, keepdims=False).astype(BF) for j in (1, 2, 3)
    ]
    return gives, lax.dynamic_index_in_dim(x, mine, 0, keepdims=False).astype(F32)


def scatter_join(total, gives, size):
    top, _ = bits_of(size)
    for j, give in zip((1, 2, 3), gives, strict=True):
        total = total + swap(give, "dp", size, j * top).astype(F32)
    return total


def after(x, *others):
    return lax.optimization_barrier((x, *others))[0]


def normalize(values):
    center = jnp.mean(values, axis=-1, keepdims=True)
    centered = values - center
    variance = jnp.mean(centered * centered, axis=-1, keepdims=True)
    inverse = lax.rsqrt(variance + EPSILON)
    return centered * inverse, inverse


def gelu_cdf(values):
    return 0.5 * (1.0 + lax.erf(values * (1.0 / math.sqrt(2.0))))


def layer(
    size, frames_in, ln1_gain, ln1_bias, w_qkv, b_qv, w_o, b_o,
    ln2_gain, ln2_bias, w_fc1, b_fc1, w_fc2, b_fc2, cotangent,
):
    clips, valid, wide = frames_in.shape
    assert clips == 1
    ff = w_fc1.shape[1]
    part = w_qkv.shape[0]
    group = wide // 2
    half = -(-valid // 256) * 256
    here = lax.axis_index("seq")

    def pad(block):
        return jnp.pad(block[0], ((0, half - valid), (0, 0)))

    def other(x):
        return swap(x, "seq", 2, 1)

    def pick(x, axis, index):
        return lax.dynamic_index_in_dim(x, index, axis, keepdims=False)

    per = ff // wide
    me = lax.axis_index("dp")
    _, bits = bits_of(size)

    vectors = jnp.concatenate([ln1_gain, ln1_bias, b_qv, b_o, ln2_gain, ln2_bias, b_fc1, b_fc2])
    count = vectors.shape[0] // part
    columns = lax.optimization_barrier(
        jnp.pad(vectors.reshape(count, part).T, ((0, 0), (0, 128 - count)))
    )
    w_mine = [
        lax.dynamic_slice_in_dim(w_qkv, j * wide + here * group, group, axis=1) for j in range(3)
    ]
    held, place = gather_blocks(jnp.concatenate(w_mine + [columns], axis=1), size)
    if part % 16:
        held = jnp.take(held, place, axis=0, mode="clip").reshape(1, wide, 3 * group + 128)
        place = jnp.zeros((1,), jnp.int32)
    place = jnp.concatenate([place, jnp.full((1,), here, jnp.int32)])
    fc2_local = w_fc2.reshape(per, part, wide).transpose(1, 0, 2).reshape(part, ff)
    later = lax.all_gather(
        jnp.concatenate([fc2_local, w_o, w_fc1], axis=1), "dp", axis=0, tiled=True
    )
    out_full, fc1_full = later[:, ff : ff + wide], later[:, ff + wide :]
    weights = later
    if part % 16:
        fc2_full = later[:, :ff].reshape(size, part, per, wide)
        weights = (fc2_full.transpose(0, 2, 1, 3).reshape(ff, wide), fc1_full, out_full)

    prepared = prepare(frames_in, half, 0)
    inverse_one = prepared[2]
    normed_both, normed_t, _ = prepare(other(frames_in), half, 1, prepared[:2])
    qkv, w_full, w_flipped, table, scale = projection(held, place, normed_both, part)

    def vector(start, stop):
        return table[start:stop].reshape(-1, size, part).transpose(1, 0, 2).reshape(-1)

    gain_one, bias_out = table[0], table[4]
    gain_two, shift_two = table[5], table[6]
    bias_fc1, bias_fc2 = vector(7, 7 + per), table[7 + per]
    o_mine, o_sent, lse = attention_forward(qkv, half, valid)
    o_got = other(o_sent)
    out_mine = lax.dynamic_slice_in_dim(out_full, here * group, group, axis=0)
    out_other = lax.dynamic_slice_in_dim(out_full, group - here * group, group, axis=0)
    residual = pad(frames_in).astype(F32) + dot(o_mine, out_mine) + dot(o_got, out_other) + bias_out

    normed_two, _ = normalize(residual)
    hidden_two = (normed_two * gain_two + shift_two).astype(BF)
    pre_act = dot(hidden_two, fc1_full) + bias_fc1
    cdf = gelu_cdf(pre_act)
    density = jnp.exp(-0.5 * pre_act * pre_act) * (1.0 / math.sqrt(2.0 * math.pi))
    activated, slope = lax.optimization_barrier(
        ((pre_act * cdf).astype(BF), (cdf + pre_act * density).astype(BF))
    )
    flag = jnp.full((1,), here, jnp.int32)
    (
        grad_pre_low, fc2_full, grad_residual, grad_residual_low,
        do_mine, do_sent, grad_bias_fc1, grad_sums,
    ) = feed_back(flag, weights, slope, cotangent, residual, gain_two[None], part)
    do_got = other(do_sent)
    parity = jnp.full((1,), lax.rem(me, 2), jnp.int32)
    fc2_keep, fc2_give = third_gradient(parity, activated, cotangent, size, do_sent)
    second_part = second_gradient(
        flag, fc2_give, o_mine, o_got, grad_residual_low, hidden_two, grad_pre_low
    )
    grad_second = lax.psum_scatter(second_part, "dp", scatter_dimension=0, tiled=True)

    def backward(token, start, count):
        return attention_backward(
            qkv, o_mine, o_sent, do_mine, do_got, lse, token, half, valid, start, count
        )

    x = fc2_keep.astype(F32) + swap(fc2_give, "dp", size, 1).astype(F32)
    x = x.reshape(size // 2, 2, -1, wide)
    keep, give = pick(x, 1, here).astype(BF), pick(x, 1, 1 - here).astype(BF)
    got = other(give)
    pairs = group // 128
    ds = [backward(give, 0, pairs - 1)]
    for at in range(len(bits) - 2, -1, -1):
        keep, got = after((keep, got), ds[0])
        x = keep.astype(F32) + got.astype(F32)
        keep, give = halve(x.reshape(-1, 2, *x.shape[1:]), 1, bits[at])
        keep, got = keep.astype(BF), swap(give, "dp", size, bits[at])
    fc2_keep_x, fc2_got_x = keep, got
    ds.append(backward(give, pairs - 1, 1))

    vectors = [(7, grad_bias_fc1)]
    if part % 16:
        grad_qkv, norm_sums, sums = projection_weight_gradient(normed_t, w_full, scale, ds)
        grad_bias_mine = jnp.stack([sums[0, :group], sums[0, 2 * group :]])
        zero = jnp.zeros_like(grad_bias_mine)
        grad_bias_qv = jnp.where(
            here == 0,
            jnp.concatenate([grad_bias_mine, zero], axis=1),
            jnp.concatenate([zero, grad_bias_mine], axis=1),
        )

        def as_columns(start, v):
            v = v.reshape(size, -1, part).transpose(0, 2, 1)
            return jnp.pad(v, ((0, 0), (0, 0), (start, 128 - start - v.shape[2])))

        columns = norm_sums.reshape(size, part, 128) + as_columns(2, grad_bias_qv)
        vectors += [(p, grad_sums[i]) for i, p in enumerate((4, 5, 6, 7 + per))]
        columns = columns + sum(as_columns(start, v) for start, v in vectors)
        x = jnp.concatenate([grad_qkv.reshape(size, part, -1), columns.astype(BF)], axis=2)
        keep, give = halve(x.reshape(size // 2, 2, *x.shape[1:]), 1, 1)
    else:
        sides = jnp.concatenate([parity, jnp.full((1,), here, jnp.int32)])
        keep, give = spread_weight_gradient(
            sides, ds[1], normed_t, w_full, scale, ds, grad_bias_fc1, grad_sums, part
        )
    got = swap(give, "dp", size, 1)
    for at in range(len(bits) - 2, -1, -1):
        x = keep.astype(F32) + got.astype(F32)
        keep, give = halve(x.reshape(-1, 2, *x.shape[1:]), 1, bits[at])
        got = swap(give, "dp", size, bits[at])
    fc2_keep, fc2_got = after((fc2_keep_x, fc2_got_x), give)
    fc2_gives, fc2_stay = scatter_split(fc2_keep.astype(F32) + fc2_got.astype(F32), size)
    grad_other, grad_mine = projection_input_gradient(w_flipped, ds, fc2_gives[2], half)
    grad_got = other(grad_other)
    output = dot(after(activated, *fc2_gives), fc2_full)
    output = residual + output + bias_fc2
    frames_out = output.astype(BF)[:valid][None]
    fc2_part = scatter_join(fc2_stay, fc2_gives, size).astype(BF)
    gives, stay = scatter_split(keep.astype(F32) + got.astype(F32), size)
    grad_input = input_end(
        grad_mine, grad_got, grad_residual, normed_both, gain_one[None], inverse_one, valid
    ).transpose(1, 0, 2)
    mine = scatter_join(stay, gives, size).astype(BF)
    theirs = other(mine)
    spans = ((0, 1), (1, 2), (2, 4), (4, 5), (5, 6), (6, 7), (7, 7 + per), (7 + per, 8 + per))
    grad_w_qkv, *small = finish(flag, mine, theirs, spans)
    small = [v[0] for v in small]
    fc2_got = other(fc2_part)
    fc2_sum = jnp.where(
        here == 0,
        jnp.concatenate([fc2_part, fc2_got], axis=0),
        jnp.concatenate([fc2_got, fc2_part], axis=0),
    ).astype(F32)
    out_sum, first_sum = join_second(grad_second, other(grad_second), wide)
    return (
        frames_out, grad_input, small[0], small[1], grad_w_qkv, small[2], out_sum, small[3],
        small[4], small[5], first_sum, small[6], fc2_sum, small[7],
    )


def solution(mesh):
    frames, rows, vector = P("dp", "seq", None), P("dp", None), P("dp")
    in_specs = (
        frames, vector, vector, rows, vector, rows, vector,
        vector, vector, rows, vector, rows, vector, frames,
    )
    out_specs = (
        frames, frames, vector, vector, rows, vector, rows, vector,
        vector, vector, rows, vector, rows, vector,
    )
    return jax.shard_map(
        functools.partial(layer, mesh.shape["dp"]),
        mesh=mesh, in_specs=in_specs, out_specs=out_specs, check_vma=False,
    )
```

```python
import functools
import math

import jax
import jax.numpy as jnp
from jax import lax
from jax.experimental import pallas as pl
from jax.experimental.pallas import tpu as pltpu
from jax.sharding import PartitionSpec as P


EPSILON = 1e-05
BF = jnp.bfloat16
F32 = jnp.float32
MASKED = -1e30


def dot(a, b, ca=1, cb=0):
    return lax.dot_general(a, b, (((ca,), (cb,)), ((), ())), preferred_element_type=F32)


def split3(x):
    high = x.astype(BF).astype(F32)
    rest = x - high
    mid = rest.astype(BF).astype(F32)
    return high, mid, (rest - mid).astype(BF).astype(F32)


def forward_kernel(half, valid, q_ref, k_ref, v_ref, mine_ref, sent_ref, lse_ref, kx_ref, vt_ref):
    rows = k_ref.shape[0]
    wide = q_ref.shape[0]

    kx_ref[:, :128] = k_ref[...]
    row = lax.broadcasted_iota(jnp.int32, (rows, 128), 0)
    lane = lax.broadcasted_iota(jnp.int32, (rows, 128), 1)
    padded = (lax.rem(row, half) >= valid) & (lane == 0)
    kx_ref[:, 128:] = jnp.where(padded, MASKED, 0.0).astype(BF)
    vt = v_ref[...].T
    vt_ref[0:64, :] = vt[0:64, :]
    vt_ref[64:80, :] = jnp.ones((16, rows), BF)
    vt_ref[80:144, :] = vt[64:128, :]
    vt_ref[144:160, :] = jnp.ones((16, rows), BF)

    lane = lax.broadcasted_iota(jnp.int32, (wide, 128), 1)
    q = q_ref[...] * jnp.asarray(0.125, BF)
    one = jnp.where(lane == 0, 1.0, 0.0).astype(BF)
    outs, sums = [], []
    for h in range(2):
        mine = (lane < 64) if h == 0 else (lane >= 64)
        qx = jnp.concatenate([jnp.where(mine, q, jnp.zeros_like(q)), one], axis=1)
        s = dot(kx_ref[...], qx, 1, 1)
        peak = jnp.max(s, axis=0, keepdims=True)
        p = jnp.exp(s - peak).astype(BF)
        o = dot(vt_ref[80 * h : 80 * h + 80, :], p)
        total = o[64:65, :]
        outs.append(o[0:64, :] / total)
        sums.append(peak + jnp.log(total))
    o = jnp.concatenate(outs, axis=0).T.astype(BF)
    mine_ref[...] = o[:half]
    sent_ref[...] = o[half:]
    lse_ref[...] = jnp.concatenate(sums + [jnp.zeros((6, wide), F32)], axis=0)[None]


def attention_forward(qkv, half, valid):
    rows, width = qkv.shape
    pairs = width // 3 // 128
    block = pl.BlockSpec((half, 128), lambda p: (0, p))
    return pl.pallas_call(
        functools.partial(forward_kernel, half, valid),
        grid=(pairs,),
        in_specs=[
            pl.BlockSpec((rows, 128), lambda p: (0, p)),
            pl.BlockSpec((rows, 128), lambda p: (0, pairs + p)),
            pl.BlockSpec((rows, 128), lambda p: (0, 2 * pairs + p)),
        ],
        out_specs=[block, block, pl.BlockSpec((1, 8, rows), lambda p: (p, 0, 0))],
        out_shape=[
            jax.ShapeDtypeStruct((half, pairs * 128), BF),
            jax.ShapeDtypeStruct((half, pairs * 128), BF),
            jax.ShapeDtypeStruct((pairs, 8, rows), F32),
        ],
        scratch_shapes=[pltpu.VMEM((rows, 256), BF), pltpu.VMEM((160, rows), BF)],
        cost_estimate=pl.CostEstimate(
            flops=pairs * 2 * 4 * rows * rows * 256,
            bytes_accessed=rows * width * 2 + rows * width,
            transcendentals=pairs * 2 * rows * rows,
        ),
        name="attention_forward",
    )(qkv, qkv, qkv)


def backward_kernel(
    half, valid, q_ref, k_ref, v_ref, o_mine_ref, o_sent_ref, mine_ref, got_ref, lse_ref, token_ref,
    d_ref, kt_ref, vt_ref, dkt_ref, dvt_ref,
):
    rows = k_ref.shape[0]
    step = pl.program_id(1)

    @pl.when(step == 0)
    def _():
        kt_ref[0:128, :] = k_ref[...].T
        vt_ref[0:128, :] = v_ref[...].T
        row = lax.broadcasted_iota(jnp.int32, (128, rows), 0)
        key = lax.broadcasted_iota(jnp.int32, (128, rows), 1)
        bias = jnp.where(lax.rem(key, half) >= valid, MASKED, 0.0)
        ones = jnp.where((row >= 1) & (row < 4), 1.0, 0.0)
        kt_ref[128:256, :] = jnp.where(row == 0, bias, ones).astype(BF)
        vt_ref[128:256, :] = ones.astype(BF)
        dkt_ref[...] = jnp.zeros_like(dkt_ref)
        dvt_ref[...] = jnp.zeros_like(dvt_ref)

    tile = q_ref.shape[0]
    first = step < half // tile
    lane = lax.broadcasted_iota(jnp.int32, (tile, 128), 1)
    q = q_ref[...] * jnp.asarray(0.125, BF)
    do = jnp.where(first, mine_ref[...], got_ref[...])
    o = jnp.where(first, o_mine_ref[...], o_sent_ref[...])
    product = do.astype(F32) * o.astype(F32)
    lse = lse_ref[0].T
    qt, dot_t = q.T, do.T

    def extra(x, first):
        a, b, c = split3(-x)
        tail = jnp.where(lane == 2, b, jnp.where(lane == 3, c, 0.0))
        return jnp.where(lane == 0, first, jnp.where(lane == 1, a, tail)).astype(BF)

    dq = []
    for h in range(2):
        mine = (lane < 64) if h == 0 else (lane >= 64)
        delta = jnp.sum(jnp.where(mine, product, 0.0), axis=1, keepdims=True)
        qx = jnp.concatenate(
            [jnp.where(mine, q, jnp.zeros_like(q)), extra(lse[:, h : h + 1], 1.0)], axis=1
        )
        dx = jnp.concatenate([jnp.where(mine, do, jnp.zeros_like(do)), extra(delta, 0.0)], axis=1)
        p = jnp.exp(dot(qx, kt_ref[...]))
        low = p.astype(BF)
        ds = (p * dot(dx, vt_ref[...])).astype(BF)
        dq.append(dot(ds, k_ref[...]))
        part = slice(64 * h, 64 * h + 64)
        dkt_ref[part, :] += dot(qt[part, :], ds)
        dvt_ref[part, :] += dot(dot_t[part, :], low)
    dq = (jnp.where(lane < 64, dq[0], dq[1]) * 0.125).astype(BF)
    d_ref[0, pl.ds(pl.multiple_of(step * tile, 128), tile), :] = dq

    @pl.when(step == pl.num_programs(1) - 1)
    def _():
        d_ref[1] = dkt_ref[...].T.astype(BF)
        d_ref[2] = dvt_ref[...].T.astype(BF)


def attention_backward(qkv, o_mine, o_sent, do_mine, do_got, lse, token, half, valid, start, count):
    rows, width = qkv.shape
    pairs = width // 3 // 128

    def whole(part):
        return pl.BlockSpec((rows, 128), lambda p, i: (0, part * pairs + start + p))

    tile = 256
    per_half = half // tile
    block = pl.BlockSpec((tile, 128), lambda p, i: (i, start + p))
    fixed = pl.BlockSpec((tile, 128), lambda p, i: (lax.rem(i, per_half), start + p))
    return pl.pallas_call(
        functools.partial(backward_kernel, half, valid),
        grid=(count, 2 * per_half),
        in_specs=[
            block, whole(1), whole(2), fixed, fixed, fixed, fixed,
            pl.BlockSpec((1, 8, tile), lambda p, i: (start + p, 0, i)),
            pl.BlockSpec(memory_space=pl.ANY),
        ],
        out_specs=pl.BlockSpec((3, rows, 128), lambda p, i: (0, 0, p)),
        out_shape=jax.ShapeDtypeStruct((3, rows, count * 128), BF),
        scratch_shapes=[
            pltpu.VMEM((256, rows), BF),
            pltpu.VMEM((256, rows), BF),
            pltpu.VMEM((128, rows), F32),
            pltpu.VMEM((128, rows), F32),
        ],
        cost_estimate=pl.CostEstimate(
            flops=count * 2 * 8 * rows * rows * 256,
            bytes_accessed=count * rows * 128 * 16,
            transcendentals=count * 2 * rows * rows,
        ),
        name="attention_backward",
    )(qkv, qkv, qkv, o_mine, o_sent, do_mine, do_got, lse, token)


def rows_below(x, start, valid):
    row = start + lax.broadcasted_iota(jnp.int32, x.shape, 0)
    return jnp.where(row < valid, x, jnp.zeros_like(x))


def prepare_kernel(valid, x_ref, *refs):
    normed_ref, flipped_ref, inverse_ref = refs[-3:]
    tile, wide = normed_ref.shape
    x = rows_below(x_ref[0].astype(F32), pl.program_id(0) * tile, valid)
    centered = x - jnp.mean(x, axis=-1, keepdims=True)
    inverse = lax.rsqrt(jnp.mean(centered * centered, axis=-1, keepdims=True) + EPSILON)
    normed = centered * inverse
    normed_ref[...] = normed
    inverse_ref[...] = jnp.broadcast_to(inverse, inverse_ref.shape)
    flipped_ref[:wide, :] = normed.T.astype(BF)
    flipped_ref[wide:, :] = jnp.ones((16, tile), BF)


def prepare(frames, half, block, filled=()):
    _, valid, wide = frames.shape
    tile = 384
    first = block * (half // tile)
    return pl.pallas_call(
        functools.partial(prepare_kernel, valid),
        grid=(half // tile,),
        in_specs=[pl.BlockSpec((1, tile, wide), lambda i: (0, i, 0))]
        + [pl.BlockSpec(memory_space=pl.ANY)] * len(filled),
        out_specs=[
            pl.BlockSpec((tile, wide), lambda i: (first + i, 0)),
            pl.BlockSpec((wide + 16, tile), lambda i: (0, first + i)),
            pl.BlockSpec((tile, 128), lambda i: (i, 0)),
        ],
        out_shape=[
            jax.ShapeDtypeStruct((2 * half, wide), F32),
            jax.ShapeDtypeStruct((wide + 16, 2 * half), BF),
            jax.ShapeDtypeStruct((half, 128), F32),
        ],
        input_output_aliases={1: 0, 2: 1} if filled else {},
        cost_estimate=pl.CostEstimate(
            flops=half * wide * 16, bytes_accessed=half * wide * 8, transcendentals=half
        ),
        name="prepare",
    )(frames, *filled)


def attend_kernel(valid, place_ref, x_ref, mine_ref, got_ref, w_ref, rows_ref, sum_ref, h_ref):
    tile = sum_ref.shape[0]
    group = mine_ref.shape[1]
    here = place_ref[0]
    first = w_ref[pl.ds(pl.multiple_of(here * group, 128), group), :]
    other = w_ref[pl.ds(pl.multiple_of(group - here * group, 128), group), :]
    total = dot(mine_ref[...], first) + dot(got_ref[...], other)
    x = rows_below(x_ref[0].astype(F32), pl.program_id(0) * tile, valid)
    total = x + total + rows_ref[4:5, :]
    sum_ref[...] = total
    centered = total - jnp.mean(total, axis=-1, keepdims=True)
    inverse = lax.rsqrt(jnp.mean(centered * centered, axis=-1, keepdims=True) + EPSILON)
    h_ref[...] = (centered * inverse * rows_ref[5:6, :] + rows_ref[6:7, :]).astype(BF)


def attend(here, frames, mine, got, w, column, table):
    _, valid, wide = frames.shape
    half, group = mine.shape
    tile = 128
    block = pl.BlockSpec((tile, group), lambda i, p: (i, 0))
    out = pl.BlockSpec((tile, wide), lambda i, p: (i, 0))
    return pl.pallas_call(
        functools.partial(attend_kernel, valid),
        grid_spec=pltpu.PrefetchScalarGridSpec(
            num_scalar_prefetch=1,
            grid=(half // tile,),
            in_specs=[
                pl.BlockSpec((1, tile, wide), lambda i, p: (0, i, 0)), block, block,
                pl.BlockSpec((wide, wide), lambda i, p: (0, column)),
                pl.BlockSpec((16, wide), lambda i, p: (0, 0)),
            ],
            out_specs=[out, out],
        ),
        out_shape=[
            jax.ShapeDtypeStruct((half, wide), F32),
            jax.ShapeDtypeStruct((half, wide), BF),
        ],
        cost_estimate=pl.CostEstimate(
            flops=4 * half * wide * group, bytes_accessed=half * wide * 10, transcendentals=half
        ),
        name="attend",
    )(here, frames, mine, got, w, table)


def projection_kernel(
    part, group, place_ref, held_ref, x_ref, qkv_ref, w_ref, wt_ref, rows_ref, scale_ref,
    gain_ref, bias_ref, columns_ref,
):
    wide, width = w_ref.shape

    @pl.when(pl.program_id(0) == 0)
    def _():
        blocks, extent, _ = held_ref.shape
        for d in range(blocks):
            block = held_ref[place_ref[d]]
            w_ref[d * extent : (d + 1) * extent, :] = block[:, :width]
            columns_ref[d * extent : (d + 1) * extent, :] = block[:, width:].astype(F32)
        wt_ref[...] = w_ref[...].T
        table = columns_ref[...].T[:16, :]
        rows_ref[...] = table
        scale_ref[:, :128] = jnp.broadcast_to(columns_ref[:, 0:1], (wide, 128))
        scale_ref[:, 128:] = jnp.broadcast_to(columns_ref[:, 1:2], (wide, 128))
        gain_ref[...] = table[:8]
        here = place_ref[blocks]
        lane = lax.broadcasted_iota(jnp.int32, (wide, group), 0)
        entry = lax.broadcasted_iota(jnp.int32, (wide, group), 1)
        base = lane + part * (lane // part) - group * here
        low = table.astype(BF)
        for v in range(2):
            total = jnp.zeros((16, group), F32)
            for j in range(2):
                chosen = entry == base + part * j - wide * v
                picked = dot(low, jnp.where(chosen, 1.0, 0.0).astype(BF))
                total = total + picked[2 + j : 3 + j, :]
            bias_ref[:, 2 * v * group : (2 * v + 1) * group] = total[:8]
        bias_ref[:, group : 2 * group] = jnp.zeros((8, group), F32)

    h = (x_ref[...] * gain_ref[0:1, :] + gain_ref[1:2, :]).astype(BF)
    qkv_ref[...] = (dot(h, w_ref[...]) + bias_ref[0:1, :]).astype(BF)


def projection(held, place, normed, part):
    blocks, extent, across = held.shape
    width = across - 128
    rows, wide = normed.shape
    tile = 384

    def fixed(*shape):
        return pl.BlockSpec(shape, lambda i, p: tuple(0 for _ in shape))

    return pl.pallas_call(
        functools.partial(projection_kernel, part, width // 3),
        grid_spec=pltpu.PrefetchScalarGridSpec(
            num_scalar_prefetch=1,
            grid=(rows // tile,),
            in_specs=[fixed(blocks, extent, across), pl.BlockSpec((tile, wide), lambda i, p: (i, 0))],
            out_specs=[
                pl.BlockSpec((tile, width), lambda i, p: (i, 0)),
                fixed(wide, width), fixed(width, wide), fixed(16, wide), fixed(wide, 256),
            ],
            scratch_shapes=[
                pltpu.VMEM((8, wide), F32),
                pltpu.VMEM((8, width), F32),
                pltpu.VMEM((wide, 128), F32),
            ],
        ),
        out_shape=[
            jax.ShapeDtypeStruct((rows, width), BF),
            jax.ShapeDtypeStruct((wide, width), BF),
            jax.ShapeDtypeStruct((width, wide), BF),
            jax.ShapeDtypeStruct((16, wide), F32),
            jax.ShapeDtypeStruct((wide, 256), F32),
        ],
        cost_estimate=pl.CostEstimate(
            flops=2 * rows * wide * width, bytes_accessed=rows * wide * 8, transcendentals=0
        ),
        name="projection",
    )(place, held, normed)


def weight_kernel(pieces, xt_ref, w_ref, scale_ref, *refs):
    d_refs, (g_ref, c_ref, s_ref) = refs[:pieces], refs[pieces:]
    d = jnp.concatenate([r[0] for r in d_refs], axis=1)
    m = dot(xt_ref[...], d)
    s = m[w_ref.shape[0] :][:8]
    m = m[: w_ref.shape[0]]
    s_ref[...] = s
    gain, shift = scale_ref[:, 0:1], scale_ref[:, 128:129]
    total = s[0:1, :]
    g_ref[...] = (gain * m + shift * total).astype(BF)
    w = w_ref[...].astype(F32)
    lane = lax.broadcasted_iota(jnp.int32, c_ref.shape, 1)
    first = jnp.sum(w * m, axis=1, keepdims=True)
    second = jnp.sum(w * total, axis=1, keepdims=True)
    now = jnp.where(lane == 0, first, jnp.where(lane == 1, second, 0.0))
    before = jnp.where(pl.program_id(0) == 0, jnp.zeros_like(now), c_ref[...])
    c_ref[...] = before + now


def projection_weight_gradient(xt, w, scale, ds):
    tall, rows = xt.shape
    wide = w.shape[0]
    group = sum(d.shape[2] for d in ds)
    return pl.pallas_call(
        functools.partial(weight_kernel, len(ds)),
        grid=(3,),
        in_specs=[
            pl.BlockSpec((tall, rows), lambda j: (0, 0)),
            pl.BlockSpec((wide, group), lambda j: (0, j)),
            pl.BlockSpec((wide, 256), lambda j: (0, 0)),
        ]
        + [pl.BlockSpec((1, *d.shape[1:]), lambda j: (j, 0, 0)) for d in ds],
        out_specs=[
            pl.BlockSpec((wide, group), lambda j: (0, j)),
            pl.BlockSpec((wide, 128), lambda j: (0, 0)),
            pl.BlockSpec((8, group), lambda j: (0, j)),
        ],
        out_shape=[
            jax.ShapeDtypeStruct((wide, 3 * group), BF),
            jax.ShapeDtypeStruct((wide, 128), F32),
            jax.ShapeDtypeStruct((8, 3 * group), F32),
        ],
        cost_estimate=pl.CostEstimate(
            flops=2 * rows * wide * 3 * group, bytes_accessed=rows * wide * 4, transcendentals=0
        ),
        name="projection_weight_gradient",
    )(xt, w, scale, *ds)


def spread_kernel(
    part, pieces, per, place_ref, token_ref, xt_ref, w_ref, scale_ref, *refs
):
    d_refs, refs = refs[:pieces], refs[pieces:]
    b_ref, v_ref, keep_ref, give_ref, c_ref, s_ref, first_ref, second_ref = refs
    step = pl.program_id(0)
    wide, group = w_ref.shape
    d = jnp.concatenate([r[0] for r in d_refs], axis=1)
    m = dot(xt_ref[...], d)
    s = m[wide : wide + 8]
    s_ref[step] = s

    @pl.when(step == 0)
    def _():
        first_ref[...] = jnp.zeros_like(first_ref)
        second_ref[...] = jnp.zeros_like(second_ref)

    gain, shift = scale_ref[:, :128], scale_ref[:, 128:]
    one, two, gs = first_ref[...], second_ref[...], []
    for i in range(group // 128):
        columns = slice(128 * i, 128 * (i + 1))
        piece, w, total = m[:wide, columns], w_ref[:, columns].astype(F32), s[0:1, columns]
        one, two = one + w * piece, two + w * total
        gs.append((gain * piece + shift * total).astype(BF))
    first_ref[...], second_ref[...] = one, two
    at = pl.ds(pl.multiple_of(step * group, 128), group)
    spread_store(part, place_ref, keep_ref, give_ref, jnp.concatenate(gs, axis=1), at)

    @pl.when(step == 2)
    def _():
        lane = lax.broadcasted_iota(jnp.int32, c_ref.shape, 1)
        second = jnp.sum(second_ref[...], axis=1, keepdims=True)
        first = jnp.sum(first_ref[...], axis=1, keepdims=True)
        columns = jnp.where(lane == 0, first, jnp.where(lane == 1, second, 0.0))
        small = v_ref[...].T
        for i, name in enumerate((4, 5, 6, 7 + per)):
            columns = jnp.where(lane == name, small[:, i : i + 1], columns)
        v = jnp.broadcast_to(b_ref[...], (8, b_ref.shape[1])).T[:, 0:1]
        for j in range(per):
            column = jnp.concatenate(
                [v[(d * per + j) * part :][:part] for d in range(wide // part)], axis=0
            )
            columns = jnp.where(lane == 7 + j, column, columns)
        c_ref[...] = columns
        half = group // 2
        low = lane[:half]
        for side in (0, 2):
            v = s_ref[side].T[:, 0:1]
            at = pl.ds(pl.multiple_of(place_ref[1] * half + side * wide // 4, 64), half)
            block = c_ref[at, :]
            for j in range(2):
                column = jnp.concatenate(
                    [v[(2 * d + j) * part :][:part] for d in range(half // part)], axis=0
                )
                block = jnp.where(low == 2 + j, column, block)
            c_ref[at, :] = block
        g = c_ref[...].astype(BF)
        spread_store(part, place_ref, keep_ref, give_ref, g, pl.ds(3 * group, 128))


def spread_store(part, place_ref, keep_ref, give_ref, value, columns):
    value = value.reshape(keep_ref.shape[0], 2, part, value.shape[1])
    even, odd = value[:, 0], value[:, 1]
    low = place_ref[0] == 0
    keep_ref[:, :, columns] = jnp.where(low, even, odd)
    give_ref[:, :, columns] = jnp.where(low, odd, even)


def spread_weight_gradient(place, token, xt, w, scale, ds, bias, sums, part):
    _, rows = xt.shape
    wide = w.shape[0]
    group = sum(d.shape[2] for d in ds)
    size = wide // part
    out = pl.BlockSpec((size // 2, part, 3 * group + 128), lambda j, p: (0, 0, 0))

    def fixed(x):
        return pl.BlockSpec(x.shape, lambda j, p: (0, 0))

    return pl.pallas_call(
        functools.partial(spread_kernel, part, len(ds), bias.shape[1] // wide),
        grid_spec=pltpu.PrefetchScalarGridSpec(
            num_scalar_prefetch=1,
            grid=(3,),
            in_specs=[
                pl.BlockSpec(memory_space=pl.ANY),
                fixed(xt),
                pl.BlockSpec((wide, group), lambda j, p: (0, j)),
                fixed(scale),
            ]
            + [pl.BlockSpec((1, *d.shape[1:]), lambda j, p: (j, 0, 0)) for d in ds]
            + [fixed(bias), fixed(sums)],
            out_specs=[out, out],
            scratch_shapes=[
                pltpu.VMEM((wide, 128), F32),
                pltpu.VMEM((3, 8, group), F32),
                pltpu.VMEM((wide, 128), F32),
                pltpu.VMEM((wide, 128), F32),
            ],
        ),
        out_shape=[jax.ShapeDtypeStruct((size // 2, part, 3 * group + 128), BF)] * 2,
        cost_estimate=pl.CostEstimate(
            flops=2 * rows * wide * 3 * group, bytes_accessed=rows * wide * 4, transcendentals=0
        ),
        name="spread_weight_gradient",
    )(place, token, xt, w, scale, *ds, bias, sums)


def input_kernel(pieces, token_ref, wt_ref, *refs):
    d_refs, out_ref = refs[:pieces], refs[pieces]
    d = jnp.concatenate([r[j] for j in range(3) for r in d_refs], axis=1)
    out_ref[...] = dot(d, wt_ref[...]).astype(out_ref.dtype)


def projection_input_gradient(wt, ds, token, half, block, kind):
    wide = wt.shape[1]
    tile = 256
    start = block * (half // tile)
    return pl.pallas_call(
        functools.partial(input_kernel, len(ds)),
        grid=(half // tile,),
        in_specs=[pl.BlockSpec(memory_space=pl.ANY), pl.BlockSpec(wt.shape, lambda i: (0, 0))]
        + [pl.BlockSpec((3, tile, d.shape[2]), lambda i: (0, start + i, 0)) for d in ds],
        out_specs=pl.BlockSpec((tile, wide), lambda i: (i, 0)),
        out_shape=jax.ShapeDtypeStruct((half, wide), kind),
        cost_estimate=pl.CostEstimate(
            flops=2 * half * wt.size, bytes_accessed=half * wt.shape[0] * 4, transcendentals=0
        ),
        name="projection_input_gradient",
    )(token, wt, *ds)


def second_kernel(place_ref, token_ref, mine_ref, got_ref, drb_ref, h_ref, du_ref, out_ref, ht_ref):
    group = mine_ref.shape[1]
    step = pl.program_id(0)

    @pl.when(step == 0)
    def _():
        ht_ref[...] = h_ref[...].T
        here = place_ref[0]
        first = pl.multiple_of(here * group, 128)
        other = pl.multiple_of(group - here * group, 128)
        out_ref[pl.ds(first, group), :] = dot(mine_ref[...], drb_ref[...], 0, 0).astype(BF)
        out_ref[pl.ds(other, group), :] = dot(got_ref[...], drb_ref[...], 0, 0).astype(BF)

    @pl.when(step > 0)
    def _():
        out_ref[...] = dot(ht_ref[...], du_ref[...]).astype(BF)


def second_gradient(here, token, o_mine, o_got, drb, hidden, du):
    rows, wide = hidden.shape
    ff = du.shape[1]

    def fixed(x):
        return pl.BlockSpec(x.shape, lambda i, p: (0, 0))

    return pl.pallas_call(
        second_kernel,
        grid_spec=pltpu.PrefetchScalarGridSpec(
            num_scalar_prefetch=1,
            grid=(1 + ff // wide,),
            in_specs=[
                pl.BlockSpec(memory_space=pl.ANY), fixed(o_mine), fixed(o_got), fixed(drb), fixed(hidden),
                pl.BlockSpec((rows, wide), lambda i, p: (0, jnp.maximum(i - 1, 0))),
            ],
            out_specs=pl.BlockSpec((wide, wide), lambda i, p: (0, i)),
            scratch_shapes=[pltpu.VMEM((wide, rows), BF)],
        ),
        out_shape=jax.ShapeDtypeStruct((wide, wide + ff), BF),
        cost_estimate=pl.CostEstimate(
            flops=2 * rows * wide * (wide + ff), bytes_accessed=rows * ff * 4, transcendentals=0
        ),
        name="second_gradient",
    )(here, token, o_mine, o_got, drb, hidden, du)


def fill_rows(ref, x):
    valid = x.shape[0]
    start = valid // 16 * 16
    ref[start:, :] = jnp.zeros((ref.shape[0] - start, ref.shape[1]), ref.dtype)
    ref[:valid, :] = x


def third_kernel(place_ref, z_ref, cot_ref, token_ref, keep_ref, give_ref, padded_ref):
    @pl.when(pl.program_id(0) == 0)
    def _():
        fill_rows(padded_ref, cot_ref[0])

    value = dot(z_ref[...], padded_ref[...], 0, 0).astype(BF)
    owners, extent, wide = keep_ref.shape
    value = value.reshape(owners, 2, extent, wide)

    @pl.when(place_ref[0] == 0)
    def _():
        keep_ref[...] = value[:, 0]
        give_ref[...] = value[:, 1]

    @pl.when(place_ref[0] == 1)
    def _():
        keep_ref[...] = value[:, 1]
        give_ref[...] = value[:, 0]


def third_gradient(parity, activated, cotangent, size, token):
    _, valid, wide = cotangent.shape
    rows, ff = activated.shape
    extent = ff // size
    owners = wide // extent // 2
    out = pl.BlockSpec((owners, extent, wide), lambda i, p: (i, 0, 0))
    return pl.pallas_call(
        third_kernel,
        grid_spec=pltpu.PrefetchScalarGridSpec(
            num_scalar_prefetch=1,
            grid=(ff // wide,),
            in_specs=[
                pl.BlockSpec((rows, wide), lambda i, p: (0, i)),
                pl.BlockSpec((1, valid, wide), lambda i, p: (0, 0, 0)),
                pl.BlockSpec(memory_space=pl.ANY),
            ],
            out_specs=[out, out],
            scratch_shapes=[pltpu.VMEM((rows, wide), BF)],
        ),
        out_shape=[jax.ShapeDtypeStruct((size // 2, extent, wide), BF)] * 2,
        cost_estimate=pl.CostEstimate(
            flops=2 * rows * wide * ff, bytes_accessed=rows * ff * 4, transcendentals=0
        ),
        name="third_gradient",
    )(parity, activated, cotangent, token)


def feed_back_kernel(
    part, place_ref, fc2_ref, fc1_ref, out_ref, slope_ref, cot_ref, residual_ref, gain_ref,
    du_ref, flat_ref, grad_ref, low_ref, mine_ref, sent_ref, bias_ref, sums_ref,
    total_ref, padded_ref,
):
    step = pl.program_id(0)
    rows, wide = total_ref.shape
    group = mine_ref.shape[1]
    per = fc2_ref.shape[1] // wide

    @pl.when(step == 0)
    def _():
        fill_rows(padded_ref, cot_ref[0])
        total_ref[...] = jnp.zeros_like(total_ref)

    if part:
        for d in range(fc2_ref.shape[0] // part):
            for j in range(per):
                block = fc2_ref[d * part : (d + 1) * part, j * wide : (j + 1) * wide]
                flat_ref[(d * per + j) * part : (d * per + j + 1) * part, :] = block
    else:
        flat_ref[...] = fc2_ref[...]
    du = dot(padded_ref[...], flat_ref[...], 1, 1) * slope_ref[...].astype(F32)
    bias_ref[...] = jnp.sum(du, axis=0, keepdims=True)
    du = du.astype(BF)
    du_ref[...] = du
    total_ref[...] += dot(du, fc1_ref[...], 1, 1)

    @pl.when(step == pl.num_programs(0) - 1)
    def _():
        tile = 64

        def body(i, sums):
            at = pl.ds(pl.multiple_of(i * tile, tile), tile)
            r = residual_ref[at, :]
            centered = r - jnp.mean(r, axis=-1, keepdims=True)
            inverse = lax.rsqrt(jnp.mean(centered * centered, axis=-1, keepdims=True) + EPSILON)
            normed = centered * inverse
            dh = total_ref[at, :]
            weighted = dh * gain_ref[...]
            first = jnp.mean(weighted, axis=-1, keepdims=True)
            second = jnp.mean(weighted * normed, axis=-1, keepdims=True)
            g = padded_ref[at, :].astype(F32)
            grad = g + inverse * (weighted - first - normed * second)
            grad_ref[at, :] = grad
            low_ref[at, :] = grad.astype(BF)
            parts = (grad, dh * normed, dh, g)
            return tuple(s + jnp.sum(p, axis=0, keepdims=True) for s, p in zip(sums, parts, strict=True))

        zero = jnp.zeros((1, wide), F32)
        sums = lax.fori_loop(0, rows // tile, body, (zero,) * 4)
        sums_ref[...] = jnp.concatenate(sums + (jnp.zeros((4, wide), F32),), axis=0)
        here = place_ref[0]
        mine = out_ref[pl.ds(pl.multiple_of(here * group, 128), group), :]
        other = out_ref[pl.ds(pl.multiple_of(group - here * group, 128), group), :]
        sent_ref[...] = dot(low_ref[...], other, 1, 1).astype(BF)
        mine_ref[...] = dot(low_ref[...], mine, 1, 1).astype(BF)


def feed_back(here, weights, slope, cotangent, residual, gain, part):
    rows, ff = slope.shape
    _, valid, wide = cotangent.shape
    group = wide // 2
    per = ff // wide
    if part % 16:
        part = 0
        fc2, fc1, out = weights
        fc2_spec = pl.BlockSpec((wide, wide), lambda i, p: (i, 0))
        fc1_spec = pl.BlockSpec((wide, wide), lambda i, p: (0, i))
        out_spec = pl.BlockSpec((wide, wide), lambda i, p: (0, 0))
    else:
        fc2 = fc1 = out = weights
        fc2_spec = pl.BlockSpec((wide // per, ff), lambda i, p: (i, 0))
        fc1_spec = pl.BlockSpec((wide, wide), lambda i, p: (0, per + 1 + i))
        out_spec = pl.BlockSpec((wide, wide), lambda i, p: (0, per))

    def fixed(*shape):
        return pl.BlockSpec(shape, lambda i, p: tuple(0 for _ in shape))

    block = pl.BlockSpec((rows, wide), lambda i, p: (0, i))
    return pl.pallas_call(
        functools.partial(feed_back_kernel, part),
        grid_spec=pltpu.PrefetchScalarGridSpec(
            num_scalar_prefetch=1,
            grid=(per,),
            in_specs=[
                fc2_spec, fc1_spec, out_spec, block, fixed(1, valid, wide), fixed(rows, wide),
                fixed(1, wide),
            ],
            out_specs=[
                block, pl.BlockSpec((wide, wide), lambda i, p: (i, 0)), fixed(rows, wide),
                fixed(rows, wide), fixed(rows, group), fixed(rows, group),
                pl.BlockSpec((1, wide), lambda i, p: (0, i)), fixed(8, wide),
            ],
            scratch_shapes=[pltpu.VMEM((rows, wide), F32), pltpu.VMEM((rows, wide), BF)],
        ),
        out_shape=[
            jax.ShapeDtypeStruct((rows, ff), BF),
            jax.ShapeDtypeStruct((ff, wide), BF),
            jax.ShapeDtypeStruct((rows, wide), F32),
            jax.ShapeDtypeStruct((rows, wide), BF),
            jax.ShapeDtypeStruct((rows, group), BF),
            jax.ShapeDtypeStruct((rows, group), BF),
            jax.ShapeDtypeStruct((1, ff), F32),
            jax.ShapeDtypeStruct((8, wide), F32),
        ],
        cost_estimate=pl.CostEstimate(
            flops=4 * rows * wide * ff, bytes_accessed=ff * wide * 10, transcendentals=rows
        ),
        name="feed_back",
    )(here, fc2, fc1, out, slope, cotangent, residual, gain)


def finish_kernel(spans, place_ref, mine_ref, theirs_ref, w_ref, *refs):
    here = place_ref[0]
    group = w_ref.shape[1] // 6
    mine, theirs = mine_ref[...].astype(F32), theirs_ref[...].astype(F32)
    for j in range(3):
        part = slice(j * group, (j + 1) * group)
        at = (2 * j * group) + here * group
        w_ref[:, pl.ds(pl.multiple_of(at, 128), group)] = mine[:, part]
        at = (2 * j + 1) * group - here * group
        w_ref[:, pl.ds(pl.multiple_of(at, 128), group)] = theirs[:, part]
    rows = (mine[:, 3 * group :] + theirs[:, 3 * group :]).T
    for (start, stop), ref in zip(spans, refs, strict=True):
        ref[...] = jnp.concatenate([rows[i : i + 1] for i in range(start, stop)], axis=1)


def finish(here, mine, theirs, spans):
    part, across = mine.shape
    width = 2 * (across - 128)

    def fixed(*shape):
        return pl.BlockSpec(shape, lambda i, p: (0, 0))

    sizes = [(1, (stop - start) * part) for start, stop in spans]
    return pl.pallas_call(
        functools.partial(finish_kernel, spans),
        grid_spec=pltpu.PrefetchScalarGridSpec(
            num_scalar_prefetch=1,
            grid=(1,),
            in_specs=[fixed(part, across)] * 2,
            out_specs=[fixed(part, width)] + [fixed(*shape) for shape in sizes],
        ),
        out_shape=[jax.ShapeDtypeStruct((part, width), F32)]
        + [jax.ShapeDtypeStruct(shape, F32) for shape in sizes],
        name="finish",
    )(here, mine, theirs)


def output_kernel(token_ref, z_ref, w_ref, residual_ref, rows_ref, out_ref, total_ref):
    step = pl.program_id(0)

    @pl.when(step == 0)
    def _():
        total_ref[...] = residual_ref[...] + rows_ref[-1:, :]

    total_ref[...] += dot(z_ref[...], w_ref[...])

    @pl.when(step == pl.num_programs(0) - 1)
    def _():
        out_ref[0] = total_ref[: out_ref.shape[1], :].astype(BF)


def output_end(token, activated, w, residual, bias, valid):
    rows, ff = activated.shape
    wide = w.shape[1]
    return pl.pallas_call(
        output_kernel,
        grid=(ff // wide,),
        in_specs=[
            pl.BlockSpec(memory_space=pl.ANY),
            pl.BlockSpec((rows, wide), lambda i: (0, i)),
            pl.BlockSpec((wide, wide), lambda i: (i, 0)),
            pl.BlockSpec((rows, wide), lambda i: (0, 0)),
            pl.BlockSpec((1, wide), lambda i: (0, 0)),
        ],
        out_specs=pl.BlockSpec((1, valid, wide), lambda i: (0, 0, 0)),
        out_shape=jax.ShapeDtypeStruct((1, valid, wide), BF),
        scratch_shapes=[pltpu.VMEM((rows, wide), F32)],
        cost_estimate=pl.CostEstimate(
            flops=2 * rows * wide * ff, bytes_accessed=rows * ff * 4, transcendentals=0
        ),
        name="output_end",
    )(token, activated, w, residual, bias)


def join_kernel(mine_ref, theirs_ref, out_ref, first_ref):
    wide = out_ref.shape[1]
    mine, theirs = mine_ref[...].astype(F32), theirs_ref[...].astype(F32)
    out_ref[...] = mine[:, :wide] + theirs[:, :wide]
    first_ref[...] = mine[:, wide:] + theirs[:, wide:]


def join_second(mine, theirs, wide):
    part, across = mine.shape
    return pl.pallas_call(
        join_kernel,
        out_shape=[
            jax.ShapeDtypeStruct((part, wide), F32),
            jax.ShapeDtypeStruct((part, across - wide), F32),
        ],
        name="join_second",
    )(mine, theirs)


def input_end_kernel(mine_ref, got_ref, residual_ref, normed_ref, gain_ref, inverse_ref, out_ref):
    normed = normed_ref[...]
    weighted = (mine_ref[...] + got_ref[...].astype(F32)) * gain_ref[...]
    first = jnp.mean(weighted, axis=-1, keepdims=True)
    second = jnp.mean(weighted * normed, axis=-1, keepdims=True)
    out_ref[:, 0, :] = residual_ref[...] + inverse_ref[:, 0:1] * (weighted - first - normed * second)


def input_end(mine, got, residual, normed, gain, inverse, valid):
    half, wide = mine.shape
    tile = 256
    block = pl.BlockSpec((tile, wide), lambda i: (i, 0))
    return pl.pallas_call(
        input_end_kernel,
        grid=(half // tile,),
        in_specs=[
            block, block, block, block, pl.BlockSpec((1, wide), lambda i: (0, 0)),
            pl.BlockSpec((tile, 128), lambda i: (i, 0)),
        ],
        out_specs=pl.BlockSpec((tile, 1, wide), lambda i: (i, 0, 0)),
        out_shape=jax.ShapeDtypeStruct((valid, 1, wide), F32),
        cost_estimate=pl.CostEstimate(
            flops=half * wide * 10, bytes_accessed=half * wide * 18, transcendentals=0
        ),
        name="input_end",
    )(mine, got, residual, normed, gain, inverse)


def swap(x, axis, size, bit):
    return lax.ppermute(x, axis, [(i, i ^ bit) for i in range(size)])


def bits_of(size):
    top = size // 4
    return top, [1 << b for b in range(top.bit_length() - 2, -1, -1)]


def gather_blocks(x, size):
    me = lax.axis_index("dp")
    top, bits = bits_of(size)
    held = jnp.stack([x] + [swap(x, "dp", size, j * top) for j in (1, 2, 3)])
    where = [j * top for j in range(4)]
    for bit in bits:
        held = jnp.concatenate([held, swap(held, "dp", size, bit)])
        where = where + [w ^ bit for w in where]
    place = [0] * size
    for i, w in enumerate(where):
        place[w] = i
    return held, jnp.asarray(place, jnp.int32)[me ^ jnp.arange(size)]


def halve(x, axis, bit):
    mine = lax.rem(lax.axis_index("dp") // bit, 2)
    keep = lax.dynamic_index_in_dim(x, mine, axis, keepdims=False)
    give = lax.dynamic_index_in_dim(x, 1 - mine, axis, keepdims=False)
    return keep, give.astype(BF)


def scatter_split(x, size):
    top, _ = bits_of(size)
    mine = lax.axis_index("dp") // top
    gives = [
        lax.dynamic_index_in_dim(x, mine ^ j, 0, keepdims=False).astype(BF) for j in (1, 2, 3)
    ]
    return gives, lax.dynamic_index_in_dim(x, mine, 0, keepdims=False).astype(F32)


def scatter_join(total, gives, size):
    top, _ = bits_of(size)
    for j, give in zip((1, 2, 3), gives, strict=True):
        total = total + swap(give, "dp", size, j * top).astype(F32)
    return total


def after(x, *others):
    return lax.optimization_barrier((x, *others))[0]


def gelu_cdf(values):
    return 0.5 * (1.0 + lax.erf(values * (1.0 / math.sqrt(2.0))))


def layer(
    size, frames_in, ln1_gain, ln1_bias, w_qkv, b_qv, w_o, b_o,
    ln2_gain, ln2_bias, w_fc1, b_fc1, w_fc2, b_fc2, cotangent,
):
    clips, valid, wide = frames_in.shape
    assert clips == 1
    ff = w_fc1.shape[1]
    part = w_qkv.shape[0]
    group = wide // 2
    half = -(-valid // 256) * 256
    here = lax.axis_index("seq")

    def other(x):
        return swap(x, "seq", 2, 1)

    def pick(x, axis, index):
        return lax.dynamic_index_in_dim(x, index, axis, keepdims=False)

    per = ff // wide
    me = lax.axis_index("dp")
    _, bits = bits_of(size)

    vectors = jnp.concatenate([ln1_gain, ln1_bias, b_qv, b_o, ln2_gain, ln2_bias, b_fc1, b_fc2])
    count = vectors.shape[0] // part
    columns = lax.optimization_barrier(
        jnp.pad(vectors.reshape(count, part).T, ((0, 0), (0, 128 - count)))
    )
    w_mine = [
        lax.dynamic_slice_in_dim(w_qkv, j * wide + here * group, group, axis=1) for j in range(3)
    ]
    held, place = gather_blocks(jnp.concatenate(w_mine + [columns], axis=1), size)
    if part % 16:
        held = jnp.take(held, place, axis=0, mode="clip").reshape(1, wide, 3 * group + 128)
        place = jnp.zeros((1,), jnp.int32)
    place = jnp.concatenate([place, jnp.full((1,), here, jnp.int32)])
    fc2_local = w_fc2.reshape(per, part, wide).transpose(1, 0, 2).reshape(part, ff)
    later = lax.all_gather(
        jnp.concatenate([fc2_local, w_o, w_fc1], axis=1), "dp", axis=0, tiled=True
    )
    out_full, fc1_full = later[:, ff : ff + wide], later[:, ff + wide :]
    weights = later
    if part % 16:
        fc2_full = later[:, :ff].reshape(size, part, per, wide)
        weights = (fc2_full.transpose(0, 2, 1, 3).reshape(ff, wide), fc1_full, out_full)

    prepared = prepare(frames_in, half, 0)
    inverse_one = prepared[2]
    normed_both, normed_t, _ = prepare(other(frames_in), half, 1, prepared[:2])
    qkv, w_full, w_flipped, table, scale = projection(held, place, normed_both, part)

    def vector(start, stop):
        return table[start:stop].reshape(-1, size, part).transpose(1, 0, 2).reshape(-1)

    gain_one, gain_two = table[0], table[5]
    bias_fc1, bias_fc2 = vector(7, 7 + per), table[7 + per]
    o_mine, o_sent, lse = attention_forward(qkv, half, valid)
    o_got = other(o_sent)
    flag = jnp.full((1,), here, jnp.int32)
    if part % 16:
        residual, hidden_two = attend(flag, frames_in, o_mine, o_got, out_full, 0, table)
    else:
        residual, hidden_two = attend(flag, frames_in, o_mine, o_got, later, per, table)

    pre_act = dot(hidden_two, fc1_full) + bias_fc1
    cdf = gelu_cdf(pre_act)
    density = jnp.exp(-0.5 * pre_act * pre_act) * (1.0 / math.sqrt(2.0 * math.pi))
    activated, slope = lax.optimization_barrier(
        ((pre_act * cdf).astype(BF), (cdf + pre_act * density).astype(BF))
    )
    (
        grad_pre_low, fc2_full, grad_residual, grad_residual_low,
        do_mine, do_sent, grad_bias_fc1, grad_sums,
    ) = feed_back(flag, weights, slope, cotangent, residual, gain_two[None], part)
    do_got = other(do_sent)
    parity = jnp.full((1,), lax.rem(me, 2), jnp.int32)
    fc2_keep, fc2_give = third_gradient(parity, activated, cotangent, size, do_sent)
    second_part = second_gradient(
        flag, fc2_give, o_mine, o_got, grad_residual_low, hidden_two, grad_pre_low
    )
    grad_second = lax.psum_scatter(second_part, "dp", scatter_dimension=0, tiled=True)

    def backward(token, start, count):
        return attention_backward(
            qkv, o_mine, o_sent, do_mine, do_got, lse, token, half, valid, start, count
        )

    x = fc2_keep.astype(F32) + swap(fc2_give, "dp", size, 1).astype(F32)
    x = x.reshape(size // 2, 2, -1, wide)
    keep, give = pick(x, 1, here).astype(BF), pick(x, 1, 1 - here).astype(BF)
    got = other(give)
    ds = [backward(give, 0, group // 128)]
    grad_other = projection_input_gradient(w_flipped, ds, ds[0], half, 1, BF)
    grad_got = other(grad_other)
    for at in range(len(bits) - 2, -1, -1):
        x = after(keep, grad_other).astype(F32) + got.astype(F32)
        keep, give = halve(x.reshape(-1, 2, *x.shape[1:]), 1, bits[at])
        keep, got = keep.astype(BF), swap(give, "dp", size, bits[at])
    fc2_keep_x, fc2_got_x = keep, got

    vectors = [(7, grad_bias_fc1)]
    if part % 16:
        grad_qkv, norm_sums, sums = projection_weight_gradient(normed_t, w_full, scale, ds)
        grad_bias_mine = jnp.stack([sums[0, :group], sums[0, 2 * group :]])
        zero = jnp.zeros_like(grad_bias_mine)
        grad_bias_qv = jnp.where(
            here == 0,
            jnp.concatenate([grad_bias_mine, zero], axis=1),
            jnp.concatenate([zero, grad_bias_mine], axis=1),
        )

        def as_columns(start, v):
            v = v.reshape(size, -1, part).transpose(0, 2, 1)
            return jnp.pad(v, ((0, 0), (0, 0), (start, 128 - start - v.shape[2])))

        columns = norm_sums.reshape(size, part, 128) + as_columns(2, grad_bias_qv)
        vectors += [(p, grad_sums[i]) for i, p in enumerate((4, 5, 6, 7 + per))]
        columns = columns + sum(as_columns(start, v) for start, v in vectors)
        x = jnp.concatenate([grad_qkv.reshape(size, part, -1), columns.astype(BF)], axis=2)
        keep, give = halve(x.reshape(size // 2, 2, *x.shape[1:]), 1, 1)
    else:
        sides = jnp.concatenate([parity, jnp.full((1,), here, jnp.int32)])
        keep, give = spread_weight_gradient(
            sides, give, normed_t, w_full, scale, ds, grad_bias_fc1, grad_sums, part
        )
    got = swap(give, "dp", size, 1)
    for at in range(len(bits) - 2, -1, -1):
        x = keep.astype(F32) + got.astype(F32)
        keep, give = halve(x.reshape(-1, 2, *x.shape[1:]), 1, bits[at])
        got = swap(give, "dp", size, bits[at])
    fc2_keep, fc2_got = after((fc2_keep_x, fc2_got_x), give)
    fc2_gives, fc2_stay = scatter_split(fc2_keep.astype(F32) + fc2_got.astype(F32), size)
    grad_mine = projection_input_gradient(w_flipped, ds, fc2_gives[2], half, 0, F32)
    frames_out = output_end(
        fc2_gives[2], activated, fc2_full, residual, bias_fc2[None], valid
    )
    fc2_part = scatter_join(fc2_stay, fc2_gives, size).astype(BF)
    gives, stay = scatter_split(keep.astype(F32) + got.astype(F32), size)
    grad_input = input_end(
        grad_mine, grad_got, grad_residual, normed_both, gain_one[None], inverse_one, valid
    ).transpose(1, 0, 2)
    mine = scatter_join(stay, gives, size).astype(BF)
    theirs = other(mine)
    spans = ((0, 1), (1, 2), (2, 4), (4, 5), (5, 6), (6, 7), (7, 7 + per), (7 + per, 8 + per))
    grad_w_qkv, *small = finish(flag, mine, theirs, spans)
    small = [v[0] for v in small]
    fc2_got = other(fc2_part)
    fc2_sum = jnp.where(
        here == 0,
        jnp.concatenate([fc2_part, fc2_got], axis=0),
        jnp.concatenate([fc2_got, fc2_part], axis=0),
    ).astype(F32)
    out_sum, first_sum = join_second(grad_second, other(grad_second), wide)
    return (
        frames_out, grad_input, small[0], small[1], grad_w_qkv, small[2], out_sum, small[3],
        small[4], small[5], first_sum, small[6], fc2_sum, small[7],
    )


def solution(mesh):
    frames, rows, vector = P("dp", "seq", None), P("dp", None), P("dp")
    in_specs = (
        frames, vector, vector, rows, vector, rows, vector,
        vector, vector, rows, vector, rows, vector, frames,
    )
    out_specs = (
        frames, frames, vector, vector, rows, vector, rows, vector,
        vector, vector, rows, vector, rows, vector,
    )
    return jax.shard_map(
        functools.partial(layer, mesh.shape["dp"]),
        mesh=mesh, in_specs=in_specs, out_specs=out_specs, check_vma=False,
    )
```

```python
import functools
import math

import jax
import jax.numpy as jnp
from jax import lax
from jax.experimental import pallas as pl
from jax.experimental.pallas import tpu as pltpu
from jax.sharding import PartitionSpec as P


EPSILON = 1e-05
BF = jnp.bfloat16
F32 = jnp.float32
MASKED = -1e30


def dot(a, b, ca=1, cb=0):
    return lax.dot_general(a, b, (((ca,), (cb,)), ((), ())), preferred_element_type=F32)


def split3(x):
    high = x.astype(BF).astype(F32)
    rest = x - high
    mid = rest.astype(BF).astype(F32)
    return high, mid, (rest - mid).astype(BF).astype(F32)


def forward_kernel(half, valid, q_ref, k_ref, v_ref, mine_ref, sent_ref, lse_ref, kx_ref, vt_ref):
    rows = k_ref.shape[0]
    wide = q_ref.shape[0]

    kx_ref[:, :128] = k_ref[...]
    row = lax.broadcasted_iota(jnp.int32, (rows, 128), 0)
    lane = lax.broadcasted_iota(jnp.int32, (rows, 128), 1)
    padded = (lax.rem(row, half) >= valid) & (lane == 0)
    kx_ref[:, 128:] = jnp.where(padded, MASKED, 0.0).astype(BF)
    vt = v_ref[...].T
    vt_ref[0:64, :] = vt[0:64, :]
    vt_ref[64:80, :] = jnp.ones((16, rows), BF)
    vt_ref[80:144, :] = vt[64:128, :]
    vt_ref[144:160, :] = jnp.ones((16, rows), BF)

    lane = lax.broadcasted_iota(jnp.int32, (wide, 128), 1)
    q = q_ref[...] * jnp.asarray(0.125, BF)
    one = jnp.where(lane == 0, 1.0, 0.0).astype(BF)
    outs, sums = [], []
    for h in range(2):
        mine = (lane < 64) if h == 0 else (lane >= 64)
        qx = jnp.concatenate([jnp.where(mine, q, jnp.zeros_like(q)), one], axis=1)
        s = dot(kx_ref[...], qx, 1, 1)
        peak = jnp.max(s, axis=0, keepdims=True)
        p = jnp.exp(s - peak).astype(BF)
        o = dot(vt_ref[80 * h : 80 * h + 80, :], p)
        total = o[64:65, :]
        outs.append(o[0:64, :] / total)
        sums.append(peak + jnp.log(total))
    o = jnp.concatenate(outs, axis=0).T.astype(BF)
    mine_ref[...] = o[:half]
    sent_ref[...] = o[half:]
    lse_ref[...] = jnp.concatenate(sums + [jnp.zeros((6, wide), F32)], axis=0)[None]


def attention_forward(qkv, half, valid):
    rows, width = qkv.shape
    pairs = width // 3 // 128
    block = pl.BlockSpec((half, 128), lambda p: (0, p))
    return pl.pallas_call(
        functools.partial(forward_kernel, half, valid),
        grid=(pairs,),
        in_specs=[
            pl.BlockSpec((rows, 128), lambda p: (0, p)),
            pl.BlockSpec((rows, 128), lambda p: (0, pairs + p)),
            pl.BlockSpec((rows, 128), lambda p: (0, 2 * pairs + p)),
        ],
        out_specs=[block, block, pl.BlockSpec((1, 8, rows), lambda p: (p, 0, 0))],
        out_shape=[
            jax.ShapeDtypeStruct((half, pairs * 128), BF),
            jax.ShapeDtypeStruct((half, pairs * 128), BF),
            jax.ShapeDtypeStruct((pairs, 8, rows), F32),
        ],
        scratch_shapes=[pltpu.VMEM((rows, 256), BF), pltpu.VMEM((160, rows), BF)],
        cost_estimate=pl.CostEstimate(
            flops=pairs * 2 * 4 * rows * rows * 256,
            bytes_accessed=rows * width * 2 + rows * width,
            transcendentals=pairs * 2 * rows * rows,
        ),
        name="attention_forward",
    )(qkv, qkv, qkv)


def backward_kernel(
    half, valid, q_ref, k_ref, v_ref, o_mine_ref, o_sent_ref, mine_ref, got_ref, lse_ref, token_ref,
    d_ref, kt_ref, vt_ref, dkt_ref, dvt_ref,
):
    rows = k_ref.shape[0]
    step = pl.program_id(1)

    @pl.when(step == 0)
    def _():
        kt_ref[0:128, :] = k_ref[...].T
        vt_ref[0:128, :] = v_ref[...].T
        row = lax.broadcasted_iota(jnp.int32, (128, rows), 0)
        key = lax.broadcasted_iota(jnp.int32, (128, rows), 1)
        bias = jnp.where(lax.rem(key, half) >= valid, MASKED, 0.0)
        ones = jnp.where((row >= 1) & (row < 4), 1.0, 0.0)
        kt_ref[128:256, :] = jnp.where(row == 0, bias, ones).astype(BF)
        vt_ref[128:256, :] = ones.astype(BF)
        dkt_ref[...] = jnp.zeros_like(dkt_ref)
        dvt_ref[...] = jnp.zeros_like(dvt_ref)

    tile = q_ref.shape[0]
    first = step < half // tile
    lane = lax.broadcasted_iota(jnp.int32, (tile, 128), 1)
    q = q_ref[...] * jnp.asarray(0.125, BF)
    do = jnp.where(first, mine_ref[...], got_ref[...])
    o = jnp.where(first, o_mine_ref[...], o_sent_ref[...])
    product = do.astype(F32) * o.astype(F32)
    lse = lse_ref[0].T
    qt, dot_t = q.T, do.T

    def extra(x, first):
        a, b, c = split3(-x)
        tail = jnp.where(lane == 2, b, jnp.where(lane == 3, c, 0.0))
        return jnp.where(lane == 0, first, jnp.where(lane == 1, a, tail)).astype(BF)

    dq = []
    for h in range(2):
        mine = (lane < 64) if h == 0 else (lane >= 64)
        delta = jnp.sum(jnp.where(mine, product, 0.0), axis=1, keepdims=True)
        qx = jnp.concatenate(
            [jnp.where(mine, q, jnp.zeros_like(q)), extra(lse[:, h : h + 1], 1.0)], axis=1
        )
        dx = jnp.concatenate([jnp.where(mine, do, jnp.zeros_like(do)), extra(delta, 0.0)], axis=1)
        p = jnp.exp(dot(qx, kt_ref[...]))
        low = p.astype(BF)
        ds = (p * dot(dx, vt_ref[...])).astype(BF)
        dq.append(dot(ds, k_ref[...]))
        part = slice(64 * h, 64 * h + 64)
        dkt_ref[part, :] += dot(qt[part, :], ds)
        dvt_ref[part, :] += dot(dot_t[part, :], low)
    dq = (jnp.where(lane < 64, dq[0], dq[1]) * 0.125).astype(BF)
    d_ref[0, pl.ds(pl.multiple_of(step * tile, 128), tile), :] = dq

    @pl.when(step == pl.num_programs(1) - 1)
    def _():
        d_ref[1] = dkt_ref[...].T.astype(BF)
        d_ref[2] = dvt_ref[...].T.astype(BF)


def attention_backward(qkv, o_mine, o_sent, do_mine, do_got, lse, token, half, valid, start, count):
    rows, width = qkv.shape
    pairs = width // 3 // 128

    def whole(part):
        return pl.BlockSpec((rows, 128), lambda p, i: (0, part * pairs + start + p))

    tile = 384
    per_half = half // tile
    block = pl.BlockSpec((tile, 128), lambda p, i: (i, start + p))
    fixed = pl.BlockSpec((tile, 128), lambda p, i: (lax.rem(i, per_half), start + p))
    return pl.pallas_call(
        functools.partial(backward_kernel, half, valid),
        grid=(count, 2 * per_half),
        in_specs=[
            block, whole(1), whole(2), fixed, fixed, fixed, fixed,
            pl.BlockSpec((1, 8, tile), lambda p, i: (start + p, 0, i)),
            pl.BlockSpec(memory_space=pl.ANY),
        ],
        out_specs=pl.BlockSpec((3, rows, 128), lambda p, i: (0, 0, p)),
        out_shape=jax.ShapeDtypeStruct((3, rows, count * 128), BF),
        scratch_shapes=[
            pltpu.VMEM((256, rows), BF),
            pltpu.VMEM((256, rows), BF),
            pltpu.VMEM((128, rows), F32),
            pltpu.VMEM((128, rows), F32),
        ],
        cost_estimate=pl.CostEstimate(
            flops=count * 2 * 8 * rows * rows * 256,
            bytes_accessed=count * rows * 128 * 16,
            transcendentals=count * 2 * rows * rows,
        ),
        name="attention_backward",
    )(qkv, qkv, qkv, o_mine, o_sent, do_mine, do_got, lse, token)


def rows_below(x, start, valid):
    row = start + lax.broadcasted_iota(jnp.int32, x.shape, 0)
    return jnp.where(row < valid, x, jnp.zeros_like(x))


def prepare_kernel(valid, x_ref, *refs):
    normed_ref, flipped_ref, inverse_ref = refs[-3:]
    tile, wide = normed_ref.shape
    x = rows_below(x_ref[0].astype(F32), pl.program_id(0) * tile, valid)
    centered = x - jnp.mean(x, axis=-1, keepdims=True)
    inverse = lax.rsqrt(jnp.mean(centered * centered, axis=-1, keepdims=True) + EPSILON)
    normed = centered * inverse
    normed_ref[...] = normed
    inverse_ref[...] = jnp.broadcast_to(inverse, inverse_ref.shape)
    flipped_ref[:wide, :] = normed.T.astype(BF)
    flipped_ref[wide:, :] = jnp.ones((16, tile), BF)


def prepare(frames, half, block, filled=()):
    _, valid, wide = frames.shape
    tile = 384
    first = block * (half // tile)
    return pl.pallas_call(
        functools.partial(prepare_kernel, valid),
        grid=(half // tile,),
        in_specs=[pl.BlockSpec((1, tile, wide), lambda i: (0, i, 0))]
        + [pl.BlockSpec(memory_space=pl.ANY)] * len(filled),
        out_specs=[
            pl.BlockSpec((tile, wide), lambda i: (first + i, 0)),
            pl.BlockSpec((wide + 16, tile), lambda i: (0, first + i)),
            pl.BlockSpec((tile, 128), lambda i: (i, 0)),
        ],
        out_shape=[
            jax.ShapeDtypeStruct((2 * half, wide), F32),
            jax.ShapeDtypeStruct((wide + 16, 2 * half), BF),
            jax.ShapeDtypeStruct((half, 128), F32),
        ],
        input_output_aliases={1: 0, 2: 1} if filled else {},
        cost_estimate=pl.CostEstimate(
            flops=half * wide * 16, bytes_accessed=half * wide * 8, transcendentals=half
        ),
        name="prepare",
    )(frames, *filled)


def attend_kernel(valid, place_ref, x_ref, mine_ref, got_ref, w_ref, rows_ref, sum_ref, h_ref):
    tile = sum_ref.shape[0]
    group = mine_ref.shape[1]
    here = place_ref[0]
    first = w_ref[pl.ds(pl.multiple_of(here * group, 128), group), :]
    other = w_ref[pl.ds(pl.multiple_of(group - here * group, 128), group), :]
    total = dot(mine_ref[...], first) + dot(got_ref[...], other)
    x = rows_below(x_ref[0].astype(F32), pl.program_id(0) * tile, valid)
    total = x + total + rows_ref[4:5, :]
    sum_ref[...] = total
    centered = total - jnp.mean(total, axis=-1, keepdims=True)
    inverse = lax.rsqrt(jnp.mean(centered * centered, axis=-1, keepdims=True) + EPSILON)
    h_ref[...] = (centered * inverse * rows_ref[5:6, :] + rows_ref[6:7, :]).astype(BF)


def attend(here, frames, mine, got, w, column, table):
    _, valid, wide = frames.shape
    half, group = mine.shape
    tile = 256
    block = pl.BlockSpec((tile, group), lambda i, p: (i, 0))
    out = pl.BlockSpec((tile, wide), lambda i, p: (i, 0))
    return pl.pallas_call(
        functools.partial(attend_kernel, valid),
        grid_spec=pltpu.PrefetchScalarGridSpec(
            num_scalar_prefetch=1,
            grid=(half // tile,),
            in_specs=[
                pl.BlockSpec((1, tile, wide), lambda i, p: (0, i, 0)), block, block,
                pl.BlockSpec((wide, wide), lambda i, p: (0, column)),
                pl.BlockSpec((16, wide), lambda i, p: (0, 0)),
            ],
            out_specs=[out, out],
        ),
        out_shape=[
            jax.ShapeDtypeStruct((half, wide), F32),
            jax.ShapeDtypeStruct((half, wide), BF),
        ],
        cost_estimate=pl.CostEstimate(
            flops=4 * half * wide * group, bytes_accessed=half * wide * 10, transcendentals=half
        ),
        name="attend",
    )(here, frames, mine, got, w, table)


def projection_kernel(
    part, group, place_ref, held_ref, x_ref, qkv_ref, w_ref, wt_ref, rows_ref, scale_ref,
    gain_ref, bias_ref, columns_ref,
):
    wide, width = w_ref.shape

    @pl.when(pl.program_id(0) == 0)
    def _():
        blocks, extent, _ = held_ref.shape
        for d in range(blocks):
            block = held_ref[place_ref[d]]
            w_ref[d * extent : (d + 1) * extent, :] = block[:, :width]
            columns_ref[d * extent : (d + 1) * extent, :] = block[:, width:].astype(F32)
        wt_ref[...] = w_ref[...].T
        table = columns_ref[...].T[:16, :]
        rows_ref[...] = table
        scale_ref[:, :128] = jnp.broadcast_to(columns_ref[:, 0:1], (wide, 128))
        scale_ref[:, 128:] = jnp.broadcast_to(columns_ref[:, 1:2], (wide, 128))
        gain_ref[...] = table[:8]
        here = place_ref[blocks]
        few = group // 2
        row = lax.broadcasted_iota(jnp.int32, (few, group), 0)
        entry = lax.broadcasted_iota(jnp.int32, (few, group), 1)
        base = row + part * (row // part)
        for v in range(2):
            at = pl.multiple_of(v * (wide // 2) + here * few, 64)
            low = columns_ref[pl.ds(at, few), :].T[:16].astype(BF)
            total = jnp.zeros((16, group), F32)
            for j in range(2):
                chosen = entry == base + part * j
                picked = dot(low, jnp.where(chosen, 1.0, 0.0).astype(BF))
                total = total + picked[2 + j : 3 + j, :]
            bias_ref[:, 2 * v * group : (2 * v + 1) * group] = total[:8]
        bias_ref[:, group : 2 * group] = jnp.zeros((8, group), F32)

    h = (x_ref[...] * gain_ref[0:1, :] + gain_ref[1:2, :]).astype(BF)
    qkv_ref[...] = (dot(h, w_ref[...]) + bias_ref[0:1, :]).astype(BF)


def projection(held, place, normed, part):
    blocks, extent, across = held.shape
    width = across - 128
    rows, wide = normed.shape
    tile = 384

    def fixed(*shape):
        return pl.BlockSpec(shape, lambda i, p: tuple(0 for _ in shape))

    return pl.pallas_call(
        functools.partial(projection_kernel, part, width // 3),
        grid_spec=pltpu.PrefetchScalarGridSpec(
            num_scalar_prefetch=1,
            grid=(rows // tile,),
            in_specs=[fixed(blocks, extent, across), pl.BlockSpec((tile, wide), lambda i, p: (i, 0))],
            out_specs=[
                pl.BlockSpec((tile, width), lambda i, p: (i, 0)),
                fixed(wide, width), fixed(width, wide), fixed(16, wide), fixed(wide, 256),
            ],
            scratch_shapes=[
                pltpu.VMEM((8, wide), F32),
                pltpu.VMEM((8, width), F32),
                pltpu.VMEM((wide, 128), F32),
            ],
        ),
        out_shape=[
            jax.ShapeDtypeStruct((rows, width), BF),
            jax.ShapeDtypeStruct((wide, width), BF),
            jax.ShapeDtypeStruct((width, wide), BF),
            jax.ShapeDtypeStruct((16, wide), F32),
            jax.ShapeDtypeStruct((wide, 256), F32),
        ],
        cost_estimate=pl.CostEstimate(
            flops=2 * rows * wide * width, bytes_accessed=rows * wide * 8, transcendentals=0
        ),
        name="projection",
    )(place, held, normed)


def weight_kernel(pieces, xt_ref, w_ref, scale_ref, *refs):
    d_refs, (g_ref, c_ref, s_ref) = refs[:pieces], refs[pieces:]
    d = jnp.concatenate([r[0] for r in d_refs], axis=1)
    m = dot(xt_ref[...], d)
    s = m[w_ref.shape[0] :][:8]
    m = m[: w_ref.shape[0]]
    s_ref[...] = s
    gain, shift = scale_ref[:, 0:1], scale_ref[:, 128:129]
    total = s[0:1, :]
    g_ref[...] = (gain * m + shift * total).astype(BF)
    w = w_ref[...].astype(F32)
    lane = lax.broadcasted_iota(jnp.int32, c_ref.shape, 1)
    first = jnp.sum(w * m, axis=1, keepdims=True)
    second = jnp.sum(w * total, axis=1, keepdims=True)
    now = jnp.where(lane == 0, first, jnp.where(lane == 1, second, 0.0))
    before = jnp.where(pl.program_id(0) == 0, jnp.zeros_like(now), c_ref[...])
    c_ref[...] = before + now


def projection_weight_gradient(xt, w, scale, ds):
    tall, rows = xt.shape
    wide = w.shape[0]
    group = sum(d.shape[2] for d in ds)
    return pl.pallas_call(
        functools.partial(weight_kernel, len(ds)),
        grid=(3,),
        in_specs=[
            pl.BlockSpec((tall, rows), lambda j: (0, 0)),
            pl.BlockSpec((wide, group), lambda j: (0, j)),
            pl.BlockSpec((wide, 256), lambda j: (0, 0)),
        ]
        + [pl.BlockSpec((1, *d.shape[1:]), lambda j: (j, 0, 0)) for d in ds],
        out_specs=[
            pl.BlockSpec((wide, group), lambda j: (0, j)),
            pl.BlockSpec((wide, 128), lambda j: (0, 0)),
            pl.BlockSpec((8, group), lambda j: (0, j)),
        ],
        out_shape=[
            jax.ShapeDtypeStruct((wide, 3 * group), BF),
            jax.ShapeDtypeStruct((wide, 128), F32),
            jax.ShapeDtypeStruct((8, 3 * group), F32),
        ],
        cost_estimate=pl.CostEstimate(
            flops=2 * rows * wide * 3 * group, bytes_accessed=rows * wide * 4, transcendentals=0
        ),
        name="projection_weight_gradient",
    )(xt, w, scale, *ds)


def spread_kernel(
    part, pieces, per, place_ref, token_ref, xt_ref, w_ref, scale_ref, *refs
):
    d_refs, refs = refs[:pieces], refs[pieces:]
    b_ref, v_ref, keep_ref, give_ref, c_ref, s_ref, first_ref, second_ref = refs
    step = pl.program_id(0)
    wide, group = w_ref.shape
    d = jnp.concatenate([r[0] for r in d_refs], axis=1)
    m = dot(xt_ref[...], d)
    s = m[wide : wide + 8]
    s_ref[step] = s

    @pl.when(step == 0)
    def _():
        first_ref[...] = jnp.zeros_like(first_ref)
        second_ref[...] = jnp.zeros_like(second_ref)

    gain, shift = scale_ref[:, :128], scale_ref[:, 128:]
    one, two, gs = first_ref[...], second_ref[...], []
    for i in range(group // 128):
        columns = slice(128 * i, 128 * (i + 1))
        piece, w, total = m[:wide, columns], w_ref[:, columns].astype(F32), s[0:1, columns]
        one, two = one + w * piece, two + w * total
        gs.append((gain * piece + shift * total).astype(BF))
    first_ref[...], second_ref[...] = one, two
    at = pl.ds(pl.multiple_of(step * group, 128), group)
    spread_store(part, place_ref, keep_ref, give_ref, jnp.concatenate(gs, axis=1), at)

    @pl.when(step == 2)
    def _():
        lane = lax.broadcasted_iota(jnp.int32, c_ref.shape, 1)
        second = jnp.sum(second_ref[...], axis=1, keepdims=True)
        first = jnp.sum(first_ref[...], axis=1, keepdims=True)
        columns = jnp.where(lane == 0, first, jnp.where(lane == 1, second, 0.0))
        small = v_ref[...].T
        for i, name in enumerate((4, 5, 6, 7 + per)):
            columns = jnp.where(lane == name, small[:, i : i + 1], columns)
        v = jnp.broadcast_to(b_ref[...], (8, b_ref.shape[1])).T[:, 0:1]
        for j in range(per):
            column = jnp.concatenate(
                [v[(d * per + j) * part :][:part] for d in range(wide // part)], axis=0
            )
            columns = jnp.where(lane == 7 + j, column, columns)
        c_ref[...] = columns
        half = group // 2
        low = lane[:half]
        for side in (0, 2):
            v = s_ref[side].T[:, 0:1]
            at = pl.ds(pl.multiple_of(place_ref[1] * half + side * wide // 4, 64), half)
            block = c_ref[at, :]
            for j in range(2):
                column = jnp.concatenate(
                    [v[(2 * d + j) * part :][:part] for d in range(half // part)], axis=0
                )
                block = jnp.where(low == 2 + j, column, block)
            c_ref[at, :] = block
        g = c_ref[...].astype(BF)
        spread_store(part, place_ref, keep_ref, give_ref, g, pl.ds(3 * group, 128))


def spread_store(part, place_ref, keep_ref, give_ref, value, columns):
    value = value.reshape(keep_ref.shape[0], 2, part, value.shape[1])
    even, odd = value[:, 0], value[:, 1]
    low = place_ref[0] == 0
    keep_ref[:, :, columns] = jnp.where(low, even, odd)
    give_ref[:, :, columns] = jnp.where(low, odd, even)


def spread_weight_gradient(place, token, xt, w, scale, ds, bias, sums, part):
    _, rows = xt.shape
    wide = w.shape[0]
    group = sum(d.shape[2] for d in ds)
    size = wide // part
    out = pl.BlockSpec((size // 2, part, 3 * group + 128), lambda j, p: (0, 0, 0))

    def fixed(x):
        return pl.BlockSpec(x.shape, lambda j, p: (0, 0))

    return pl.pallas_call(
        functools.partial(spread_kernel, part, len(ds), bias.shape[1] // wide),
        grid_spec=pltpu.PrefetchScalarGridSpec(
            num_scalar_prefetch=1,
            grid=(3,),
            in_specs=[
                pl.BlockSpec(memory_space=pl.ANY),
                fixed(xt),
                pl.BlockSpec((wide, group), lambda j, p: (0, j)),
                fixed(scale),
            ]
            + [pl.BlockSpec((1, *d.shape[1:]), lambda j, p: (j, 0, 0)) for d in ds]
            + [fixed(bias), fixed(sums)],
            out_specs=[out, out],
            scratch_shapes=[
                pltpu.VMEM((wide, 128), F32),
                pltpu.VMEM((3, 8, group), F32),
                pltpu.VMEM((wide, 128), F32),
                pltpu.VMEM((wide, 128), F32),
            ],
        ),
        out_shape=[jax.ShapeDtypeStruct((size // 2, part, 3 * group + 128), BF)] * 2,
        cost_estimate=pl.CostEstimate(
            flops=2 * rows * wide * 3 * group, bytes_accessed=rows * wide * 4, transcendentals=0
        ),
        name="spread_weight_gradient",
    )(place, token, xt, w, scale, *ds, bias, sums)


def input_kernel(pieces, token_ref, wt_ref, *refs):
    d_refs, out_ref = refs[:pieces], refs[pieces]
    d = jnp.concatenate([r[j] for j in range(3) for r in d_refs], axis=1)
    out_ref[...] = dot(d, wt_ref[...]).astype(out_ref.dtype)


def projection_input_gradient(wt, ds, token, half, block, kind):
    wide = wt.shape[1]
    tile = 384
    start = block * (half // tile)
    return pl.pallas_call(
        functools.partial(input_kernel, len(ds)),
        grid=(half // tile,),
        in_specs=[pl.BlockSpec(memory_space=pl.ANY), pl.BlockSpec(wt.shape, lambda i: (0, 0))]
        + [pl.BlockSpec((3, tile, d.shape[2]), lambda i: (0, start + i, 0)) for d in ds],
        out_specs=pl.BlockSpec((tile, wide), lambda i: (i, 0)),
        out_shape=jax.ShapeDtypeStruct((half, wide), kind),
        cost_estimate=pl.CostEstimate(
            flops=2 * half * wt.size, bytes_accessed=half * wt.shape[0] * 4, transcendentals=0
        ),
        name="projection_input_gradient",
    )(token, wt, *ds)


def second_kernel(place_ref, token_ref, mine_ref, got_ref, drb_ref, h_ref, du_ref, out_ref, ht_ref):
    group = mine_ref.shape[1]
    step = pl.program_id(0)

    @pl.when(step == 0)
    def _():
        ht_ref[...] = h_ref[...].T
        here = place_ref[0]
        first = pl.multiple_of(here * group, 128)
        other = pl.multiple_of(group - here * group, 128)
        out_ref[pl.ds(first, group), :] = dot(mine_ref[...], drb_ref[...], 0, 0).astype(BF)
        out_ref[pl.ds(other, group), :] = dot(got_ref[...], drb_ref[...], 0, 0).astype(BF)

    @pl.when(step > 0)
    def _():
        out_ref[...] = dot(ht_ref[...], du_ref[...]).astype(BF)


def second_gradient(here, token, o_mine, o_got, drb, hidden, du):
    rows, wide = hidden.shape
    ff = du.shape[1]

    def fixed(x):
        return pl.BlockSpec(x.shape, lambda i, p: (0, 0))

    return pl.pallas_call(
        second_kernel,
        grid_spec=pltpu.PrefetchScalarGridSpec(
            num_scalar_prefetch=1,
            grid=(1 + ff // wide,),
            in_specs=[
                pl.BlockSpec(memory_space=pl.ANY), fixed(o_mine), fixed(o_got), fixed(drb), fixed(hidden),
                pl.BlockSpec((rows, wide), lambda i, p: (0, jnp.maximum(i - 1, 0))),
            ],
            out_specs=pl.BlockSpec((wide, wide), lambda i, p: (0, i)),
            scratch_shapes=[pltpu.VMEM((wide, rows), BF)],
        ),
        out_shape=jax.ShapeDtypeStruct((wide, wide + ff), BF),
        cost_estimate=pl.CostEstimate(
            flops=2 * rows * wide * (wide + ff), bytes_accessed=rows * ff * 4, transcendentals=0
        ),
        name="second_gradient",
    )(here, token, o_mine, o_got, drb, hidden, du)


def pack_kernel(fc2_ref, out_ref, fc1_ref, packed_ref):
    part, wide = out_ref.shape
    per = fc2_ref.shape[0] // part
    for j in range(per):
        packed_ref[:, j * wide : (j + 1) * wide] = fc2_ref[j * part : (j + 1) * part, :]
    packed_ref[:, per * wide : (per + 1) * wide] = out_ref[...]
    packed_ref[:, (per + 1) * wide :] = fc1_ref[...]


def pack(w_fc2, w_o, w_fc1):
    part, wide = w_o.shape
    across = wide + 2 * w_fc1.shape[1]
    return pl.pallas_call(
        pack_kernel, out_shape=jax.ShapeDtypeStruct((part, across), BF), name="pack"
    )(w_fc2, w_o, w_fc1)


def fill_rows(ref, x):
    valid = x.shape[0]
    start = valid // 16 * 16
    ref[start:, :] = jnp.zeros((ref.shape[0] - start, ref.shape[1]), ref.dtype)
    ref[:valid, :] = x


def third_kernel(place_ref, z_ref, cot_ref, token_ref, keep_ref, give_ref, padded_ref):
    @pl.when(pl.program_id(0) == 0)
    def _():
        fill_rows(padded_ref, cot_ref[0])

    value = dot(z_ref[...], padded_ref[...], 0, 0).astype(BF)
    owners, extent, wide = keep_ref.shape
    value = value.reshape(owners, 2, extent, wide)

    @pl.when(place_ref[0] == 0)
    def _():
        keep_ref[...] = value[:, 0]
        give_ref[...] = value[:, 1]

    @pl.when(place_ref[0] == 1)
    def _():
        keep_ref[...] = value[:, 1]
        give_ref[...] = value[:, 0]


def third_gradient(parity, activated, cotangent, size, token):
    _, valid, wide = cotangent.shape
    rows, ff = activated.shape
    extent = ff // size
    owners = wide // extent // 2
    out = pl.BlockSpec((owners, extent, wide), lambda i, p: (i, 0, 0))
    return pl.pallas_call(
        third_kernel,
        grid_spec=pltpu.PrefetchScalarGridSpec(
            num_scalar_prefetch=1,
            grid=(ff // wide,),
            in_specs=[
                pl.BlockSpec((rows, wide), lambda i, p: (0, i)),
                pl.BlockSpec((1, valid, wide), lambda i, p: (0, 0, 0)),
                pl.BlockSpec(memory_space=pl.ANY),
            ],
            out_specs=[out, out],
            scratch_shapes=[pltpu.VMEM((rows, wide), BF)],
        ),
        out_shape=[jax.ShapeDtypeStruct((size // 2, extent, wide), BF)] * 2,
        cost_estimate=pl.CostEstimate(
            flops=2 * rows * wide * ff, bytes_accessed=rows * ff * 4, transcendentals=0
        ),
        name="third_gradient",
    )(parity, activated, cotangent, token)


def feed_back_kernel(
    part, place_ref, fc2_ref, fc1_ref, late_out_ref, slope_ref, cot_ref, late_ref, gain_ref,
    du_ref, flat_ref, low_ref, mine_ref, sent_ref, bias_ref, sums_ref,
    total_ref, padded_ref, out_ref, residual_ref, sem_ref,
):
    step = pl.program_id(0)
    rows, wide = total_ref.shape
    group = mine_ref.shape[1]
    per = fc2_ref.shape[1] // wide

    first = per * wide if part else 0
    copies = (
        pltpu.make_async_copy(late_out_ref.at[:, first : first + wide], out_ref, sem_ref.at[0]),
        pltpu.make_async_copy(late_ref, residual_ref, sem_ref.at[1]),
    )

    @pl.when(step == 0)
    def _():
        for copy in copies:
            copy.start()
        fill_rows(padded_ref, cot_ref[0])
        total_ref[...] = jnp.zeros_like(total_ref)

    if part:
        for d in range(fc2_ref.shape[0] // part):
            for j in range(per):
                block = fc2_ref[d * part : (d + 1) * part, j * wide : (j + 1) * wide]
                flat_ref[(d * per + j) * part : (d * per + j + 1) * part, :] = block
    else:
        flat_ref[...] = fc2_ref[...]
    du = dot(padded_ref[...], flat_ref[...], 1, 1) * slope_ref[...].astype(F32)
    bias_ref[...] = jnp.sum(du, axis=0, keepdims=True)
    du = du.astype(BF)
    du_ref[...] = du
    total_ref[...] += dot(du, fc1_ref[...], 1, 1)

    @pl.when(step == pl.num_programs(0) - 1)
    def _():
        for copy in copies:
            copy.wait()
        tile = 64

        def body(i, sums):
            at = pl.ds(pl.multiple_of(i * tile, tile), tile)
            r = residual_ref[at, :]
            centered = r - jnp.mean(r, axis=-1, keepdims=True)
            inverse = lax.rsqrt(jnp.mean(centered * centered, axis=-1, keepdims=True) + EPSILON)
            normed = centered * inverse
            dh = total_ref[at, :]
            weighted = dh * gain_ref[...]
            first = jnp.mean(weighted, axis=-1, keepdims=True)
            second = jnp.mean(weighted * normed, axis=-1, keepdims=True)
            g = padded_ref[at, :].astype(F32)
            grad = g + inverse * (weighted - first - normed * second)
            low_ref[at, :] = grad.astype(BF)
            parts = (grad, dh * normed, dh, g)
            return tuple(s + jnp.sum(p, axis=0, keepdims=True) for s, p in zip(sums, parts, strict=True))

        zero = jnp.zeros((1, wide), F32)
        sums = lax.fori_loop(0, rows // tile, body, (zero,) * 4)
        sums_ref[...] = jnp.concatenate(sums + (jnp.zeros((4, wide), F32),), axis=0)
        here = place_ref[0]
        mine = out_ref[pl.ds(pl.multiple_of(here * group, 128), group), :]
        other = out_ref[pl.ds(pl.multiple_of(group - here * group, 128), group), :]
        sent_ref[...] = dot(low_ref[...], other, 1, 1).astype(BF)
        mine_ref[...] = dot(low_ref[...], mine, 1, 1).astype(BF)


def feed_back(here, weights, slope, cotangent, residual, gain, part):
    rows, ff = slope.shape
    _, valid, wide = cotangent.shape
    group = wide // 2
    per = ff // wide
    if part % 16:
        part = 0
        fc2, fc1, out = weights
        fc2_spec = pl.BlockSpec((wide, wide), lambda i, p: (i, 0))
        fc1_spec = pl.BlockSpec((wide, wide), lambda i, p: (0, i))
    else:
        fc2 = fc1 = out = weights
        fc2_spec = pl.BlockSpec((wide // per, ff), lambda i, p: (i, 0))
        fc1_spec = pl.BlockSpec((wide, wide), lambda i, p: (0, per + 1 + i))

    def fixed(*shape):
        return pl.BlockSpec(shape, lambda i, p: tuple(0 for _ in shape))

    block = pl.BlockSpec((rows, wide), lambda i, p: (0, i))
    return pl.pallas_call(
        functools.partial(feed_back_kernel, part),
        grid_spec=pltpu.PrefetchScalarGridSpec(
            num_scalar_prefetch=1,
            grid=(per,),
            in_specs=[
                fc2_spec, fc1_spec, pl.BlockSpec(memory_space=pl.ANY), block,
                fixed(1, valid, wide), pl.BlockSpec(memory_space=pl.ANY), fixed(1, wide),
            ],
            out_specs=[
                block, pl.BlockSpec((wide, wide), lambda i, p: (i, 0)),
                fixed(rows, wide), fixed(rows, group), fixed(rows, group),
                pl.BlockSpec((1, wide), lambda i, p: (0, i)), fixed(8, wide),
            ],
            scratch_shapes=[
                pltpu.VMEM((rows, wide), F32),
                pltpu.VMEM((rows, wide), BF),
                pltpu.VMEM((wide, wide), BF),
                pltpu.VMEM((rows, wide), F32),
                pltpu.SemaphoreType.DMA((2,)),
            ],
        ),
        out_shape=[
            jax.ShapeDtypeStruct((rows, ff), BF),
            jax.ShapeDtypeStruct((ff, wide), BF),
            jax.ShapeDtypeStruct((rows, wide), BF),
            jax.ShapeDtypeStruct((rows, group), BF),
            jax.ShapeDtypeStruct((rows, group), BF),
            jax.ShapeDtypeStruct((1, ff), F32),
            jax.ShapeDtypeStruct((8, wide), F32),
        ],
        cost_estimate=pl.CostEstimate(
            flops=4 * rows * wide * ff, bytes_accessed=ff * wide * 10, transcendentals=rows
        ),
        name="feed_back",
    )(here, fc2, fc1, out, slope, cotangent, residual, gain)


def finish_kernel(spans, place_ref, mine_ref, theirs_ref, w_ref, *refs):
    here = place_ref[0]
    group = w_ref.shape[1] // 6
    mine, theirs = mine_ref[...].astype(F32), theirs_ref[...].astype(F32)
    for j in range(3):
        part = slice(j * group, (j + 1) * group)
        at = (2 * j * group) + here * group
        w_ref[:, pl.ds(pl.multiple_of(at, 128), group)] = mine[:, part]
        at = (2 * j + 1) * group - here * group
        w_ref[:, pl.ds(pl.multiple_of(at, 128), group)] = theirs[:, part]
    rows = (mine[:, 3 * group :] + theirs[:, 3 * group :]).T
    for (start, stop), ref in zip(spans, refs, strict=True):
        ref[...] = jnp.concatenate([rows[i : i + 1] for i in range(start, stop)], axis=1)


def finish(here, mine, theirs, spans):
    part, across = mine.shape
    width = 2 * (across - 128)

    def fixed(*shape):
        return pl.BlockSpec(shape, lambda i, p: (0, 0))

    sizes = [(1, (stop - start) * part) for start, stop in spans]
    return pl.pallas_call(
        functools.partial(finish_kernel, spans),
        grid_spec=pltpu.PrefetchScalarGridSpec(
            num_scalar_prefetch=1,
            grid=(1,),
            in_specs=[fixed(part, across)] * 2,
            out_specs=[fixed(part, width)] + [fixed(*shape) for shape in sizes],
        ),
        out_shape=[jax.ShapeDtypeStruct((part, width), F32)]
        + [jax.ShapeDtypeStruct(shape, F32) for shape in sizes],
        name="finish",
    )(here, mine, theirs)


def output_kernel(token_ref, z_ref, w_ref, residual_ref, rows_ref, out_ref, total_ref):
    step = pl.program_id(0)

    @pl.when(step == 0)
    def _():
        total_ref[...] = residual_ref[...] + rows_ref[-1:, :]

    total_ref[...] += dot(z_ref[...], w_ref[...])

    @pl.when(step == pl.num_programs(0) - 1)
    def _():
        out_ref[0] = total_ref[: out_ref.shape[1], :].astype(BF)


def output_end(token, activated, w, residual, bias, valid):
    rows, ff = activated.shape
    wide = w.shape[1]
    return pl.pallas_call(
        output_kernel,
        grid=(ff // wide,),
        in_specs=[
            pl.BlockSpec(memory_space=pl.ANY),
            pl.BlockSpec((rows, wide), lambda i: (0, i)),
            pl.BlockSpec((wide, wide), lambda i: (i, 0)),
            pl.BlockSpec((rows, wide), lambda i: (0, 0)),
            pl.BlockSpec((1, wide), lambda i: (0, 0)),
        ],
        out_specs=pl.BlockSpec((1, valid, wide), lambda i: (0, 0, 0)),
        out_shape=jax.ShapeDtypeStruct((1, valid, wide), BF),
        scratch_shapes=[pltpu.VMEM((rows, wide), F32)],
        cost_estimate=pl.CostEstimate(
            flops=2 * rows * wide * ff, bytes_accessed=rows * ff * 4, transcendentals=0
        ),
        name="output_end",
    )(token, activated, w, residual, bias)


def join_kernel(mine_ref, theirs_ref, out_ref, first_ref):
    wide = out_ref.shape[1]
    mine, theirs = mine_ref[...].astype(F32), theirs_ref[...].astype(F32)
    out_ref[...] = mine[:, :wide] + theirs[:, :wide]
    first_ref[...] = mine[:, wide:] + theirs[:, wide:]


def join_second(mine, theirs, wide):
    part, across = mine.shape
    return pl.pallas_call(
        join_kernel,
        out_shape=[
            jax.ShapeDtypeStruct((part, wide), F32),
            jax.ShapeDtypeStruct((part, across - wide), F32),
        ],
        name="join_second",
    )(mine, theirs)


def input_end_kernel(mine_ref, got_ref, residual_ref, normed_ref, gain_ref, inverse_ref, out_ref):
    normed = normed_ref[...]
    weighted = (mine_ref[...].astype(F32) + got_ref[...].astype(F32)) * gain_ref[...]
    first = jnp.mean(weighted, axis=-1, keepdims=True)
    second = jnp.mean(weighted * normed, axis=-1, keepdims=True)
    out_ref[:, 0, :] = residual_ref[...].astype(F32) + inverse_ref[:, 0:1] * (weighted - first - normed * second)


def input_end(mine, got, residual, normed, gain, inverse, valid):
    half, wide = mine.shape
    tile = 384
    block = pl.BlockSpec((tile, wide), lambda i: (i, 0))
    return pl.pallas_call(
        input_end_kernel,
        grid=(half // tile,),
        in_specs=[
            block, block, block, block, pl.BlockSpec((1, wide), lambda i: (0, 0)),
            pl.BlockSpec((tile, 128), lambda i: (i, 0)),
        ],
        out_specs=pl.BlockSpec((tile, 1, wide), lambda i: (i, 0, 0)),
        out_shape=jax.ShapeDtypeStruct((valid, 1, wide), F32),
        cost_estimate=pl.CostEstimate(
            flops=half * wide * 10, bytes_accessed=half * wide * 18, transcendentals=0
        ),
        name="input_end",
    )(mine, got, residual, normed, gain, inverse)


def swap(x, axis, size, bit):
    return lax.ppermute(x, axis, [(i, i ^ bit) for i in range(size)])


def bits_of(size):
    top = size // 4
    return top, [1 << b for b in range(top.bit_length() - 2, -1, -1)]


def gather_blocks(x, size):
    me = lax.axis_index("dp")
    top, bits = bits_of(size)
    held = jnp.stack([x] + [swap(x, "dp", size, j * top) for j in (1, 2, 3)])
    where = [j * top for j in range(4)]
    for bit in bits:
        held = jnp.concatenate([held, swap(held, "dp", size, bit)])
        where = where + [w ^ bit for w in where]
    place = [0] * size
    for i, w in enumerate(where):
        place[w] = i
    return held, jnp.asarray(place, jnp.int32)[me ^ jnp.arange(size)]


def halve(x, axis, bit):
    mine = lax.rem(lax.axis_index("dp") // bit, 2)
    keep = lax.dynamic_index_in_dim(x, mine, axis, keepdims=False)
    give = lax.dynamic_index_in_dim(x, 1 - mine, axis, keepdims=False)
    return keep, give.astype(BF)


def scatter_split(x, size):
    top, _ = bits_of(size)
    mine = lax.axis_index("dp") // top
    gives = [
        lax.dynamic_index_in_dim(x, mine ^ j, 0, keepdims=False).astype(BF) for j in (1, 2, 3)
    ]
    return gives, lax.dynamic_index_in_dim(x, mine, 0, keepdims=False).astype(F32)


def scatter_join(total, gives, size):
    top, _ = bits_of(size)
    for j, give in zip((1, 2, 3), gives, strict=True):
        total = total + swap(give, "dp", size, j * top).astype(F32)
    return total


def after(x, *others):
    return lax.optimization_barrier((x, *others))[0]


def gelu_cdf(values):
    return 0.5 * (1.0 + lax.erf(values * (1.0 / math.sqrt(2.0))))


def layer(
    size, frames_in, ln1_gain, ln1_bias, w_qkv, b_qv, w_o, b_o,
    ln2_gain, ln2_bias, w_fc1, b_fc1, w_fc2, b_fc2, cotangent,
):
    clips, valid, wide = frames_in.shape
    assert clips == 1
    ff = w_fc1.shape[1]
    part = w_qkv.shape[0]
    group = wide // 2
    half = -(-valid // 256) * 256
    here = lax.axis_index("seq")

    def other(x):
        return swap(x, "seq", 2, 1)

    def pick(x, axis, index):
        return lax.dynamic_index_in_dim(x, index, axis, keepdims=False)

    per = ff // wide
    me = lax.axis_index("dp")
    _, bits = bits_of(size)

    vectors = jnp.concatenate([ln1_gain, ln1_bias, b_qv, b_o, ln2_gain, ln2_bias, b_fc1, b_fc2])
    count = vectors.shape[0] // part
    columns = lax.optimization_barrier(
        jnp.pad(vectors.reshape(count, part).T, ((0, 0), (0, 128 - count)))
    )
    w_mine = [
        lax.dynamic_slice_in_dim(w_qkv, j * wide + here * group, group, axis=1) for j in range(3)
    ]
    held, place = gather_blocks(jnp.concatenate(w_mine + [columns], axis=1), size)
    if part % 16:
        held = jnp.take(held, place, axis=0, mode="clip").reshape(1, wide, 3 * group + 128)
        place = jnp.zeros((1,), jnp.int32)
    place = jnp.concatenate([place, jnp.full((1,), here, jnp.int32)])
    if part % 16:
        fc2_local = w_fc2.reshape(per, part, wide).transpose(1, 0, 2).reshape(part, ff)
        packed = jnp.concatenate([fc2_local, w_o, w_fc1], axis=1)
    else:
        packed = pack(w_fc2, w_o, w_fc1)
    later = lax.all_gather(packed, "dp", axis=0, tiled=True)
    out_full, fc1_full = later[:, ff : ff + wide], later[:, ff + wide :]
    weights = later
    if part % 16:
        fc2_full = later[:, :ff].reshape(size, part, per, wide)
        weights = (fc2_full.transpose(0, 2, 1, 3).reshape(ff, wide), fc1_full, out_full)

    prepared = prepare(frames_in, half, 0)
    inverse_one = prepared[2]
    normed_both, normed_t, _ = prepare(other(frames_in), half, 1, prepared[:2])
    qkv, w_full, w_flipped, table, scale = projection(held, place, normed_both, part)

    def vector(start, stop):
        return table[start:stop].reshape(-1, size, part).transpose(1, 0, 2).reshape(-1)

    gain_one, gain_two = table[0], table[5]
    bias_fc1, bias_fc2 = vector(7, 7 + per), table[7 + per]
    o_mine, o_sent, lse = attention_forward(qkv, half, valid)
    o_got = other(o_sent)
    flag = jnp.full((1,), here, jnp.int32)
    if part % 16:
        residual, hidden_two = attend(flag, frames_in, o_mine, o_got, out_full, 0, table)
    else:
        residual, hidden_two = attend(flag, frames_in, o_mine, o_got, later, per, table)

    pre_act = dot(hidden_two, fc1_full) + bias_fc1
    cdf = gelu_cdf(pre_act)
    density = jnp.exp(-0.5 * pre_act * pre_act) * (1.0 / math.sqrt(2.0 * math.pi))
    activated, slope = lax.optimization_barrier(
        ((pre_act * cdf).astype(BF), (cdf + pre_act * density).astype(BF))
    )
    (
        grad_pre_low, fc2_full, grad_residual_low,
        do_mine, do_sent, grad_bias_fc1, grad_sums,
    ) = feed_back(flag, weights, slope, cotangent, residual, gain_two[None], part)
    do_got = other(do_sent)
    parity = jnp.full((1,), lax.rem(me, 2), jnp.int32)
    fc2_keep, fc2_give = third_gradient(parity, activated, cotangent, size, do_sent)
    second_part = second_gradient(
        flag, fc2_give, o_mine, o_got, grad_residual_low, hidden_two, grad_pre_low
    )
    grad_second = lax.psum_scatter(second_part, "dp", scatter_dimension=0, tiled=True)

    def backward(token, start, count):
        return attention_backward(
            qkv, o_mine, o_sent, do_mine, do_got, lse, token, half, valid, start, count
        )

    x = fc2_keep.astype(F32) + swap(fc2_give, "dp", size, 1).astype(F32)
    x = x.reshape(size // 2, 2, -1, wide)
    keep, give = pick(x, 1, here).astype(BF), pick(x, 1, 1 - here).astype(BF)
    got = other(give)
    ds = [backward(give, 0, group // 128)]
    grad_other = projection_input_gradient(w_flipped, ds, ds[0], half, 1, BF)
    grad_got = other(grad_other)
    for at in range(len(bits) - 2, -1, -1):
        x = after(keep, grad_other).astype(F32) + got.astype(F32)
        keep, give = halve(x.reshape(-1, 2, *x.shape[1:]), 1, bits[at])
        keep, got = keep.astype(BF), swap(give, "dp", size, bits[at])
    fc2_keep_x, fc2_got_x = keep, got

    vectors = [(7, grad_bias_fc1)]
    if part % 16:
        grad_qkv, norm_sums, sums = projection_weight_gradient(normed_t, w_full, scale, ds)
        grad_bias_mine = jnp.stack([sums[0, :group], sums[0, 2 * group :]])
        zero = jnp.zeros_like(grad_bias_mine)
        grad_bias_qv = jnp.where(
            here == 0,
            jnp.concatenate([grad_bias_mine, zero], axis=1),
            jnp.concatenate([zero, grad_bias_mine], axis=1),
        )

        def as_columns(start, v):
            v = v.reshape(size, -1, part).transpose(0, 2, 1)
            return jnp.pad(v, ((0, 0), (0, 0), (start, 128 - start - v.shape[2])))

        columns = norm_sums.reshape(size, part, 128) + as_columns(2, grad_bias_qv)
        vectors += [(p, grad_sums[i]) for i, p in enumerate((4, 5, 6, 7 + per))]
        columns = columns + sum(as_columns(start, v) for start, v in vectors)
        x = jnp.concatenate([grad_qkv.reshape(size, part, -1), columns.astype(BF)], axis=2)
        keep, give = halve(x.reshape(size // 2, 2, *x.shape[1:]), 1, 1)
    else:
        sides = jnp.concatenate([parity, jnp.full((1,), here, jnp.int32)])
        keep, give = spread_weight_gradient(
            sides, give, normed_t, w_full, scale, ds, grad_bias_fc1, grad_sums, part
        )
    got = swap(give, "dp", size, 1)
    for at in range(len(bits) - 2, -1, -1):
        x = keep.astype(F32) + got.astype(F32)
        keep, give = halve(x.reshape(-1, 2, *x.shape[1:]), 1, bits[at])
        got = swap(give, "dp", size, bits[at])
    fc2_keep, fc2_got = after((fc2_keep_x, fc2_got_x), give)
    fc2_gives, fc2_stay = scatter_split(fc2_keep.astype(F32) + fc2_got.astype(F32), size)
    grad_mine = projection_input_gradient(w_flipped, ds, fc2_gives[2], half, 0, BF)
    frames_out = output_end(
        fc2_gives[2], activated, fc2_full, residual, bias_fc2[None], valid
    )
    fc2_part = scatter_join(fc2_stay, fc2_gives, size).astype(BF)
    gives, stay = scatter_split(keep.astype(F32) + got.astype(F32), size)
    grad_input = input_end(
        grad_mine, grad_got, grad_residual_low, normed_both, gain_one[None], inverse_one, valid
    ).transpose(1, 0, 2)
    mine = scatter_join(stay, gives, size).astype(BF)
    theirs = other(mine)
    spans = ((0, 1), (1, 2), (2, 4), (4, 5), (5, 6), (6, 7), (7, 7 + per), (7 + per, 8 + per))
    grad_w_qkv, *small = finish(flag, mine, theirs, spans)
    small = [v[0] for v in small]
    fc2_got = other(fc2_part)
    fc2_sum = jnp.where(
        here == 0,
        jnp.concatenate([fc2_part, fc2_got], axis=0),
        jnp.concatenate([fc2_got, fc2_part], axis=0),
    ).astype(F32)
    out_sum, first_sum = join_second(grad_second, other(grad_second), wide)
    return (
        frames_out, grad_input, small[0], small[1], grad_w_qkv, small[2], out_sum, small[3],
        small[4], small[5], first_sum, small[6], fc2_sum, small[7],
    )


def solution(mesh):
    frames, rows, vector = P("dp", "seq", None), P("dp", None), P("dp")
    in_specs = (
        frames, vector, vector, rows, vector, rows, vector,
        vector, vector, rows, vector, rows, vector, frames,
    )
    out_specs = (
        frames, frames, vector, vector, rows, vector, rows, vector,
        vector, vector, rows, vector, rows, vector,
    )
    return jax.shard_map(
        functools.partial(layer, mesh.shape["dp"]),
        mesh=mesh, in_specs=in_specs, out_specs=out_specs, check_vma=False,
    )
```

```python
import functools
import math

import jax
import jax.numpy as jnp
from jax import lax
from jax.experimental import pallas as pl
from jax.experimental.pallas import tpu as pltpu
from jax.sharding import PartitionSpec as P


EPSILON = 1e-05
BF = jnp.bfloat16
F32 = jnp.float32
MASKED = -1e30


def dot(a, b, ca=1, cb=0):
    return lax.dot_general(a, b, (((ca,), (cb,)), ((), ())), preferred_element_type=F32)


def split3(x):
    high = x.astype(BF).astype(F32)
    rest = x - high
    mid = rest.astype(BF).astype(F32)
    return high, mid, (rest - mid).astype(BF).astype(F32)


def forward_kernel(half, valid, q_ref, k_ref, v_ref, mine_ref, sent_ref, lse_ref, kx_ref, vt_ref):
    rows = k_ref.shape[0]
    wide = q_ref.shape[0]

    kx_ref[:, :128] = k_ref[...]
    row = lax.broadcasted_iota(jnp.int32, (rows, 128), 0)
    lane = lax.broadcasted_iota(jnp.int32, (rows, 128), 1)
    padded = (lax.rem(row, half) >= valid) & (lane == 0)
    kx_ref[:, 128:] = jnp.where(padded, MASKED, 0.0).astype(BF)
    vt = v_ref[...].T
    vt_ref[0:64, :] = vt[0:64, :]
    vt_ref[64:80, :] = jnp.ones((16, rows), BF)
    vt_ref[80:144, :] = vt[64:128, :]
    vt_ref[144:160, :] = jnp.ones((16, rows), BF)

    lane = lax.broadcasted_iota(jnp.int32, (wide, 128), 1)
    q = q_ref[...] * jnp.asarray(0.125, BF)
    one = jnp.where(lane == 0, 1.0, 0.0).astype(BF)
    outs, sums = [], []
    for h in range(2):
        mine = (lane < 64) if h == 0 else (lane >= 64)
        qx = jnp.concatenate([jnp.where(mine, q, jnp.zeros_like(q)), one], axis=1)
        s = dot(kx_ref[...], qx, 1, 1)
        peak = jnp.max(s, axis=0, keepdims=True)
        p = jnp.exp(s - peak).astype(BF)
        o = dot(vt_ref[80 * h : 80 * h + 80, :], p)
        total = o[64:65, :]
        outs.append(o[0:64, :] / total)
        sums.append(peak + jnp.log(total))
    o = jnp.concatenate(outs, axis=0).T.astype(BF)
    mine_ref[...] = o[:half]
    sent_ref[...] = o[half:]
    lse_ref[...] = jnp.concatenate(sums + [jnp.zeros((6, wide), F32)], axis=0)[None]


def attention_forward(qkv, half, valid):
    rows, width = qkv.shape
    pairs = width // 3 // 128
    block = pl.BlockSpec((half, 128), lambda p: (0, p))
    return pl.pallas_call(
        functools.partial(forward_kernel, half, valid),
        grid=(pairs,),
        in_specs=[
            pl.BlockSpec((rows, 128), lambda p: (0, p)),
            pl.BlockSpec((rows, 128), lambda p: (0, pairs + p)),
            pl.BlockSpec((rows, 128), lambda p: (0, 2 * pairs + p)),
        ],
        out_specs=[block, block, pl.BlockSpec((1, 8, rows), lambda p: (p, 0, 0))],
        out_shape=[
            jax.ShapeDtypeStruct((half, pairs * 128), BF),
            jax.ShapeDtypeStruct((half, pairs * 128), BF),
            jax.ShapeDtypeStruct((pairs, 8, rows), F32),
        ],
        scratch_shapes=[pltpu.VMEM((rows, 256), BF), pltpu.VMEM((160, rows), BF)],
        cost_estimate=pl.CostEstimate(
            flops=pairs * 2 * 4 * rows * rows * 256,
            bytes_accessed=rows * width * 2 + rows * width,
            transcendentals=pairs * 2 * rows * rows,
        ),
        name="attention_forward",
    )(qkv, qkv, qkv)


def backward_kernel(
    half, valid, q_ref, k_ref, v_ref, o_mine_ref, o_sent_ref, mine_ref, got_ref, lse_ref, token_ref,
    d_ref, kt_ref, vt_ref, dkt_ref, dvt_ref,
):
    rows = k_ref.shape[0]
    step = pl.program_id(1)

    @pl.when(step == 0)
    def _():
        kt_ref[0:128, :] = k_ref[...].T
        vt_ref[0:128, :] = v_ref[...].T
        row = lax.broadcasted_iota(jnp.int32, (128, rows), 0)
        key = lax.broadcasted_iota(jnp.int32, (128, rows), 1)
        bias = jnp.where(lax.rem(key, half) >= valid, MASKED, 0.0)
        ones = jnp.where((row >= 1) & (row < 4), 1.0, 0.0)
        kt_ref[128:256, :] = jnp.where(row == 0, bias, ones).astype(BF)
        vt_ref[128:256, :] = ones.astype(BF)
        dkt_ref[...] = jnp.zeros_like(dkt_ref)
        dvt_ref[...] = jnp.zeros_like(dvt_ref)

    tile = q_ref.shape[0]
    first = step < half // tile
    lane = lax.broadcasted_iota(jnp.int32, (tile, 128), 1)
    q = q_ref[...] * jnp.asarray(0.125, BF)
    do = jnp.where(first, mine_ref[...], got_ref[...])
    o = jnp.where(first, o_mine_ref[...], o_sent_ref[...])
    product = do.astype(F32) * o.astype(F32)
    lse = lse_ref[0].T
    qt, dot_t = q.T, do.T

    def extra(x, first):
        a, b, c = split3(-x)
        tail = jnp.where(lane == 2, b, jnp.where(lane == 3, c, 0.0))
        return jnp.where(lane == 0, first, jnp.where(lane == 1, a, tail)).astype(BF)

    dq = []
    for h in range(2):
        mine = (lane < 64) if h == 0 else (lane >= 64)
        delta = jnp.sum(jnp.where(mine, product, 0.0), axis=1, keepdims=True)
        qx = jnp.concatenate(
            [jnp.where(mine, q, jnp.zeros_like(q)), extra(lse[:, h : h + 1], 1.0)], axis=1
        )
        dx = jnp.concatenate([jnp.where(mine, do, jnp.zeros_like(do)), extra(delta, 0.0)], axis=1)
        p = jnp.exp(dot(qx, kt_ref[...]))
        low = p.astype(BF)
        ds = (p * dot(dx, vt_ref[...])).astype(BF)
        dq.append(dot(ds, k_ref[...]))
        part = slice(64 * h, 64 * h + 64)
        dkt_ref[part, :] += dot(qt[part, :], ds)
        dvt_ref[part, :] += dot(dot_t[part, :], low)
    dq = (jnp.where(lane < 64, dq[0], dq[1]) * 0.125).astype(BF)
    d_ref[0, pl.ds(pl.multiple_of(step * tile, 128), tile), :] = dq

    @pl.when(step == pl.num_programs(1) - 1)
    def _():
        d_ref[1] = dkt_ref[...].T.astype(BF)
        d_ref[2] = dvt_ref[...].T.astype(BF)


def attention_backward(qkv, o_mine, o_sent, do_mine, do_got, lse, token, half, valid, start, count):
    rows, width = qkv.shape
    pairs = width // 3 // 128

    def whole(part):
        return pl.BlockSpec((rows, 128), lambda p, i: (0, part * pairs + start + p))

    tile = 384
    per_half = half // tile
    block = pl.BlockSpec((tile, 128), lambda p, i: (i, start + p))
    fixed = pl.BlockSpec((tile, 128), lambda p, i: (lax.rem(i, per_half), start + p))
    return pl.pallas_call(
        functools.partial(backward_kernel, half, valid),
        grid=(count, 2 * per_half),
        in_specs=[
            block, whole(1), whole(2), fixed, fixed, fixed, fixed,
            pl.BlockSpec((1, 8, tile), lambda p, i: (start + p, 0, i)),
            pl.BlockSpec(memory_space=pl.ANY),
        ],
        out_specs=pl.BlockSpec((3, rows, 128), lambda p, i: (0, 0, p)),
        out_shape=jax.ShapeDtypeStruct((3, rows, count * 128), BF),
        scratch_shapes=[
            pltpu.VMEM((256, rows), BF),
            pltpu.VMEM((256, rows), BF),
            pltpu.VMEM((128, rows), F32),
            pltpu.VMEM((128, rows), F32),
        ],
        cost_estimate=pl.CostEstimate(
            flops=count * 2 * 8 * rows * rows * 256,
            bytes_accessed=count * rows * 128 * 16,
            transcendentals=count * 2 * rows * rows,
        ),
        name="attention_backward",
    )(qkv, qkv, qkv, o_mine, o_sent, do_mine, do_got, lse, token)


def rows_below(x, start, valid):
    row = start + lax.broadcasted_iota(jnp.int32, x.shape, 0)
    return jnp.where(row < valid, x, jnp.zeros_like(x))


def prepare_kernel(valid, x_ref, *refs):
    normed_ref, flipped_ref, inverse_ref = refs[-3:]
    tile, wide = normed_ref.shape
    x = rows_below(x_ref[0].astype(F32), pl.program_id(0) * tile, valid)
    centered = x - jnp.mean(x, axis=-1, keepdims=True)
    inverse = lax.rsqrt(jnp.mean(centered * centered, axis=-1, keepdims=True) + EPSILON)
    normed = centered * inverse
    normed_ref[...] = normed
    inverse_ref[...] = jnp.broadcast_to(inverse, inverse_ref.shape)
    flipped_ref[:wide, :] = normed.T.astype(BF)
    flipped_ref[wide:, :] = jnp.ones((16, tile), BF)


def prepare(frames, half, block, filled=()):
    _, valid, wide = frames.shape
    tile = 384
    first = block * (half // tile)
    return pl.pallas_call(
        functools.partial(prepare_kernel, valid),
        grid=(half // tile,),
        in_specs=[pl.BlockSpec((1, tile, wide), lambda i: (0, i, 0))]
        + [pl.BlockSpec(memory_space=pl.ANY)] * len(filled),
        out_specs=[
            pl.BlockSpec((tile, wide), lambda i: (first + i, 0)),
            pl.BlockSpec((wide + 16, tile), lambda i: (0, first + i)),
            pl.BlockSpec((tile, 128), lambda i: (i, 0)),
        ],
        out_shape=[
            jax.ShapeDtypeStruct((2 * half, wide), F32),
            jax.ShapeDtypeStruct((wide + 16, 2 * half), BF),
            jax.ShapeDtypeStruct((half, 128), F32),
        ],
        input_output_aliases={1: 0, 2: 1} if filled else {},
        cost_estimate=pl.CostEstimate(
            flops=half * wide * 16, bytes_accessed=half * wide * 8, transcendentals=half
        ),
        name="prepare",
    )(frames, *filled)


def attend_kernel(valid, place_ref, x_ref, mine_ref, got_ref, w_ref, rows_ref, sum_ref, h_ref):
    tile = sum_ref.shape[0]
    group = mine_ref.shape[1]
    here = place_ref[0]
    first = w_ref[pl.ds(pl.multiple_of(here * group, 128), group), :]
    other = w_ref[pl.ds(pl.multiple_of(group - here * group, 128), group), :]
    total = dot(mine_ref[...], first) + dot(got_ref[...], other)
    x = rows_below(x_ref[0].astype(F32), pl.program_id(0) * tile, valid)
    total = x + total + rows_ref[4:5, :]
    sum_ref[...] = total
    centered = total - jnp.mean(total, axis=-1, keepdims=True)
    inverse = lax.rsqrt(jnp.mean(centered * centered, axis=-1, keepdims=True) + EPSILON)
    h_ref[...] = (centered * inverse * rows_ref[5:6, :] + rows_ref[6:7, :]).astype(BF)


def attend(here, frames, mine, got, w, column, table):
    _, valid, wide = frames.shape
    half, group = mine.shape
    tile = 256
    block = pl.BlockSpec((tile, group), lambda i, p: (i, 0))
    out = pl.BlockSpec((tile, wide), lambda i, p: (i, 0))
    return pl.pallas_call(
        functools.partial(attend_kernel, valid),
        grid_spec=pltpu.PrefetchScalarGridSpec(
            num_scalar_prefetch=1,
            grid=(half // tile,),
            in_specs=[
                pl.BlockSpec((1, tile, wide), lambda i, p: (0, i, 0)), block, block,
                pl.BlockSpec((wide, wide), lambda i, p: (0, column)),
                pl.BlockSpec((16, wide), lambda i, p: (0, 0)),
            ],
            out_specs=[out, out],
        ),
        out_shape=[
            jax.ShapeDtypeStruct((half, wide), F32),
            jax.ShapeDtypeStruct((half, wide), BF),
        ],
        cost_estimate=pl.CostEstimate(
            flops=4 * half * wide * group, bytes_accessed=half * wide * 10, transcendentals=half
        ),
        name="attend",
    )(here, frames, mine, got, w, table)


def projection_kernel(
    part, group, place_ref, held_ref, x_ref, qkv_ref, w_ref, wt_ref, rows_ref, scale_ref,
    gain_ref, bias_ref, columns_ref,
):
    wide, width = w_ref.shape

    @pl.when(pl.program_id(0) == 0)
    def _():
        blocks, extent, _ = held_ref.shape
        for d in range(blocks):
            block = held_ref[place_ref[2 + d]]
            w_ref[d * extent : (d + 1) * extent, :] = block[:, :width]
            columns_ref[d * extent : (d + 1) * extent, :] = block[:, width:].astype(F32)
        wt_ref[...] = w_ref[...].T
        table = columns_ref[...].T[:16, :]
        rows_ref[...] = table
        scale_ref[:, :128] = jnp.broadcast_to(columns_ref[:, 0:1], (wide, 128))
        scale_ref[:, 128:] = jnp.broadcast_to(columns_ref[:, 1:2], (wide, 128))
        gain_ref[...] = table[:8]
        here = place_ref[0]
        few = group // 2
        row = lax.broadcasted_iota(jnp.int32, (few, group), 0)
        entry = lax.broadcasted_iota(jnp.int32, (few, group), 1)
        base = row + part * (row // part)
        for v in range(2):
            at = pl.multiple_of(v * (wide // 2) + here * few, 64)
            low = columns_ref[pl.ds(at, few), :].T[:16].astype(BF)
            total = jnp.zeros((16, group), F32)
            for j in range(2):
                chosen = entry == base + part * j
                picked = dot(low, jnp.where(chosen, 1.0, 0.0).astype(BF))
                total = total + picked[2 + j : 3 + j, :]
            bias_ref[:, 2 * v * group : (2 * v + 1) * group] = total[:8]
        bias_ref[:, group : 2 * group] = jnp.zeros((8, group), F32)

    h = (x_ref[...] * gain_ref[0:1, :] + gain_ref[1:2, :]).astype(BF)
    qkv_ref[...] = (dot(h, w_ref[...]) + bias_ref[0:1, :]).astype(BF)


def projection(held, place, normed, part):
    blocks, extent, across = held.shape
    width = across - 128
    rows, wide = normed.shape
    tile = 384

    def fixed(*shape):
        return pl.BlockSpec(shape, lambda i, p: tuple(0 for _ in shape))

    return pl.pallas_call(
        functools.partial(projection_kernel, part, width // 3),
        grid_spec=pltpu.PrefetchScalarGridSpec(
            num_scalar_prefetch=1,
            grid=(rows // tile,),
            in_specs=[fixed(blocks, extent, across), pl.BlockSpec((tile, wide), lambda i, p: (i, 0))],
            out_specs=[
                pl.BlockSpec((tile, width), lambda i, p: (i, 0)),
                fixed(wide, width), fixed(width, wide), fixed(16, wide), fixed(wide, 256),
            ],
            scratch_shapes=[
                pltpu.VMEM((8, wide), F32),
                pltpu.VMEM((8, width), F32),
                pltpu.VMEM((wide, 128), F32),
            ],
        ),
        out_shape=[
            jax.ShapeDtypeStruct((rows, width), BF),
            jax.ShapeDtypeStruct((wide, width), BF),
            jax.ShapeDtypeStruct((width, wide), BF),
            jax.ShapeDtypeStruct((16, wide), F32),
            jax.ShapeDtypeStruct((wide, 256), F32),
        ],
        cost_estimate=pl.CostEstimate(
            flops=2 * rows * wide * width, bytes_accessed=rows * wide * 8, transcendentals=0
        ),
        name="projection",
    )(place, held, normed)


def weight_kernel(pieces, xt_ref, w_ref, scale_ref, *refs):
    d_refs, (g_ref, c_ref, s_ref) = refs[:pieces], refs[pieces:]
    d = jnp.concatenate([r[0] for r in d_refs], axis=1)
    m = dot(xt_ref[...], d)
    s = m[w_ref.shape[0] :][:8]
    m = m[: w_ref.shape[0]]
    s_ref[...] = s
    gain, shift = scale_ref[:, 0:1], scale_ref[:, 128:129]
    total = s[0:1, :]
    g_ref[...] = (gain * m + shift * total).astype(BF)
    w = w_ref[...].astype(F32)
    lane = lax.broadcasted_iota(jnp.int32, c_ref.shape, 1)
    first = jnp.sum(w * m, axis=1, keepdims=True)
    second = jnp.sum(w * total, axis=1, keepdims=True)
    now = jnp.where(lane == 0, first, jnp.where(lane == 1, second, 0.0))
    before = jnp.where(pl.program_id(0) == 0, jnp.zeros_like(now), c_ref[...])
    c_ref[...] = before + now


def projection_weight_gradient(xt, w, scale, ds):
    tall, rows = xt.shape
    wide = w.shape[0]
    group = sum(d.shape[2] for d in ds)
    return pl.pallas_call(
        functools.partial(weight_kernel, len(ds)),
        grid=(3,),
        in_specs=[
            pl.BlockSpec((tall, rows), lambda j: (0, 0)),
            pl.BlockSpec((wide, group), lambda j: (0, j)),
            pl.BlockSpec((wide, 256), lambda j: (0, 0)),
        ]
        + [pl.BlockSpec((1, *d.shape[1:]), lambda j: (j, 0, 0)) for d in ds],
        out_specs=[
            pl.BlockSpec((wide, group), lambda j: (0, j)),
            pl.BlockSpec((wide, 128), lambda j: (0, 0)),
            pl.BlockSpec((8, group), lambda j: (0, j)),
        ],
        out_shape=[
            jax.ShapeDtypeStruct((wide, 3 * group), BF),
            jax.ShapeDtypeStruct((wide, 128), F32),
            jax.ShapeDtypeStruct((8, 3 * group), F32),
        ],
        cost_estimate=pl.CostEstimate(
            flops=2 * rows * wide * 3 * group, bytes_accessed=rows * wide * 4, transcendentals=0
        ),
        name="projection_weight_gradient",
    )(xt, w, scale, *ds)


def spread_kernel(
    part, pieces, per, place_ref, token_ref, xt_ref, w_ref, scale_ref, *refs
):
    d_refs, refs = refs[:pieces], refs[pieces:]
    b_ref, v_ref, keep_ref, give_ref, c_ref, s_ref, first_ref, second_ref = refs
    step = pl.program_id(0)
    wide, group = w_ref.shape
    d = jnp.concatenate([r[0] for r in d_refs], axis=1)
    m = dot(xt_ref[...], d)
    s = m[wide : wide + 8]
    s_ref[step] = s

    @pl.when(step == 0)
    def _():
        first_ref[...] = jnp.zeros_like(first_ref)
        second_ref[...] = jnp.zeros_like(second_ref)

    gain, shift = scale_ref[:, :128], scale_ref[:, 128:]
    one, two, gs = first_ref[...], second_ref[...], []
    for i in range(group // 128):
        columns = slice(128 * i, 128 * (i + 1))
        piece, w, total = m[:wide, columns], w_ref[:, columns].astype(F32), s[0:1, columns]
        one, two = one + w * piece, two + w * total
        gs.append((gain * piece + shift * total).astype(BF))
    first_ref[...], second_ref[...] = one, two
    at = pl.ds(pl.multiple_of(step * group, 128), group)
    spread_store(part, place_ref, keep_ref, give_ref, jnp.concatenate(gs, axis=1), at)

    @pl.when(step == 2)
    def _():
        lane = lax.broadcasted_iota(jnp.int32, c_ref.shape, 1)
        second = jnp.sum(second_ref[...], axis=1, keepdims=True)
        first = jnp.sum(first_ref[...], axis=1, keepdims=True)
        columns = jnp.where(lane == 0, first, jnp.where(lane == 1, second, 0.0))
        small = v_ref[...].T
        for i, name in enumerate((4, 5, 6, 7 + per)):
            columns = jnp.where(lane == name, small[:, i : i + 1], columns)
        v = jnp.broadcast_to(b_ref[...], (8, b_ref.shape[1])).T[:, 0:1]
        for j in range(per):
            column = jnp.concatenate(
                [v[(d * per + j) * part :][:part] for d in range(wide // part)], axis=0
            )
            columns = jnp.where(lane == 7 + j, column, columns)
        c_ref[...] = columns
        half = group // 2
        low = lane[:half]
        for side in (0, 2):
            v = s_ref[side].T[:, 0:1]
            at = pl.ds(pl.multiple_of(place_ref[0] * half + side * wide // 4, 64), half)
            block = c_ref[at, :]
            for j in range(2):
                column = jnp.concatenate(
                    [v[(2 * d + j) * part :][:part] for d in range(half // part)], axis=0
                )
                block = jnp.where(low == 2 + j, column, block)
            c_ref[at, :] = block
        g = c_ref[...].astype(BF)
        spread_store(part, place_ref, keep_ref, give_ref, g, pl.ds(3 * group, 128))


def spread_store(part, place_ref, keep_ref, give_ref, value, columns):
    value = value.reshape(keep_ref.shape[0], 2, part, value.shape[1])
    even, odd = value[:, 0], value[:, 1]
    low = place_ref[1] == 0
    keep_ref[:, :, columns] = jnp.where(low, even, odd)
    give_ref[:, :, columns] = jnp.where(low, odd, even)


def spread_weight_gradient(place, token, xt, w, scale, ds, bias, sums, part):
    _, rows = xt.shape
    wide = w.shape[0]
    group = sum(d.shape[2] for d in ds)
    size = wide // part
    out = pl.BlockSpec((size // 2, part, 3 * group + 128), lambda j, p: (0, 0, 0))

    def fixed(x):
        return pl.BlockSpec(x.shape, lambda j, p: (0, 0))

    return pl.pallas_call(
        functools.partial(spread_kernel, part, len(ds), bias.shape[1] // wide),
        grid_spec=pltpu.PrefetchScalarGridSpec(
            num_scalar_prefetch=1,
            grid=(3,),
            in_specs=[
                pl.BlockSpec(memory_space=pl.ANY),
                fixed(xt),
                pl.BlockSpec((wide, group), lambda j, p: (0, j)),
                fixed(scale),
            ]
            + [pl.BlockSpec((1, *d.shape[1:]), lambda j, p: (j, 0, 0)) for d in ds]
            + [fixed(bias), fixed(sums)],
            out_specs=[out, out],
            scratch_shapes=[
                pltpu.VMEM((wide, 128), F32),
                pltpu.VMEM((3, 8, group), F32),
                pltpu.VMEM((wide, 128), F32),
                pltpu.VMEM((wide, 128), F32),
            ],
        ),
        out_shape=[jax.ShapeDtypeStruct((size // 2, part, 3 * group + 128), BF)] * 2,
        cost_estimate=pl.CostEstimate(
            flops=2 * rows * wide * 3 * group, bytes_accessed=rows * wide * 4, transcendentals=0
        ),
        name="spread_weight_gradient",
    )(place, token, xt, w, scale, *ds, bias, sums)


def input_kernel(pieces, token_ref, wt_ref, *refs):
    d_refs, out_ref = refs[:pieces], refs[pieces]
    d = jnp.concatenate([r[j] for j in range(3) for r in d_refs], axis=1)
    out_ref[...] = dot(d, wt_ref[...]).astype(out_ref.dtype)


def projection_input_gradient(wt, ds, token, half, block, kind):
    wide = wt.shape[1]
    tile = 384
    start = block * (half // tile)
    return pl.pallas_call(
        functools.partial(input_kernel, len(ds)),
        grid=(half // tile,),
        in_specs=[pl.BlockSpec(memory_space=pl.ANY), pl.BlockSpec(wt.shape, lambda i: (0, 0))]
        + [pl.BlockSpec((3, tile, d.shape[2]), lambda i: (0, start + i, 0)) for d in ds],
        out_specs=pl.BlockSpec((tile, wide), lambda i: (i, 0)),
        out_shape=jax.ShapeDtypeStruct((half, wide), kind),
        cost_estimate=pl.CostEstimate(
            flops=2 * half * wt.size, bytes_accessed=half * wt.shape[0] * 4, transcendentals=0
        ),
        name="projection_input_gradient",
    )(token, wt, *ds)


def second_kernel(place_ref, token_ref, mine_ref, got_ref, drb_ref, h_ref, du_ref, out_ref, ht_ref):
    group = mine_ref.shape[1]
    step = pl.program_id(0)

    @pl.when(step == 0)
    def _():
        ht_ref[...] = h_ref[...].T
        here = place_ref[0]
        first = pl.multiple_of(here * group, 128)
        other = pl.multiple_of(group - here * group, 128)
        out_ref[pl.ds(first, group), :] = dot(mine_ref[...], drb_ref[...], 0, 0).astype(BF)
        out_ref[pl.ds(other, group), :] = dot(got_ref[...], drb_ref[...], 0, 0).astype(BF)

    @pl.when(step > 0)
    def _():
        out_ref[...] = dot(ht_ref[...], du_ref[...]).astype(BF)


def second_gradient(here, token, o_mine, o_got, drb, hidden, du):
    rows, wide = hidden.shape
    ff = du.shape[1]

    def fixed(x):
        return pl.BlockSpec(x.shape, lambda i, p: (0, 0))

    return pl.pallas_call(
        second_kernel,
        grid_spec=pltpu.PrefetchScalarGridSpec(
            num_scalar_prefetch=1,
            grid=(1 + ff // wide,),
            in_specs=[
                pl.BlockSpec(memory_space=pl.ANY), fixed(o_mine), fixed(o_got), fixed(drb), fixed(hidden),
                pl.BlockSpec((rows, wide), lambda i, p: (0, jnp.maximum(i - 1, 0))),
            ],
            out_specs=pl.BlockSpec((wide, wide), lambda i, p: (0, i)),
            scratch_shapes=[pltpu.VMEM((wide, rows), BF)],
        ),
        out_shape=jax.ShapeDtypeStruct((wide, wide + ff), BF),
        cost_estimate=pl.CostEstimate(
            flops=2 * rows * wide * (wide + ff), bytes_accessed=rows * ff * 4, transcendentals=0
        ),
        name="second_gradient",
    )(here, token, o_mine, o_got, drb, hidden, du)


def pack_kernel(fc2_ref, out_ref, fc1_ref, packed_ref):
    part, wide = out_ref.shape
    per = fc2_ref.shape[0] // part
    for j in range(per):
        packed_ref[:, j * wide : (j + 1) * wide] = fc2_ref[j * part : (j + 1) * part, :]
    packed_ref[:, per * wide : (per + 1) * wide] = out_ref[...]
    packed_ref[:, (per + 1) * wide :] = fc1_ref[...]


def pack(w_fc2, w_o, w_fc1):
    part, wide = w_o.shape
    across = wide + 2 * w_fc1.shape[1]
    return pl.pallas_call(
        pack_kernel, out_shape=jax.ShapeDtypeStruct((part, across), BF), name="pack"
    )(w_fc2, w_o, w_fc1)


def fill_rows(ref, x):
    valid = x.shape[0]
    start = valid // 16 * 16
    ref[start:, :] = jnp.zeros((ref.shape[0] - start, ref.shape[1]), ref.dtype)
    ref[:valid, :] = x


def third_kernel(place_ref, z_ref, cot_ref, token_ref, keep_ref, give_ref, padded_ref):
    @pl.when(pl.program_id(0) == 0)
    def _():
        fill_rows(padded_ref, cot_ref[0])

    value = dot(z_ref[...], padded_ref[...], 0, 0).astype(BF)
    owners, extent, wide = keep_ref.shape
    value = value.reshape(owners, 2, extent, wide)

    @pl.when(place_ref[1] == 0)
    def _():
        keep_ref[...] = value[:, 0]
        give_ref[...] = value[:, 1]

    @pl.when(place_ref[1] == 1)
    def _():
        keep_ref[...] = value[:, 1]
        give_ref[...] = value[:, 0]


def third_gradient(flag, activated, cotangent, size, token):
    _, valid, wide = cotangent.shape
    rows, ff = activated.shape
    extent = ff // size
    owners = wide // extent // 2
    out = pl.BlockSpec((owners, extent, wide), lambda i, p: (i, 0, 0))
    return pl.pallas_call(
        third_kernel,
        grid_spec=pltpu.PrefetchScalarGridSpec(
            num_scalar_prefetch=1,
            grid=(ff // wide,),
            in_specs=[
                pl.BlockSpec((rows, wide), lambda i, p: (0, i)),
                pl.BlockSpec((1, valid, wide), lambda i, p: (0, 0, 0)),
                pl.BlockSpec(memory_space=pl.ANY),
            ],
            out_specs=[out, out],
            scratch_shapes=[pltpu.VMEM((rows, wide), BF)],
        ),
        out_shape=[jax.ShapeDtypeStruct((size // 2, extent, wide), BF)] * 2,
        cost_estimate=pl.CostEstimate(
            flops=2 * rows * wide * ff, bytes_accessed=rows * ff * 4, transcendentals=0
        ),
        name="third_gradient",
    )(flag, activated, cotangent, token)


def feed_back_kernel(
    part, place_ref, fc2_ref, fc1_ref, late_out_ref, slope_ref, cot_ref, late_ref, gain_ref,
    du_ref, flat_ref, low_ref, mine_ref, sent_ref, bias_ref, sums_ref,
    total_ref, padded_ref, out_ref, residual_ref, sem_ref,
):
    step = pl.program_id(0)
    rows, wide = total_ref.shape
    group = mine_ref.shape[1]
    per = fc2_ref.shape[1] // wide

    first = per * wide if part else 0
    copies = (
        pltpu.make_async_copy(late_out_ref.at[:, first : first + wide], out_ref, sem_ref.at[0]),
        pltpu.make_async_copy(late_ref, residual_ref, sem_ref.at[1]),
    )

    @pl.when(step == 0)
    def _():
        for copy in copies:
            copy.start()
        fill_rows(padded_ref, cot_ref[0])
        total_ref[...] = jnp.zeros_like(total_ref)

    if part:
        for d in range(fc2_ref.shape[0] // part):
            for j in range(per):
                block = fc2_ref[d * part : (d + 1) * part, j * wide : (j + 1) * wide]
                flat_ref[(d * per + j) * part : (d * per + j + 1) * part, :] = block
    else:
        flat_ref[...] = fc2_ref[...]
    du = dot(padded_ref[...], flat_ref[...], 1, 1) * slope_ref[...].astype(F32)
    bias_ref[...] = jnp.sum(du, axis=0, keepdims=True)
    du = du.astype(BF)
    du_ref[...] = du
    total_ref[...] += dot(du, fc1_ref[...], 1, 1)

    @pl.when(step == pl.num_programs(0) - 1)
    def _():
        for copy in copies:
            copy.wait()
        tile = 64

        def body(i, sums):
            at = pl.ds(pl.multiple_of(i * tile, tile), tile)
            r = residual_ref[at, :]
            centered = r - jnp.mean(r, axis=-1, keepdims=True)
            inverse = lax.rsqrt(jnp.mean(centered * centered, axis=-1, keepdims=True) + EPSILON)
            normed = centered * inverse
            dh = total_ref[at, :]
            weighted = dh * gain_ref[...]
            first = jnp.mean(weighted, axis=-1, keepdims=True)
            second = jnp.mean(weighted * normed, axis=-1, keepdims=True)
            g = padded_ref[at, :].astype(F32)
            grad = g + inverse * (weighted - first - normed * second)
            low_ref[at, :] = grad.astype(BF)
            parts = (grad, dh * normed, dh, g)
            return tuple(s + jnp.sum(p, axis=0, keepdims=True) for s, p in zip(sums, parts, strict=True))

        zero = jnp.zeros((1, wide), F32)
        sums = lax.fori_loop(0, rows // tile, body, (zero,) * 4)
        sums_ref[...] = jnp.concatenate(sums + (jnp.zeros((4, wide), F32),), axis=0)
        here = place_ref[0]
        mine = out_ref[pl.ds(pl.multiple_of(here * group, 128), group), :]
        other = out_ref[pl.ds(pl.multiple_of(group - here * group, 128), group), :]
        sent_ref[...] = dot(low_ref[...], other, 1, 1).astype(BF)
        mine_ref[...] = dot(low_ref[...], mine, 1, 1).astype(BF)


def feed_back(here, weights, slope, cotangent, residual, gain, part):
    rows, ff = slope.shape
    _, valid, wide = cotangent.shape
    group = wide // 2
    per = ff // wide
    if part % 16:
        part = 0
        fc2, fc1, out = weights
        fc2_spec = pl.BlockSpec((wide, wide), lambda i, p: (i, 0))
        fc1_spec = pl.BlockSpec((wide, wide), lambda i, p: (0, i))
    else:
        fc2 = fc1 = out = weights
        fc2_spec = pl.BlockSpec((wide // per, ff), lambda i, p: (i, 0))
        fc1_spec = pl.BlockSpec((wide, wide), lambda i, p: (0, per + 1 + i))

    def fixed(*shape):
        return pl.BlockSpec(shape, lambda i, p: tuple(0 for _ in shape))

    block = pl.BlockSpec((rows, wide), lambda i, p: (0, i))
    return pl.pallas_call(
        functools.partial(feed_back_kernel, part),
        grid_spec=pltpu.PrefetchScalarGridSpec(
            num_scalar_prefetch=1,
            grid=(per,),
            in_specs=[
                fc2_spec, fc1_spec, pl.BlockSpec(memory_space=pl.ANY), block,
                fixed(1, valid, wide), pl.BlockSpec(memory_space=pl.ANY), fixed(1, wide),
            ],
            out_specs=[
                block, pl.BlockSpec((wide, wide), lambda i, p: (i, 0)),
                fixed(rows, wide), fixed(rows, group), fixed(rows, group),
                pl.BlockSpec((1, wide), lambda i, p: (0, i)), fixed(8, wide),
            ],
            scratch_shapes=[
                pltpu.VMEM((rows, wide), F32),
                pltpu.VMEM((rows, wide), BF),
                pltpu.VMEM((wide, wide), BF),
                pltpu.VMEM((rows, wide), F32),
                pltpu.SemaphoreType.DMA((2,)),
            ],
        ),
        out_shape=[
            jax.ShapeDtypeStruct((rows, ff), BF),
            jax.ShapeDtypeStruct((ff, wide), BF),
            jax.ShapeDtypeStruct((rows, wide), BF),
            jax.ShapeDtypeStruct((rows, group), BF),
            jax.ShapeDtypeStruct((rows, group), BF),
            jax.ShapeDtypeStruct((1, ff), F32),
            jax.ShapeDtypeStruct((8, wide), F32),
        ],
        cost_estimate=pl.CostEstimate(
            flops=4 * rows * wide * ff, bytes_accessed=ff * wide * 10, transcendentals=rows
        ),
        name="feed_back",
    )(here, fc2, fc1, out, slope, cotangent, residual, gain)


def finish_kernel(spans, place_ref, mine_ref, theirs_ref, w_ref, *refs):
    here = place_ref[0]
    group = w_ref.shape[1] // 6
    mine, theirs = mine_ref[...].astype(F32), theirs_ref[...].astype(F32)
    for j in range(3):
        part = slice(j * group, (j + 1) * group)
        at = (2 * j * group) + here * group
        w_ref[:, pl.ds(pl.multiple_of(at, 128), group)] = mine[:, part]
        at = (2 * j + 1) * group - here * group
        w_ref[:, pl.ds(pl.multiple_of(at, 128), group)] = theirs[:, part]
    rows = (mine[:, 3 * group :] + theirs[:, 3 * group :]).T
    for (start, stop), ref in zip(spans, refs, strict=True):
        ref[...] = jnp.concatenate([rows[i : i + 1] for i in range(start, stop)], axis=1)


def finish(here, mine, theirs, spans):
    part, across = mine.shape
    width = 2 * (across - 128)

    def fixed(*shape):
        return pl.BlockSpec(shape, lambda i, p: (0, 0))

    sizes = [(1, (stop - start) * part) for start, stop in spans]
    return pl.pallas_call(
        functools.partial(finish_kernel, spans),
        grid_spec=pltpu.PrefetchScalarGridSpec(
            num_scalar_prefetch=1,
            grid=(1,),
            in_specs=[fixed(part, across)] * 2,
            out_specs=[fixed(part, width)] + [fixed(*shape) for shape in sizes],
        ),
        out_shape=[jax.ShapeDtypeStruct((part, width), F32)]
        + [jax.ShapeDtypeStruct(shape, F32) for shape in sizes],
        name="finish",
    )(here, mine, theirs)


def output_kernel(
    token_ref, z_ref, w_ref, late_ref, rows_ref, out_ref, total_ref, residual_ref, sem_ref
):
    step = pl.program_id(0)
    copy = pltpu.make_async_copy(late_ref, residual_ref, sem_ref)

    @pl.when(step == 0)
    def _():
        copy.start()
        total_ref[...] = jnp.zeros_like(total_ref)

    total_ref[...] += dot(z_ref[...], w_ref[...])

    @pl.when(step == pl.num_programs(0) - 1)
    def _():
        copy.wait()
        total = total_ref[...] + residual_ref[...] + rows_ref[-1:, :]
        out_ref[0] = total[: out_ref.shape[1], :].astype(BF)


def output_end(token, activated, w, residual, bias, valid):
    rows, ff = activated.shape
    wide = w.shape[1]
    return pl.pallas_call(
        output_kernel,
        grid=(ff // wide,),
        in_specs=[
            pl.BlockSpec(memory_space=pl.ANY),
            pl.BlockSpec((rows, wide), lambda i: (0, i)),
            pl.BlockSpec((wide, wide), lambda i: (i, 0)),
            pl.BlockSpec(memory_space=pl.ANY),
            pl.BlockSpec((1, wide), lambda i: (0, 0)),
        ],
        out_specs=pl.BlockSpec((1, valid, wide), lambda i: (0, 0, 0)),
        out_shape=jax.ShapeDtypeStruct((1, valid, wide), BF),
        scratch_shapes=[
            pltpu.VMEM((rows, wide), F32),
            pltpu.VMEM((rows, wide), F32),
            pltpu.SemaphoreType.DMA,
        ],
        cost_estimate=pl.CostEstimate(
            flops=2 * rows * wide * ff, bytes_accessed=rows * ff * 4, transcendentals=0
        ),
        name="output_end",
    )(token, activated, w, residual, bias)


def join_kernel(mine_ref, theirs_ref, out_ref, first_ref):
    wide = out_ref.shape[1]
    mine, theirs = mine_ref[...].astype(F32), theirs_ref[...].astype(F32)
    out_ref[...] = mine[:, :wide] + theirs[:, :wide]
    first_ref[...] = mine[:, wide:] + theirs[:, wide:]


def join_second(mine, theirs, wide):
    part, across = mine.shape
    return pl.pallas_call(
        join_kernel,
        out_shape=[
            jax.ShapeDtypeStruct((part, wide), F32),
            jax.ShapeDtypeStruct((part, across - wide), F32),
        ],
        name="join_second",
    )(mine, theirs)


def input_end_kernel(mine_ref, got_ref, residual_ref, normed_ref, gain_ref, inverse_ref, out_ref):
    normed = normed_ref[...]
    weighted = (mine_ref[...].astype(F32) + got_ref[...].astype(F32)) * gain_ref[...]
    first = jnp.mean(weighted, axis=-1, keepdims=True)
    second = jnp.mean(weighted * normed, axis=-1, keepdims=True)
    out_ref[:, 0, :] = residual_ref[...].astype(F32) + inverse_ref[:, 0:1] * (weighted - first - normed * second)


def input_end(mine, got, residual, normed, gain, inverse, valid):
    half, wide = mine.shape
    tile = 384
    block = pl.BlockSpec((tile, wide), lambda i: (i, 0))
    return pl.pallas_call(
        input_end_kernel,
        grid=(half // tile,),
        in_specs=[
            block, block, block, block, pl.BlockSpec((1, wide), lambda i: (0, 0)),
            pl.BlockSpec((tile, 128), lambda i: (i, 0)),
        ],
        out_specs=pl.BlockSpec((tile, 1, wide), lambda i: (i, 0, 0)),
        out_shape=jax.ShapeDtypeStruct((valid, 1, wide), F32),
        cost_estimate=pl.CostEstimate(
            flops=half * wide * 10, bytes_accessed=half * wide * 18, transcendentals=0
        ),
        name="input_end",
    )(mine, got, residual, normed, gain, inverse)


def swap(x, axis, size, bit):
    return lax.ppermute(x, axis, [(i, i ^ bit) for i in range(size)])


def bits_of(size):
    top = size // 4
    return top, [1 << b for b in range(top.bit_length() - 2, -1, -1)]


def gather_blocks(x, size):
    me = lax.axis_index("dp")
    top, bits = bits_of(size)
    held = jnp.stack([x] + [swap(x, "dp", size, j * top) for j in (1, 2, 3)])
    where = [j * top for j in range(4)]
    for bit in bits:
        held = jnp.concatenate([held, swap(held, "dp", size, bit)])
        where = where + [w ^ bit for w in where]
    place = [0] * size
    for i, w in enumerate(where):
        place[w] = i
    return held, jnp.asarray(place, jnp.int32)[me ^ jnp.arange(size)]


def halve(x, axis, bit):
    mine = lax.rem(lax.axis_index("dp") // bit, 2)
    keep = lax.dynamic_index_in_dim(x, mine, axis, keepdims=False)
    give = lax.dynamic_index_in_dim(x, 1 - mine, axis, keepdims=False)
    return keep, give.astype(BF)


def scatter_split(x, size):
    top, _ = bits_of(size)
    mine = lax.axis_index("dp") // top
    gives = [
        lax.dynamic_index_in_dim(x, mine ^ j, 0, keepdims=False).astype(BF) for j in (1, 2, 3)
    ]
    return gives, lax.dynamic_index_in_dim(x, mine, 0, keepdims=False).astype(F32)


def scatter_join(total, gives, size):
    top, _ = bits_of(size)
    for j, give in zip((1, 2, 3), gives, strict=True):
        total = total + swap(give, "dp", size, j * top).astype(F32)
    return total


def after(x, *others):
    return lax.optimization_barrier((x, *others))[0]


def gelu_cdf(values):
    return 0.5 * (1.0 + lax.erf(values * (1.0 / math.sqrt(2.0))))


def layer(
    size, frames_in, ln1_gain, ln1_bias, w_qkv, b_qv, w_o, b_o,
    ln2_gain, ln2_bias, w_fc1, b_fc1, w_fc2, b_fc2, cotangent,
):
    clips, valid, wide = frames_in.shape
    assert clips == 1
    ff = w_fc1.shape[1]
    part = w_qkv.shape[0]
    group = wide // 2
    half = -(-valid // 256) * 256
    here = lax.axis_index("seq")

    def other(x):
        return swap(x, "seq", 2, 1)

    def pick(x, axis, index):
        return lax.dynamic_index_in_dim(x, index, axis, keepdims=False)

    per = ff // wide
    me = lax.axis_index("dp")
    _, bits = bits_of(size)

    vectors = jnp.concatenate([ln1_gain, ln1_bias, b_qv, b_o, ln2_gain, ln2_bias, b_fc1, b_fc2])
    count = vectors.shape[0] // part
    columns = lax.optimization_barrier(
        jnp.pad(vectors.reshape(count, part).T, ((0, 0), (0, 128 - count)))
    )
    w_mine = [
        lax.dynamic_slice_in_dim(w_qkv, j * wide + here * group, group, axis=1) for j in range(3)
    ]
    held, place = gather_blocks(jnp.concatenate(w_mine + [columns], axis=1), size)
    if part % 16:
        held = jnp.take(held, place, axis=0, mode="clip").reshape(1, wide, 3 * group + 128)
        place = jnp.zeros((1,), jnp.int32)
    flag = jnp.concatenate([jnp.stack([here, lax.rem(me, 2)]).astype(jnp.int32), place])
    if part % 16:
        fc2_local = w_fc2.reshape(per, part, wide).transpose(1, 0, 2).reshape(part, ff)
        packed = jnp.concatenate([fc2_local, w_o, w_fc1], axis=1)
    else:
        packed = pack(w_fc2, w_o, w_fc1)
    later = lax.all_gather(packed, "dp", axis=0, tiled=True)
    out_full, fc1_full = later[:, ff : ff + wide], later[:, ff + wide :]
    weights = later
    if part % 16:
        fc2_full = later[:, :ff].reshape(size, part, per, wide)
        weights = (fc2_full.transpose(0, 2, 1, 3).reshape(ff, wide), fc1_full, out_full)

    prepared = prepare(frames_in, half, 0)
    inverse_one = prepared[2]
    normed_both, normed_t, _ = prepare(other(frames_in), half, 1, prepared[:2])
    qkv, w_full, w_flipped, table, scale = projection(held, flag, normed_both, part)

    def vector(start, stop):
        return table[start:stop].reshape(-1, size, part).transpose(1, 0, 2).reshape(-1)

    gain_one, gain_two = table[0], table[5]
    bias_fc1, bias_fc2 = vector(7, 7 + per), table[7 + per]
    o_mine, o_sent, lse = attention_forward(qkv, half, valid)
    o_got = other(o_sent)
    if part % 16:
        residual, hidden_two = attend(flag, frames_in, o_mine, o_got, out_full, 0, table)
    else:
        residual, hidden_two = attend(flag, frames_in, o_mine, o_got, later, per, table)

    pre_act = dot(hidden_two, fc1_full) + bias_fc1
    cdf = gelu_cdf(pre_act)
    density = jnp.exp(-0.5 * pre_act * pre_act) * (1.0 / math.sqrt(2.0 * math.pi))
    activated, slope = lax.optimization_barrier(
        ((pre_act * cdf).astype(BF), (cdf + pre_act * density).astype(BF))
    )
    (
        grad_pre_low, fc2_full, grad_residual_low,
        do_mine, do_sent, grad_bias_fc1, grad_sums,
    ) = feed_back(flag, weights, slope, cotangent, residual, gain_two[None], part)
    do_got = other(do_sent)
    fc2_keep, fc2_give = third_gradient(flag, activated, cotangent, size, do_sent)
    second_part = second_gradient(
        flag, fc2_give, o_mine, o_got, grad_residual_low, hidden_two, grad_pre_low
    )
    grad_second = lax.psum_scatter(second_part, "dp", scatter_dimension=0, tiled=True)

    def backward(token, start, count):
        return attention_backward(
            qkv, o_mine, o_sent, do_mine, do_got, lse, token, half, valid, start, count
        )

    x = fc2_keep.astype(F32) + swap(fc2_give, "dp", size, 1).astype(F32)
    x = x.reshape(size // 2, 2, -1, wide)
    keep, give = pick(x, 1, here).astype(BF), pick(x, 1, 1 - here).astype(BF)
    got = other(give)
    ds = [backward(give, 0, group // 128)]
    grad_other = projection_input_gradient(w_flipped, ds, ds[0], half, 1, BF)
    grad_got = other(grad_other)
    for at in range(len(bits) - 2, -1, -1):
        x = after(keep, grad_other).astype(F32) + got.astype(F32)
        keep, give = halve(x.reshape(-1, 2, *x.shape[1:]), 1, bits[at])
        keep, got = keep.astype(BF), swap(give, "dp", size, bits[at])
    fc2_keep_x, fc2_got_x = keep, got

    vectors = [(7, grad_bias_fc1)]
    if part % 16:
        grad_qkv, norm_sums, sums = projection_weight_gradient(normed_t, w_full, scale, ds)
        grad_bias_mine = jnp.stack([sums[0, :group], sums[0, 2 * group :]])
        zero = jnp.zeros_like(grad_bias_mine)
        grad_bias_qv = jnp.where(
            here == 0,
            jnp.concatenate([grad_bias_mine, zero], axis=1),
            jnp.concatenate([zero, grad_bias_mine], axis=1),
        )

        def as_columns(start, v):
            v = v.reshape(size, -1, part).transpose(0, 2, 1)
            return jnp.pad(v, ((0, 0), (0, 0), (start, 128 - start - v.shape[2])))

        columns = norm_sums.reshape(size, part, 128) + as_columns(2, grad_bias_qv)
        vectors += [(p, grad_sums[i]) for i, p in enumerate((4, 5, 6, 7 + per))]
        columns = columns + sum(as_columns(start, v) for start, v in vectors)
        x = jnp.concatenate([grad_qkv.reshape(size, part, -1), columns.astype(BF)], axis=2)
        keep, give = halve(x.reshape(size // 2, 2, *x.shape[1:]), 1, 1)
    else:
        keep, give = spread_weight_gradient(
            flag, give, normed_t, w_full, scale, ds, grad_bias_fc1, grad_sums, part
        )
    got = swap(give, "dp", size, 1)
    for at in range(len(bits) - 2, -1, -1):
        x = keep.astype(F32) + got.astype(F32)
        keep, give = halve(x.reshape(-1, 2, *x.shape[1:]), 1, bits[at])
        got = swap(give, "dp", size, bits[at])
    fc2_keep, fc2_got = after((fc2_keep_x, fc2_got_x), give)
    fc2_gives, fc2_stay = scatter_split(fc2_keep.astype(F32) + fc2_got.astype(F32), size)
    grad_mine = projection_input_gradient(w_flipped, ds, fc2_gives[2], half, 0, BF)
    frames_out = output_end(
        fc2_gives[2], activated, fc2_full, residual, bias_fc2[None], valid
    )
    fc2_part = scatter_join(fc2_stay, fc2_gives, size).astype(BF)
    gives, stay = scatter_split(keep.astype(F32) + got.astype(F32), size)
    grad_input = input_end(
        grad_mine, grad_got, grad_residual_low, normed_both, gain_one[None], inverse_one, valid
    ).transpose(1, 0, 2)
    mine = scatter_join(stay, gives, size).astype(BF)
    theirs = other(mine)
    spans = ((0, 1), (1, 2), (2, 4), (4, 5), (5, 6), (6, 7), (7, 7 + per), (7 + per, 8 + per))
    grad_w_qkv, *small = finish(flag, mine, theirs, spans)
    small = [v[0] for v in small]
    fc2_got = other(fc2_part)
    fc2_sum = jnp.where(
        here == 0,
        jnp.concatenate([fc2_part, fc2_got], axis=0),
        jnp.concatenate([fc2_got, fc2_part], axis=0),
    ).astype(F32)
    out_sum, first_sum = join_second(grad_second, other(grad_second), wide)
    return (
        frames_out, grad_input, small[0], small[1], grad_w_qkv, small[2], out_sum, small[3],
        small[4], small[5], first_sum, small[6], fc2_sum, small[7],
    )


def solution(mesh):
    frames, rows, vector = P("dp", "seq", None), P("dp", None), P("dp")
    in_specs = (
        frames, vector, vector, rows, vector, rows, vector,
        vector, vector, rows, vector, rows, vector, frames,
    )
    out_specs = (
        frames, frames, vector, vector, rows, vector, rows, vector,
        vector, vector, rows, vector, rows, vector,
    )
    return jax.shard_map(
        functools.partial(layer, mesh.shape["dp"]),
        mesh=mesh, in_specs=in_specs, out_specs=out_specs, check_vma=False,
    )
```

```python
import functools
import math

import jax
import jax.numpy as jnp
from jax import lax
from jax.experimental import pallas as pl
from jax.experimental.pallas import tpu as pltpu
from jax.sharding import PartitionSpec as P


EPSILON = 1e-05
BF = jnp.bfloat16
F32 = jnp.float32
MASKED = -1e30


def dot(a, b, ca=1, cb=0):
    return lax.dot_general(a, b, (((ca,), (cb,)), ((), ())), preferred_element_type=F32)


def split3(x):
    high = x.astype(BF).astype(F32)
    rest = x - high
    mid = rest.astype(BF).astype(F32)
    return high, mid, (rest - mid).astype(BF).astype(F32)


def forward_kernel(half, valid, q_ref, k_ref, v_ref, mine_ref, sent_ref, lse_ref, kx_ref, vt_ref):
    rows = k_ref.shape[0]
    wide = q_ref.shape[0]

    kx_ref[:, :128] = k_ref[...]
    row = lax.broadcasted_iota(jnp.int32, (rows, 128), 0)
    lane = lax.broadcasted_iota(jnp.int32, (rows, 128), 1)
    padded = (lax.rem(row, half) >= valid) & (lane == 0)
    kx_ref[:, 128:] = jnp.where(padded, MASKED, 0.0).astype(BF)
    vt = v_ref[...].T
    vt_ref[0:64, :] = vt[0:64, :]
    vt_ref[64:80, :] = jnp.ones((16, rows), BF)
    vt_ref[80:144, :] = vt[64:128, :]
    vt_ref[144:160, :] = jnp.ones((16, rows), BF)

    lane = lax.broadcasted_iota(jnp.int32, (wide, 128), 1)
    q = q_ref[...] * jnp.asarray(0.125, BF)
    one = jnp.where(lane == 0, 1.0, 0.0).astype(BF)
    outs, sums = [], []
    for h in range(2):
        mine = (lane < 64) if h == 0 else (lane >= 64)
        qx = jnp.concatenate([jnp.where(mine, q, jnp.zeros_like(q)), one], axis=1)
        s = dot(kx_ref[...], qx, 1, 1)
        peak = jnp.max(s, axis=0, keepdims=True)
        p = jnp.exp(s - peak).astype(BF)
        o = dot(vt_ref[80 * h : 80 * h + 80, :], p)
        total = o[64:65, :]
        outs.append(o[0:64, :] / total)
        sums.append(peak + jnp.log(total))
    o = jnp.concatenate(outs, axis=0).T.astype(BF)
    mine_ref[...] = o[:half]
    sent_ref[...] = o[half:]
    lse_ref[...] = jnp.concatenate(sums + [jnp.zeros((6, wide), F32)], axis=0)[None]


def attention_forward(qkv, half, valid):
    rows, width = qkv.shape
    pairs = width // 3 // 128
    block = pl.BlockSpec((half, 128), lambda p: (0, p))
    return pl.pallas_call(
        functools.partial(forward_kernel, half, valid),
        grid=(pairs,),
        in_specs=[
            pl.BlockSpec((rows, 128), lambda p: (0, p)),
            pl.BlockSpec((rows, 128), lambda p: (0, pairs + p)),
            pl.BlockSpec((rows, 128), lambda p: (0, 2 * pairs + p)),
        ],
        out_specs=[block, block, pl.BlockSpec((1, 8, rows), lambda p: (p, 0, 0))],
        out_shape=[
            jax.ShapeDtypeStruct((half, pairs * 128), BF),
            jax.ShapeDtypeStruct((half, pairs * 128), BF),
            jax.ShapeDtypeStruct((pairs, 8, rows), F32),
        ],
        scratch_shapes=[pltpu.VMEM((rows, 256), BF), pltpu.VMEM((160, rows), BF)],
        cost_estimate=pl.CostEstimate(
            flops=pairs * 2 * 4 * rows * rows * 256,
            bytes_accessed=rows * width * 2 + rows * width,
            transcendentals=pairs * 2 * rows * rows,
        ),
        name="attention_forward",
    )(qkv, qkv, qkv)


def backward_kernel(
    half, valid, q_ref, k_ref, v_ref, o_mine_ref, o_sent_ref, mine_ref, got_ref, lse_ref, token_ref,
    d_ref, kt_ref, vt_ref, dkt_ref, dvt_ref,
):
    rows = k_ref.shape[0]
    step = pl.program_id(1)

    @pl.when(step == 0)
    def _():
        kt_ref[0:128, :] = k_ref[...].T
        vt_ref[0:128, :] = v_ref[...].T
        row = lax.broadcasted_iota(jnp.int32, (128, rows), 0)
        key = lax.broadcasted_iota(jnp.int32, (128, rows), 1)
        bias = jnp.where(lax.rem(key, half) >= valid, MASKED, 0.0)
        ones = jnp.where((row >= 1) & (row < 4), 1.0, 0.0)
        kt_ref[128:256, :] = jnp.where(row == 0, bias, ones).astype(BF)
        vt_ref[128:256, :] = ones.astype(BF)
        dkt_ref[...] = jnp.zeros_like(dkt_ref)
        dvt_ref[...] = jnp.zeros_like(dvt_ref)

    tile = q_ref.shape[0]
    first = step < half // tile
    lane = lax.broadcasted_iota(jnp.int32, (tile, 128), 1)
    q = q_ref[...] * jnp.asarray(0.125, BF)
    do = jnp.where(first, mine_ref[...], got_ref[...])
    o = jnp.where(first, o_mine_ref[...], o_sent_ref[...])
    product = do.astype(F32) * o.astype(F32)
    lse = lse_ref[0].T
    qt, dot_t = q.T, do.T

    def extra(x, first):
        a, b, c = split3(-x)
        tail = jnp.where(lane == 2, b, jnp.where(lane == 3, c, 0.0))
        return jnp.where(lane == 0, first, jnp.where(lane == 1, a, tail)).astype(BF)

    dq = []
    for h in range(2):
        mine = (lane < 64) if h == 0 else (lane >= 64)
        delta = jnp.sum(jnp.where(mine, product, 0.0), axis=1, keepdims=True)
        qx = jnp.concatenate(
            [jnp.where(mine, q, jnp.zeros_like(q)), extra(lse[:, h : h + 1], 1.0)], axis=1
        )
        dx = jnp.concatenate([jnp.where(mine, do, jnp.zeros_like(do)), extra(delta, 0.0)], axis=1)
        p = jnp.exp(dot(qx, kt_ref[...]))
        low = p.astype(BF)
        ds = (p * dot(dx, vt_ref[...])).astype(BF)
        dq.append(dot(ds, k_ref[...]))
        part = slice(64 * h, 64 * h + 64)
        dkt_ref[part, :] += dot(qt[part, :], ds)
        dvt_ref[part, :] += dot(dot_t[part, :], low)
    dq = (jnp.where(lane < 64, dq[0], dq[1]) * 0.125).astype(BF)
    d_ref[0, pl.ds(pl.multiple_of(step * tile, 128), tile), :] = dq

    @pl.when(step == pl.num_programs(1) - 1)
    def _():
        d_ref[1] = dkt_ref[...].T.astype(BF)
        d_ref[2] = dvt_ref[...].T.astype(BF)


def attention_backward(qkv, o_mine, o_sent, do_mine, do_got, lse, token, half, valid, start, count):
    rows, width = qkv.shape
    pairs = width // 3 // 128

    def whole(part):
        return pl.BlockSpec((rows, 128), lambda p, i: (0, part * pairs + start + p))

    tile = 384
    per_half = half // tile
    block = pl.BlockSpec((tile, 128), lambda p, i: (i, start + p))
    fixed = pl.BlockSpec((tile, 128), lambda p, i: (lax.rem(i, per_half), start + p))
    return pl.pallas_call(
        functools.partial(backward_kernel, half, valid),
        grid=(count, 2 * per_half),
        in_specs=[
            block, whole(1), whole(2), fixed, fixed, fixed, fixed,
            pl.BlockSpec((1, 8, tile), lambda p, i: (start + p, 0, i)),
            pl.BlockSpec(memory_space=pl.ANY),
        ],
        out_specs=pl.BlockSpec((3, rows, 128), lambda p, i: (0, 0, p)),
        out_shape=jax.ShapeDtypeStruct((3, rows, count * 128), BF),
        scratch_shapes=[
            pltpu.VMEM((256, rows), BF),
            pltpu.VMEM((256, rows), BF),
            pltpu.VMEM((128, rows), F32),
            pltpu.VMEM((128, rows), F32),
        ],
        cost_estimate=pl.CostEstimate(
            flops=count * 2 * 8 * rows * rows * 256,
            bytes_accessed=count * rows * 128 * 16,
            transcendentals=count * 2 * rows * rows,
        ),
        name="attention_backward",
    )(qkv, qkv, qkv, o_mine, o_sent, do_mine, do_got, lse, token)


def rows_below(x, start, valid):
    row = start + lax.broadcasted_iota(jnp.int32, x.shape, 0)
    return jnp.where(row < valid, x, jnp.zeros_like(x))


def prepare_kernel(valid, x_ref, *refs):
    normed_ref, flipped_ref, inverse_ref = refs[-3:]
    tile, wide = normed_ref.shape
    x = rows_below(x_ref[0].astype(F32), pl.program_id(0) * tile, valid)
    centered = x - jnp.mean(x, axis=-1, keepdims=True)
    inverse = lax.rsqrt(jnp.mean(centered * centered, axis=-1, keepdims=True) + EPSILON)
    normed = centered * inverse
    normed_ref[...] = normed
    inverse_ref[...] = jnp.broadcast_to(inverse, inverse_ref.shape)
    flipped_ref[:wide, :] = normed.T.astype(BF)
    flipped_ref[wide:, :] = jnp.ones((16, tile), BF)


def prepare(frames, half, block, filled=()):
    _, valid, wide = frames.shape
    tile = 384
    first = block * (half // tile)
    return pl.pallas_call(
        functools.partial(prepare_kernel, valid),
        grid=(half // tile,),
        in_specs=[pl.BlockSpec((1, tile, wide), lambda i: (0, i, 0))]
        + [pl.BlockSpec(memory_space=pl.ANY)] * len(filled),
        out_specs=[
            pl.BlockSpec((tile, wide), lambda i: (first + i, 0)),
            pl.BlockSpec((wide + 16, tile), lambda i: (0, first + i)),
            pl.BlockSpec((tile, 128), lambda i: (i, 0)),
        ],
        out_shape=[
            jax.ShapeDtypeStruct((2 * half, wide), F32),
            jax.ShapeDtypeStruct((wide + 16, 2 * half), BF),
            jax.ShapeDtypeStruct((half, 128), F32),
        ],
        input_output_aliases={1: 0, 2: 1} if filled else {},
        cost_estimate=pl.CostEstimate(
            flops=half * wide * 16, bytes_accessed=half * wide * 8, transcendentals=half
        ),
        name="prepare",
    )(frames, *filled)


def attend_kernel(valid, place_ref, x_ref, mine_ref, got_ref, w_ref, rows_ref, sum_ref, h_ref):
    tile = sum_ref.shape[0]
    group = mine_ref.shape[1]
    here = place_ref[0]
    first = w_ref[pl.ds(pl.multiple_of(here * group, 128), group), :]
    other = w_ref[pl.ds(pl.multiple_of(group - here * group, 128), group), :]
    total = dot(mine_ref[...], first) + dot(got_ref[...], other)
    x = rows_below(x_ref[0].astype(F32), pl.program_id(0) * tile, valid)
    total = x + total + rows_ref[4:5, :]
    sum_ref[...] = total
    centered = total - jnp.mean(total, axis=-1, keepdims=True)
    inverse = lax.rsqrt(jnp.mean(centered * centered, axis=-1, keepdims=True) + EPSILON)
    h_ref[...] = (centered * inverse * rows_ref[5:6, :] + rows_ref[6:7, :]).astype(BF)


def attend(here, frames, mine, got, w, column, table):
    _, valid, wide = frames.shape
    half, group = mine.shape
    tile = 256
    block = pl.BlockSpec((tile, group), lambda i, p: (i, 0))
    out = pl.BlockSpec((tile, wide), lambda i, p: (i, 0))
    return pl.pallas_call(
        functools.partial(attend_kernel, valid),
        grid_spec=pltpu.PrefetchScalarGridSpec(
            num_scalar_prefetch=1,
            grid=(half // tile,),
            in_specs=[
                pl.BlockSpec((1, tile, wide), lambda i, p: (0, i, 0)), block, block,
                pl.BlockSpec((wide, wide), lambda i, p: (0, column)),
                pl.BlockSpec((16, wide), lambda i, p: (0, 0)),
            ],
            out_specs=[out, out],
        ),
        out_shape=[
            jax.ShapeDtypeStruct((half, wide), F32),
            jax.ShapeDtypeStruct((half, wide), BF),
        ],
        cost_estimate=pl.CostEstimate(
            flops=4 * half * wide * group, bytes_accessed=half * wide * 10, transcendentals=half
        ),
        name="attend",
    )(here, frames, mine, got, w, table)


def projection_kernel(
    part, group, place_ref, held_ref, x_ref, qkv_ref, w_ref, wt_ref, rows_ref, scale_ref,
    gain_ref, bias_ref, columns_ref,
):
    wide, width = w_ref.shape

    @pl.when(pl.program_id(0) == 0)
    def _():
        blocks, extent, _ = held_ref.shape
        for d in range(blocks):
            block = held_ref[place_ref[d]]
            w_ref[d * extent : (d + 1) * extent, :] = block[:, :width]
            columns_ref[d * extent : (d + 1) * extent, :] = block[:, width:].astype(F32)
        wt_ref[...] = w_ref[...].T
        table = columns_ref[...].T[:16, :]
        rows_ref[...] = table
        scale_ref[:, :128] = jnp.broadcast_to(columns_ref[:, 0:1], (wide, 128))
        scale_ref[:, 128:] = jnp.broadcast_to(columns_ref[:, 1:2], (wide, 128))
        gain_ref[...] = table[:8]
        here = place_ref[blocks]
        few = group // 2
        row = lax.broadcasted_iota(jnp.int32, (few, group), 0)
        entry = lax.broadcasted_iota(jnp.int32, (few, group), 1)
        base = row + part * (row // part)
        for v in range(2):
            at = pl.multiple_of(v * (wide // 2) + here * few, 64)
            low = columns_ref[pl.ds(at, few), :].T[:16].astype(BF)
            total = jnp.zeros((16, group), F32)
            for j in range(2):
                chosen = entry == base + part * j
                picked = dot(low, jnp.where(chosen, 1.0, 0.0).astype(BF))
                total = total + picked[2 + j : 3 + j, :]
            bias_ref[:, 2 * v * group : (2 * v + 1) * group] = total[:8]
        bias_ref[:, group : 2 * group] = jnp.zeros((8, group), F32)

    h = (x_ref[...] * gain_ref[0:1, :] + gain_ref[1:2, :]).astype(BF)
    qkv_ref[...] = (dot(h, w_ref[...]) + bias_ref[0:1, :]).astype(BF)


def projection(held, place, normed, part):
    blocks, extent, across = held.shape
    width = across - 128
    rows, wide = normed.shape
    tile = 384

    def fixed(*shape):
        return pl.BlockSpec(shape, lambda i, p: tuple(0 for _ in shape))

    return pl.pallas_call(
        functools.partial(projection_kernel, part, width // 3),
        grid_spec=pltpu.PrefetchScalarGridSpec(
            num_scalar_prefetch=1,
            grid=(rows // tile,),
            in_specs=[fixed(blocks, extent, across), pl.BlockSpec((tile, wide), lambda i, p: (i, 0))],
            out_specs=[
                pl.BlockSpec((tile, width), lambda i, p: (i, 0)),
                fixed(wide, width), fixed(width, wide), fixed(16, wide), fixed(wide, 256),
            ],
            scratch_shapes=[
                pltpu.VMEM((8, wide), F32),
                pltpu.VMEM((8, width), F32),
                pltpu.VMEM((wide, 128), F32),
            ],
        ),
        out_shape=[
            jax.ShapeDtypeStruct((rows, width), BF),
            jax.ShapeDtypeStruct((wide, width), BF),
            jax.ShapeDtypeStruct((width, wide), BF),
            jax.ShapeDtypeStruct((16, wide), F32),
            jax.ShapeDtypeStruct((wide, 256), F32),
        ],
        cost_estimate=pl.CostEstimate(
            flops=2 * rows * wide * width, bytes_accessed=rows * wide * 8, transcendentals=0
        ),
        name="projection",
    )(place, held, normed)


def weight_kernel(pieces, xt_ref, w_ref, scale_ref, *refs):
    d_refs, (g_ref, c_ref, s_ref) = refs[:pieces], refs[pieces:]
    d = jnp.concatenate([r[0] for r in d_refs], axis=1)
    m = dot(xt_ref[...], d)
    s = m[w_ref.shape[0] :][:8]
    m = m[: w_ref.shape[0]]
    s_ref[...] = s
    gain, shift = scale_ref[:, 0:1], scale_ref[:, 128:129]
    total = s[0:1, :]
    g_ref[...] = (gain * m + shift * total).astype(BF)
    w = w_ref[...].astype(F32)
    lane = lax.broadcasted_iota(jnp.int32, c_ref.shape, 1)
    first = jnp.sum(w * m, axis=1, keepdims=True)
    second = jnp.sum(w * total, axis=1, keepdims=True)
    now = jnp.where(lane == 0, first, jnp.where(lane == 1, second, 0.0))
    before = jnp.where(pl.program_id(0) == 0, jnp.zeros_like(now), c_ref[...])
    c_ref[...] = before + now


def projection_weight_gradient(xt, w, scale, ds):
    tall, rows = xt.shape
    wide = w.shape[0]
    group = sum(d.shape[2] for d in ds)
    return pl.pallas_call(
        functools.partial(weight_kernel, len(ds)),
        grid=(3,),
        in_specs=[
            pl.BlockSpec((tall, rows), lambda j: (0, 0)),
            pl.BlockSpec((wide, group), lambda j: (0, j)),
            pl.BlockSpec((wide, 256), lambda j: (0, 0)),
        ]
        + [pl.BlockSpec((1, *d.shape[1:]), lambda j: (j, 0, 0)) for d in ds],
        out_specs=[
            pl.BlockSpec((wide, group), lambda j: (0, j)),
            pl.BlockSpec((wide, 128), lambda j: (0, 0)),
            pl.BlockSpec((8, group), lambda j: (0, j)),
        ],
        out_shape=[
            jax.ShapeDtypeStruct((wide, 3 * group), BF),
            jax.ShapeDtypeStruct((wide, 128), F32),
            jax.ShapeDtypeStruct((8, 3 * group), F32),
        ],
        cost_estimate=pl.CostEstimate(
            flops=2 * rows * wide * 3 * group, bytes_accessed=rows * wide * 4, transcendentals=0
        ),
        name="projection_weight_gradient",
    )(xt, w, scale, *ds)


def spread_kernel(
    part, pieces, per, place_ref, token_ref, xt_ref, w_ref, scale_ref, *refs
):
    d_refs, refs = refs[:pieces], refs[pieces:]
    b_ref, v_ref, keep_ref, give_ref, c_ref, s_ref, first_ref, second_ref = refs
    step = pl.program_id(0)
    wide, group = w_ref.shape
    d = jnp.concatenate([r[0] for r in d_refs], axis=1)
    m = dot(xt_ref[...], d)
    s = m[wide : wide + 8]
    s_ref[step] = s

    @pl.when(step == 0)
    def _():
        first_ref[...] = jnp.zeros_like(first_ref)
        second_ref[...] = jnp.zeros_like(second_ref)

    gain, shift = scale_ref[:, :128], scale_ref[:, 128:]
    one, two, gs = first_ref[...], second_ref[...], []
    for i in range(group // 128):
        columns = slice(128 * i, 128 * (i + 1))
        piece, w, total = m[:wide, columns], w_ref[:, columns].astype(F32), s[0:1, columns]
        one, two = one + w * piece, two + w * total
        gs.append((gain * piece + shift * total).astype(BF))
    first_ref[...], second_ref[...] = one, two
    at = pl.ds(pl.multiple_of(step * group, 128), group)
    spread_store(part, place_ref, keep_ref, give_ref, jnp.concatenate(gs, axis=1), at)

    @pl.when(step == 2)
    def _():
        lane = lax.broadcasted_iota(jnp.int32, c_ref.shape, 1)
        second = jnp.sum(second_ref[...], axis=1, keepdims=True)
        first = jnp.sum(first_ref[...], axis=1, keepdims=True)
        columns = jnp.where(lane == 0, first, jnp.where(lane == 1, second, 0.0))
        small = v_ref[...].T
        for i, name in enumerate((4, 5, 6, 7 + per)):
            columns = jnp.where(lane == name, small[:, i : i + 1], columns)
        v = jnp.broadcast_to(b_ref[...], (8, b_ref.shape[1])).T[:, 0:1]
        for j in range(per):
            column = jnp.concatenate(
                [v[(d * per + j) * part :][:part] for d in range(wide // part)], axis=0
            )
            columns = jnp.where(lane == 7 + j, column, columns)
        c_ref[...] = columns
        half = group // 2
        low = lane[:half]
        for side in (0, 2):
            v = s_ref[side].T[:, 0:1]
            at = pl.ds(pl.multiple_of(place_ref[1] * half + side * wide // 4, 64), half)
            block = c_ref[at, :]
            for j in range(2):
                column = jnp.concatenate(
                    [v[(2 * d + j) * part :][:part] for d in range(half // part)], axis=0
                )
                block = jnp.where(low == 2 + j, column, block)
            c_ref[at, :] = block
        g = c_ref[...].astype(BF)
        spread_store(part, place_ref, keep_ref, give_ref, g, pl.ds(3 * group, 128))


def spread_store(part, place_ref, keep_ref, give_ref, value, columns):
    value = value.reshape(keep_ref.shape[0], 2, part, value.shape[1])
    even, odd = value[:, 0], value[:, 1]
    low = place_ref[0] == 0
    keep_ref[:, :, columns] = jnp.where(low, even, odd)
    give_ref[:, :, columns] = jnp.where(low, odd, even)


def spread_weight_gradient(place, token, xt, w, scale, ds, bias, sums, part):
    _, rows = xt.shape
    wide = w.shape[0]
    group = sum(d.shape[2] for d in ds)
    size = wide // part
    out = pl.BlockSpec((size // 2, part, 3 * group + 128), lambda j, p: (0, 0, 0))

    def fixed(x):
        return pl.BlockSpec(x.shape, lambda j, p: (0, 0))

    return pl.pallas_call(
        functools.partial(spread_kernel, part, len(ds), bias.shape[1] // wide),
        grid_spec=pltpu.PrefetchScalarGridSpec(
            num_scalar_prefetch=1,
            grid=(3,),
            in_specs=[
                pl.BlockSpec(memory_space=pl.ANY),
                fixed(xt),
                pl.BlockSpec((wide, group), lambda j, p: (0, j)),
                fixed(scale),
            ]
            + [pl.BlockSpec((1, *d.shape[1:]), lambda j, p: (j, 0, 0)) for d in ds]
            + [fixed(bias), fixed(sums)],
            out_specs=[out, out],
            scratch_shapes=[
                pltpu.VMEM((wide, 128), F32),
                pltpu.VMEM((3, 8, group), F32),
                pltpu.VMEM((wide, 128), F32),
                pltpu.VMEM((wide, 128), F32),
            ],
        ),
        out_shape=[jax.ShapeDtypeStruct((size // 2, part, 3 * group + 128), BF)] * 2,
        cost_estimate=pl.CostEstimate(
            flops=2 * rows * wide * 3 * group, bytes_accessed=rows * wide * 4, transcendentals=0
        ),
        name="spread_weight_gradient",
    )(place, token, xt, w, scale, *ds, bias, sums)


def input_kernel(pieces, token_ref, wt_ref, *refs):
    d_refs, out_ref = refs[:pieces], refs[pieces]
    d = jnp.concatenate([r[j] for j in range(3) for r in d_refs], axis=1)
    out_ref[...] = dot(d, wt_ref[...]).astype(out_ref.dtype)


def projection_input_gradient(wt, ds, token, half, block, kind):
    wide = wt.shape[1]
    tile = 384
    start = block * (half // tile)
    return pl.pallas_call(
        functools.partial(input_kernel, len(ds)),
        grid=(half // tile,),
        in_specs=[pl.BlockSpec(memory_space=pl.ANY), pl.BlockSpec(wt.shape, lambda i: (0, 0))]
        + [pl.BlockSpec((3, tile, d.shape[2]), lambda i: (0, start + i, 0)) for d in ds],
        out_specs=pl.BlockSpec((tile, wide), lambda i: (i, 0)),
        out_shape=jax.ShapeDtypeStruct((half, wide), kind),
        cost_estimate=pl.CostEstimate(
            flops=2 * half * wt.size, bytes_accessed=half * wt.shape[0] * 4, transcendentals=0
        ),
        name="projection_input_gradient",
    )(token, wt, *ds)


def second_kernel(place_ref, token_ref, mine_ref, got_ref, drb_ref, h_ref, du_ref, out_ref, ht_ref):
    group = mine_ref.shape[1]
    step = pl.program_id(0)

    @pl.when(step == 0)
    def _():
        ht_ref[...] = h_ref[...].T
        here = place_ref[0]
        first = pl.multiple_of(here * group, 128)
        other = pl.multiple_of(group - here * group, 128)
        out_ref[pl.ds(first, group), :] = dot(mine_ref[...], drb_ref[...], 0, 0).astype(BF)
        out_ref[pl.ds(other, group), :] = dot(got_ref[...], drb_ref[...], 0, 0).astype(BF)

    @pl.when(step > 0)
    def _():
        out_ref[...] = dot(ht_ref[...], du_ref[...]).astype(BF)


def second_gradient(here, token, o_mine, o_got, drb, hidden, du):
    rows, wide = hidden.shape
    ff = du.shape[1]

    def fixed(x):
        return pl.BlockSpec(x.shape, lambda i, p: (0, 0))

    return pl.pallas_call(
        second_kernel,
        grid_spec=pltpu.PrefetchScalarGridSpec(
            num_scalar_prefetch=1,
            grid=(1 + ff // wide,),
            in_specs=[
                pl.BlockSpec(memory_space=pl.ANY), fixed(o_mine), fixed(o_got), fixed(drb), fixed(hidden),
                pl.BlockSpec((rows, wide), lambda i, p: (0, jnp.maximum(i - 1, 0))),
            ],
            out_specs=pl.BlockSpec((wide, wide), lambda i, p: (0, i)),
            scratch_shapes=[pltpu.VMEM((wide, rows), BF)],
        ),
        out_shape=jax.ShapeDtypeStruct((wide, wide + ff), BF),
        cost_estimate=pl.CostEstimate(
            flops=2 * rows * wide * (wide + ff), bytes_accessed=rows * ff * 4, transcendentals=0
        ),
        name="second_gradient",
    )(here, token, o_mine, o_got, drb, hidden, du)


def pack_kernel(fc2_ref, out_ref, fc1_ref, packed_ref):
    part, wide = out_ref.shape
    per = fc2_ref.shape[0] // part
    for j in range(per):
        packed_ref[:, j * wide : (j + 1) * wide] = fc2_ref[j * part : (j + 1) * part, :]
    packed_ref[:, per * wide : (per + 1) * wide] = out_ref[...]
    packed_ref[:, (per + 1) * wide :] = fc1_ref[...]


def pack(w_fc2, w_o, w_fc1):
    part, wide = w_o.shape
    across = wide + 2 * w_fc1.shape[1]
    return pl.pallas_call(
        pack_kernel, out_shape=jax.ShapeDtypeStruct((part, across), BF), name="pack"
    )(w_fc2, w_o, w_fc1)


def fill_rows(ref, x):
    valid = x.shape[0]
    start = valid // 16 * 16
    ref[start:, :] = jnp.zeros((ref.shape[0] - start, ref.shape[1]), ref.dtype)
    ref[:valid, :] = x


def third_kernel(place_ref, z_ref, cot_ref, token_ref, keep_ref, give_ref, padded_ref):
    @pl.when(pl.program_id(0) == 0)
    def _():
        fill_rows(padded_ref, cot_ref[0])

    value = dot(z_ref[...], padded_ref[...], 0, 0).astype(BF)
    owners, extent, wide = keep_ref.shape
    value = value.reshape(owners, 2, extent, wide)

    @pl.when(place_ref[0] == 0)
    def _():
        keep_ref[...] = value[:, 0]
        give_ref[...] = value[:, 1]

    @pl.when(place_ref[0] == 1)
    def _():
        keep_ref[...] = value[:, 1]
        give_ref[...] = value[:, 0]


def third_gradient(parity, activated, cotangent, size, token):
    _, valid, wide = cotangent.shape
    rows, ff = activated.shape
    extent = ff // size
    owners = wide // extent // 2
    out = pl.BlockSpec((owners, extent, wide), lambda i, p: (i, 0, 0))
    return pl.pallas_call(
        third_kernel,
        grid_spec=pltpu.PrefetchScalarGridSpec(
            num_scalar_prefetch=1,
            grid=(ff // wide,),
            in_specs=[
                pl.BlockSpec((rows, wide), lambda i, p: (0, i)),
                pl.BlockSpec((1, valid, wide), lambda i, p: (0, 0, 0)),
                pl.BlockSpec(memory_space=pl.ANY),
            ],
            out_specs=[out, out],
            scratch_shapes=[pltpu.VMEM((rows, wide), BF)],
        ),
        out_shape=[jax.ShapeDtypeStruct((size // 2, extent, wide), BF)] * 2,
        cost_estimate=pl.CostEstimate(
            flops=2 * rows * wide * ff, bytes_accessed=rows * ff * 4, transcendentals=0
        ),
        name="third_gradient",
    )(parity, activated, cotangent, token)


def feed_back_kernel(
    part, place_ref, fc2_ref, fc1_ref, late_out_ref, slope_ref, cot_ref, late_ref, gain_ref,
    du_ref, flat_ref, low_ref, mine_ref, sent_ref, bias_ref, sums_ref,
    total_ref, padded_ref, out_ref, residual_ref, sem_ref,
):
    step = pl.program_id(0)
    rows, wide = total_ref.shape
    group = mine_ref.shape[1]
    per = fc2_ref.shape[1] // wide

    first = per * wide if part else 0
    copies = (
        pltpu.make_async_copy(late_out_ref.at[:, first : first + wide], out_ref, sem_ref.at[0]),
        pltpu.make_async_copy(late_ref, residual_ref, sem_ref.at[1]),
    )

    @pl.when(step == 0)
    def _():
        for copy in copies:
            copy.start()
        fill_rows(padded_ref, cot_ref[0])
        total_ref[...] = jnp.zeros_like(total_ref)

    if part:
        for d in range(fc2_ref.shape[0] // part):
            for j in range(per):
                block = fc2_ref[d * part : (d + 1) * part, j * wide : (j + 1) * wide]
                flat_ref[(d * per + j) * part : (d * per + j + 1) * part, :] = block
    else:
        flat_ref[...] = fc2_ref[...]
    du = dot(padded_ref[...], flat_ref[...], 1, 1) * slope_ref[...].astype(F32)
    bias_ref[...] = jnp.sum(du, axis=0, keepdims=True)
    du = du.astype(BF)
    du_ref[...] = du
    total_ref[...] += dot(du, fc1_ref[...], 1, 1)

    @pl.when(step == pl.num_programs(0) - 1)
    def _():
        for copy in copies:
            copy.wait()
        tile = 64

        def body(i, sums):
            at = pl.ds(pl.multiple_of(i * tile, tile), tile)
            r = residual_ref[at, :]
            centered = r - jnp.mean(r, axis=-1, keepdims=True)
            inverse = lax.rsqrt(jnp.mean(centered * centered, axis=-1, keepdims=True) + EPSILON)
            normed = centered * inverse
            dh = total_ref[at, :]
            weighted = dh * gain_ref[...]
            first = jnp.mean(weighted, axis=-1, keepdims=True)
            second = jnp.mean(weighted * normed, axis=-1, keepdims=True)
            g = padded_ref[at, :].astype(F32)
            grad = g + inverse * (weighted - first - normed * second)
            low_ref[at, :] = grad.astype(BF)
            parts = (grad, dh * normed, dh, g)
            return tuple(s + jnp.sum(p, axis=0, keepdims=True) for s, p in zip(sums, parts, strict=True))

        zero = jnp.zeros((1, wide), F32)
        sums = lax.fori_loop(0, rows // tile, body, (zero,) * 4)
        sums_ref[...] = jnp.concatenate(sums + (jnp.zeros((4, wide), F32),), axis=0)
        here = place_ref[0]
        mine = out_ref[pl.ds(pl.multiple_of(here * group, 128), group), :]
        other = out_ref[pl.ds(pl.multiple_of(group - here * group, 128), group), :]
        sent_ref[...] = dot(low_ref[...], other, 1, 1).astype(BF)
        mine_ref[...] = dot(low_ref[...], mine, 1, 1).astype(BF)


def feed_back(here, weights, slope, cotangent, residual, gain, part):
    rows, ff = slope.shape
    _, valid, wide = cotangent.shape
    group = wide // 2
    per = ff // wide
    if part % 16:
        part = 0
        fc2, fc1, out = weights
        fc2_spec = pl.BlockSpec((wide, wide), lambda i, p: (i, 0))
        fc1_spec = pl.BlockSpec((wide, wide), lambda i, p: (0, i))
    else:
        fc2 = fc1 = out = weights
        fc2_spec = pl.BlockSpec((wide // per, ff), lambda i, p: (i, 0))
        fc1_spec = pl.BlockSpec((wide, wide), lambda i, p: (0, per + 1 + i))

    def fixed(*shape):
        return pl.BlockSpec(shape, lambda i, p: tuple(0 for _ in shape))

    block = pl.BlockSpec((rows, wide), lambda i, p: (0, i))
    return pl.pallas_call(
        functools.partial(feed_back_kernel, part),
        grid_spec=pltpu.PrefetchScalarGridSpec(
            num_scalar_prefetch=1,
            grid=(per,),
            in_specs=[
                fc2_spec, fc1_spec, pl.BlockSpec(memory_space=pl.ANY), block,
                fixed(1, valid, wide), pl.BlockSpec(memory_space=pl.ANY), fixed(1, wide),
            ],
            out_specs=[
                block, pl.BlockSpec((wide, wide), lambda i, p: (i, 0)),
                fixed(rows, wide), fixed(rows, group), fixed(rows, group),
                pl.BlockSpec((1, wide), lambda i, p: (0, i)), fixed(8, wide),
            ],
            scratch_shapes=[
                pltpu.VMEM((rows, wide), F32),
                pltpu.VMEM((rows, wide), BF),
                pltpu.VMEM((wide, wide), BF),
                pltpu.VMEM((rows, wide), F32),
                pltpu.SemaphoreType.DMA((2,)),
            ],
        ),
        out_shape=[
            jax.ShapeDtypeStruct((rows, ff), BF),
            jax.ShapeDtypeStruct((ff, wide), BF),
            jax.ShapeDtypeStruct((rows, wide), BF),
            jax.ShapeDtypeStruct((rows, group), BF),
            jax.ShapeDtypeStruct((rows, group), BF),
            jax.ShapeDtypeStruct((1, ff), F32),
            jax.ShapeDtypeStruct((8, wide), F32),
        ],
        cost_estimate=pl.CostEstimate(
            flops=4 * rows * wide * ff, bytes_accessed=ff * wide * 10, transcendentals=rows
        ),
        name="feed_back",
    )(here, fc2, fc1, out, slope, cotangent, residual, gain)


def finish_kernel(spans, place_ref, mine_ref, theirs_ref, w_ref, *refs):
    here = place_ref[0]
    group = w_ref.shape[1] // 6
    mine, theirs = mine_ref[...].astype(F32), theirs_ref[...].astype(F32)
    for j in range(3):
        part = slice(j * group, (j + 1) * group)
        at = (2 * j * group) + here * group
        w_ref[:, pl.ds(pl.multiple_of(at, 128), group)] = mine[:, part]
        at = (2 * j + 1) * group - here * group
        w_ref[:, pl.ds(pl.multiple_of(at, 128), group)] = theirs[:, part]
    rows = (mine[:, 3 * group :] + theirs[:, 3 * group :]).T
    for (start, stop), ref in zip(spans, refs, strict=True):
        ref[...] = jnp.concatenate([rows[i : i + 1] for i in range(start, stop)], axis=1)


def finish(here, mine, theirs, spans):
    part, across = mine.shape
    width = 2 * (across - 128)

    def fixed(*shape):
        return pl.BlockSpec(shape, lambda i, p: (0, 0))

    sizes = [(1, (stop - start) * part) for start, stop in spans]
    return pl.pallas_call(
        functools.partial(finish_kernel, spans),
        grid_spec=pltpu.PrefetchScalarGridSpec(
            num_scalar_prefetch=1,
            grid=(1,),
            in_specs=[fixed(part, across)] * 2,
            out_specs=[fixed(part, width)] + [fixed(*shape) for shape in sizes],
        ),
        out_shape=[jax.ShapeDtypeStruct((part, width), F32)]
        + [jax.ShapeDtypeStruct(shape, F32) for shape in sizes],
        name="finish",
    )(here, mine, theirs)


def output_kernel(
    token_ref, z_ref, w_ref, late_ref, rows_ref, out_ref, total_ref, residual_ref, sem_ref
):
    step = pl.program_id(0)
    copy = pltpu.make_async_copy(late_ref, residual_ref, sem_ref)

    @pl.when(step == 0)
    def _():
        copy.start()
        total_ref[...] = jnp.zeros_like(total_ref)

    total_ref[...] += dot(z_ref[...], w_ref[...])

    @pl.when(step == pl.num_programs(0) - 1)
    def _():
        copy.wait()
        total = total_ref[...] + residual_ref[...] + rows_ref[-1:, :]
        out_ref[0] = total[: out_ref.shape[1], :].astype(BF)


def output_end(token, activated, w, residual, bias, valid):
    rows, ff = activated.shape
    wide = w.shape[1]
    return pl.pallas_call(
        output_kernel,
        grid=(ff // wide,),
        in_specs=[
            pl.BlockSpec(memory_space=pl.ANY),
            pl.BlockSpec((rows, wide), lambda i: (0, i)),
            pl.BlockSpec((wide, wide), lambda i: (i, 0)),
            pl.BlockSpec(memory_space=pl.ANY),
            pl.BlockSpec((1, wide), lambda i: (0, 0)),
        ],
        out_specs=pl.BlockSpec((1, valid, wide), lambda i: (0, 0, 0)),
        out_shape=jax.ShapeDtypeStruct((1, valid, wide), BF),
        scratch_shapes=[
            pltpu.VMEM((rows, wide), F32),
            pltpu.VMEM((rows, wide), F32),
            pltpu.SemaphoreType.DMA,
        ],
        cost_estimate=pl.CostEstimate(
            flops=2 * rows * wide * ff, bytes_accessed=rows * ff * 4, transcendentals=0
        ),
        name="output_end",
    )(token, activated, w, residual, bias)


def join_kernel(mine_ref, theirs_ref, out_ref, first_ref):
    wide = out_ref.shape[1]
    mine, theirs = mine_ref[...].astype(F32), theirs_ref[...].astype(F32)
    out_ref[...] = mine[:, :wide] + theirs[:, :wide]
    first_ref[...] = mine[:, wide:] + theirs[:, wide:]


def join_second(mine, theirs, wide):
    part, across = mine.shape
    return pl.pallas_call(
        join_kernel,
        out_shape=[
            jax.ShapeDtypeStruct((part, wide), F32),
            jax.ShapeDtypeStruct((part, across - wide), F32),
        ],
        name="join_second",
    )(mine, theirs)


def input_end_kernel(mine_ref, got_ref, residual_ref, normed_ref, gain_ref, inverse_ref, out_ref):
    normed = normed_ref[...]
    weighted = (mine_ref[...].astype(F32) + got_ref[...].astype(F32)) * gain_ref[...]
    first = jnp.mean(weighted, axis=-1, keepdims=True)
    second = jnp.mean(weighted * normed, axis=-1, keepdims=True)
    out_ref[:, 0, :] = residual_ref[...].astype(F32) + inverse_ref[:, 0:1] * (weighted - first - normed * second)


def input_end(mine, got, residual, normed, gain, inverse, valid):
    half, wide = mine.shape
    tile = 384
    block = pl.BlockSpec((tile, wide), lambda i: (i, 0))
    return pl.pallas_call(
        input_end_kernel,
        grid=(half // tile,),
        in_specs=[
            block, block, block, block, pl.BlockSpec((1, wide), lambda i: (0, 0)),
            pl.BlockSpec((tile, 128), lambda i: (i, 0)),
        ],
        out_specs=pl.BlockSpec((tile, 1, wide), lambda i: (i, 0, 0)),
        out_shape=jax.ShapeDtypeStruct((valid, 1, wide), F32),
        cost_estimate=pl.CostEstimate(
            flops=half * wide * 10, bytes_accessed=half * wide * 18, transcendentals=0
        ),
        name="input_end",
    )(mine, got, residual, normed, gain, inverse)


def swap(x, axis, size, bit):
    return lax.ppermute(x, axis, [(i, i ^ bit) for i in range(size)])


def bits_of(size):
    top = size // 4
    return top, [1 << b for b in range(top.bit_length() - 2, -1, -1)]


def gather_blocks(x, size):
    me = lax.axis_index("dp")
    top, bits = bits_of(size)
    held = jnp.stack([x] + [swap(x, "dp", size, j * top) for j in (1, 2, 3)])
    where = [j * top for j in range(4)]
    for bit in bits:
        held = jnp.concatenate([held, swap(held, "dp", size, bit)])
        where = where + [w ^ bit for w in where]
    place = [0] * size
    for i, w in enumerate(where):
        place[w] = i
    return held, jnp.asarray(place, jnp.int32)[me ^ jnp.arange(size)]


def halve(x, axis, bit):
    mine = lax.rem(lax.axis_index("dp") // bit, 2)
    keep = lax.dynamic_index_in_dim(x, mine, axis, keepdims=False)
    give = lax.dynamic_index_in_dim(x, 1 - mine, axis, keepdims=False)
    return keep, give.astype(BF)


def scatter_split(x, size):
    top, _ = bits_of(size)
    mine = lax.axis_index("dp") // top
    gives = [
        lax.dynamic_index_in_dim(x, mine ^ j, 0, keepdims=False).astype(BF) for j in (1, 2, 3)
    ]
    return gives, lax.dynamic_index_in_dim(x, mine, 0, keepdims=False).astype(F32)


def scatter_join(total, gives, size):
    top, _ = bits_of(size)
    for j, give in zip((1, 2, 3), gives, strict=True):
        total = total + swap(give, "dp", size, j * top).astype(F32)
    return total


def after(x, *others):
    return lax.optimization_barrier((x, *others))[0]


def gelu_cdf(values):
    return 0.5 * (1.0 + lax.erf(values * (1.0 / math.sqrt(2.0))))


def layer(
    size, frames_in, ln1_gain, ln1_bias, w_qkv, b_qv, w_o, b_o,
    ln2_gain, ln2_bias, w_fc1, b_fc1, w_fc2, b_fc2, cotangent,
):
    clips, valid, wide = frames_in.shape
    assert clips == 1
    ff = w_fc1.shape[1]
    part = w_qkv.shape[0]
    group = wide // 2
    half = -(-valid // 256) * 256
    here = lax.axis_index("seq")

    def other(x):
        return swap(x, "seq", 2, 1)

    def pick(x, axis, index):
        return lax.dynamic_index_in_dim(x, index, axis, keepdims=False)

    per = ff // wide
    me = lax.axis_index("dp")
    _, bits = bits_of(size)

    vectors = jnp.concatenate([ln1_gain, ln1_bias, b_qv, b_o, ln2_gain, ln2_bias, b_fc1, b_fc2])
    count = vectors.shape[0] // part
    columns = lax.optimization_barrier(
        jnp.pad(vectors.reshape(count, part).T, ((0, 0), (0, 128 - count)))
    )
    w_mine = [
        lax.dynamic_slice_in_dim(w_qkv, j * wide + here * group, group, axis=1) for j in range(3)
    ]
    held, place = gather_blocks(jnp.concatenate(w_mine + [columns], axis=1), size)
    if part % 16:
        held = jnp.take(held, place, axis=0, mode="clip").reshape(1, wide, 3 * group + 128)
        place = jnp.zeros((1,), jnp.int32)
    place = jnp.concatenate([place, jnp.full((1,), here, jnp.int32)])
    if part % 16:
        fc2_local = w_fc2.reshape(per, part, wide).transpose(1, 0, 2).reshape(part, ff)
        packed = jnp.concatenate([fc2_local, w_o, w_fc1], axis=1)
    else:
        packed = pack(w_fc2, w_o, w_fc1)
    later = lax.all_gather(packed, "dp", axis=0, tiled=True)
    out_full, fc1_full = later[:, ff : ff + wide], later[:, ff + wide :]
    weights = later
    if part % 16:
        fc2_full = later[:, :ff].reshape(size, part, per, wide)
        weights = (fc2_full.transpose(0, 2, 1, 3).reshape(ff, wide), fc1_full, out_full)

    prepared = prepare(frames_in, half, 0)
    inverse_one = prepared[2]
    normed_both, normed_t, _ = prepare(other(frames_in), half, 1, prepared[:2])
    qkv, w_full, w_flipped, table, scale = projection(held, place, normed_both, part)

    def vector(start, stop):
        return table[start:stop].reshape(-1, size, part).transpose(1, 0, 2).reshape(-1)

    gain_one, gain_two = table[0], table[5]
    bias_fc1, bias_fc2 = vector(7, 7 + per), table[7 + per]
    o_mine, o_sent, lse = attention_forward(qkv, half, valid)
    o_got = other(o_sent)
    flag = jnp.full((1,), here, jnp.int32)
    if part % 16:
        residual, hidden_two = attend(flag, frames_in, o_mine, o_got, out_full, 0, table)
    else:
        residual, hidden_two = attend(flag, frames_in, o_mine, o_got, later, per, table)

    pre_act = dot(hidden_two, fc1_full) + bias_fc1
    cdf = gelu_cdf(pre_act)
    density = jnp.exp(-0.5 * pre_act * pre_act) * (1.0 / math.sqrt(2.0 * math.pi))
    activated, slope = lax.optimization_barrier(
        ((pre_act * cdf).astype(BF), (cdf + pre_act * density).astype(BF))
    )
    (
        grad_pre_low, fc2_full, grad_residual_low,
        do_mine, do_sent, grad_bias_fc1, grad_sums,
    ) = feed_back(flag, weights, slope, cotangent, residual, gain_two[None], part)
    do_got = other(do_sent)
    parity = jnp.full((1,), lax.rem(me, 2), jnp.int32)
    fc2_keep, fc2_give = third_gradient(parity, activated, cotangent, size, do_sent)
    second_part = second_gradient(
        flag, fc2_give, o_mine, o_got, grad_residual_low, hidden_two, grad_pre_low
    )
    grad_second = lax.psum_scatter(second_part, "dp", scatter_dimension=0, tiled=True)

    def backward(token, start, count):
        return attention_backward(
            qkv, o_mine, o_sent, do_mine, do_got, lse, token, half, valid, start, count
        )

    x = fc2_keep.astype(F32) + swap(fc2_give, "dp", size, 1).astype(F32)
    x = x.reshape(size // 2, 2, -1, wide)
    keep, give = pick(x, 1, here).astype(BF), pick(x, 1, 1 - here).astype(BF)
    got = other(give)
    ds = [backward(give, 0, group // 128)]
    grad_other = projection_input_gradient(w_flipped, ds, ds[0], half, 1, BF)
    grad_got = other(grad_other)
    for at in range(len(bits) - 2, -1, -1):
        x = after(keep, grad_other).astype(F32) + got.astype(F32)
        keep, give = halve(x.reshape(-1, 2, *x.shape[1:]), 1, bits[at])
        keep, got = keep.astype(BF), swap(give, "dp", size, bits[at])
    fc2_keep_x, fc2_got_x = keep, got

    vectors = [(7, grad_bias_fc1)]
    if part % 16:
        grad_qkv, norm_sums, sums = projection_weight_gradient(normed_t, w_full, scale, ds)
        grad_bias_mine = jnp.stack([sums[0, :group], sums[0, 2 * group :]])
        zero = jnp.zeros_like(grad_bias_mine)
        grad_bias_qv = jnp.where(
            here == 0,
            jnp.concatenate([grad_bias_mine, zero], axis=1),
            jnp.concatenate([zero, grad_bias_mine], axis=1),
        )

        def as_columns(start, v):
            v = v.reshape(size, -1, part).transpose(0, 2, 1)
            return jnp.pad(v, ((0, 0), (0, 0), (start, 128 - start - v.shape[2])))

        columns = norm_sums.reshape(size, part, 128) + as_columns(2, grad_bias_qv)
        vectors += [(p, grad_sums[i]) for i, p in enumerate((4, 5, 6, 7 + per))]
        columns = columns + sum(as_columns(start, v) for start, v in vectors)
        x = jnp.concatenate([grad_qkv.reshape(size, part, -1), columns.astype(BF)], axis=2)
        keep, give = halve(x.reshape(size // 2, 2, *x.shape[1:]), 1, 1)
    else:
        sides = jnp.concatenate([parity, jnp.full((1,), here, jnp.int32)])
        keep, give = spread_weight_gradient(
            sides, give, normed_t, w_full, scale, ds, grad_bias_fc1, grad_sums, part
        )
    got = swap(give, "dp", size, 1)
    for at in range(len(bits) - 2, -1, -1):
        x = keep.astype(F32) + got.astype(F32)
        keep, give = halve(x.reshape(-1, 2, *x.shape[1:]), 1, bits[at])
        got = swap(give, "dp", size, bits[at])
    fc2_keep, fc2_got = after((fc2_keep_x, fc2_got_x), give)
    fc2_gives, fc2_stay = scatter_split(fc2_keep.astype(F32) + fc2_got.astype(F32), size)
    grad_mine = projection_input_gradient(w_flipped, ds, fc2_gives[2], half, 0, BF)
    frames_out = output_end(
        fc2_gives[2], activated, fc2_full, residual, bias_fc2[None], valid
    )
    fc2_part = scatter_join(fc2_stay, fc2_gives, size).astype(BF)
    gives, stay = scatter_split(keep.astype(F32) + got.astype(F32), size)
    grad_input = input_end(
        grad_mine, grad_got, grad_residual_low, normed_both, gain_one[None], inverse_one, valid
    ).transpose(1, 0, 2)
    mine = scatter_join(stay, gives, size).astype(BF)
    theirs = other(mine)
    spans = ((0, 1), (1, 2), (2, 4), (4, 5), (5, 6), (6, 7), (7, 7 + per), (7 + per, 8 + per))
    grad_w_qkv, *small = finish(flag, mine, theirs, spans)
    small = [v[0] for v in small]
    fc2_got = other(fc2_part)
    fc2_sum = jnp.where(
        here == 0,
        jnp.concatenate([fc2_part, fc2_got], axis=0),
        jnp.concatenate([fc2_got, fc2_part], axis=0),
    ).astype(F32)
    out_sum, first_sum = join_second(grad_second, other(grad_second), wide)
    return (
        frames_out, grad_input, small[0], small[1], grad_w_qkv, small[2], out_sum, small[3],
        small[4], small[5], first_sum, small[6], fc2_sum, small[7],
    )


def solution(mesh):
    frames, rows, vector = P("dp", "seq", None), P("dp", None), P("dp")
    in_specs = (
        frames, vector, vector, rows, vector, rows, vector,
        vector, vector, rows, vector, rows, vector, frames,
    )
    out_specs = (
        frames, frames, vector, vector, rows, vector, rows, vector,
        vector, vector, rows, vector, rows, vector,
    )
    return jax.shard_map(
        functools.partial(layer, mesh.shape["dp"]),
        mesh=mesh, in_specs=in_specs, out_specs=out_specs, check_vma=False,
    )
```

```python
import functools
import math

import jax
import jax.numpy as jnp
from jax import lax
from jax.experimental import pallas as pl
from jax.experimental.pallas import tpu as pltpu
from jax.sharding import PartitionSpec as P


EPSILON = 1e-05
BF = jnp.bfloat16
F32 = jnp.float32
MASKED = -1e30


def dot(a, b, ca=1, cb=0):
    return lax.dot_general(a, b, (((ca,), (cb,)), ((), ())), preferred_element_type=F32)


def split3(x):
    high = x.astype(BF).astype(F32)
    rest = x - high
    mid = rest.astype(BF).astype(F32)
    return high, mid, (rest - mid).astype(BF).astype(F32)


def forward_kernel(half, valid, q_ref, k_ref, v_ref, mine_ref, sent_ref, lse_ref, kx_ref, vt_ref):
    rows = k_ref.shape[0]
    wide = q_ref.shape[0]

    kx_ref[:, :128] = k_ref[...]
    row = lax.broadcasted_iota(jnp.int32, (rows, 128), 0)
    lane = lax.broadcasted_iota(jnp.int32, (rows, 128), 1)
    padded = (lax.rem(row, half) >= valid) & (lane == 0)
    kx_ref[:, 128:] = jnp.where(padded, MASKED, 0.0).astype(BF)
    vt = v_ref[...].T
    vt_ref[0:64, :] = vt[0:64, :]
    vt_ref[64:80, :] = jnp.ones((16, rows), BF)
    vt_ref[80:144, :] = vt[64:128, :]
    vt_ref[144:160, :] = jnp.ones((16, rows), BF)

    lane = lax.broadcasted_iota(jnp.int32, (wide, 128), 1)
    q = q_ref[...] * jnp.asarray(0.125, BF)
    one = jnp.where(lane == 0, 1.0, 0.0).astype(BF)
    outs, sums = [], []
    for h in range(2):
        mine = (lane < 64) if h == 0 else (lane >= 64)
        qx = jnp.concatenate([jnp.where(mine, q, jnp.zeros_like(q)), one], axis=1)
        s = dot(kx_ref[...], qx, 1, 1)
        peak = jnp.max(s, axis=0, keepdims=True)
        p = jnp.exp(s - peak).astype(BF)
        o = dot(vt_ref[80 * h : 80 * h + 80, :], p)
        total = o[64:65, :]
        outs.append(o[0:64, :] / total)
        sums.append(peak + jnp.log(total))
    o = jnp.concatenate(outs, axis=0).T.astype(BF)
    mine_ref[...] = o[:half]
    sent_ref[...] = o[half:]
    lse_ref[...] = jnp.concatenate(sums + [jnp.zeros((6, wide), F32)], axis=0)[None]


def attention_forward(qkv, half, valid):
    rows, width = qkv.shape
    pairs = width // 3 // 128
    block = pl.BlockSpec((half, 128), lambda p: (0, p))
    return pl.pallas_call(
        functools.partial(forward_kernel, half, valid),
        grid=(pairs,),
        in_specs=[
            pl.BlockSpec((rows, 128), lambda p: (0, p)),
            pl.BlockSpec((rows, 128), lambda p: (0, pairs + p)),
            pl.BlockSpec((rows, 128), lambda p: (0, 2 * pairs + p)),
        ],
        out_specs=[block, block, pl.BlockSpec((1, 8, rows), lambda p: (p, 0, 0))],
        out_shape=[
            jax.ShapeDtypeStruct((half, pairs * 128), BF),
            jax.ShapeDtypeStruct((half, pairs * 128), BF),
            jax.ShapeDtypeStruct((pairs, 8, rows), F32),
        ],
        scratch_shapes=[pltpu.VMEM((rows, 256), BF), pltpu.VMEM((160, rows), BF)],
        cost_estimate=pl.CostEstimate(
            flops=pairs * 2 * 4 * rows * rows * 256,
            bytes_accessed=rows * width * 2 + rows * width,
            transcendentals=pairs * 2 * rows * rows,
        ),
        name="attention_forward",
    )(qkv, qkv, qkv)


def backward_kernel(
    half, valid, q_ref, k_ref, v_ref, o_mine_ref, o_sent_ref, mine_ref, got_ref, lse_ref, token_ref,
    d_ref, kt_ref, vt_ref, dkt_ref, dvt_ref,
):
    rows = k_ref.shape[0]
    step = pl.program_id(1)

    @pl.when(step == 0)
    def _():
        kt_ref[0:128, :] = k_ref[...].T
        vt_ref[0:128, :] = v_ref[...].T
        row = lax.broadcasted_iota(jnp.int32, (128, rows), 0)
        key = lax.broadcasted_iota(jnp.int32, (128, rows), 1)
        bias = jnp.where(lax.rem(key, half) >= valid, MASKED, 0.0)
        ones = jnp.where((row >= 1) & (row < 4), 1.0, 0.0)
        kt_ref[128:256, :] = jnp.where(row == 0, bias, ones).astype(BF)
        vt_ref[128:256, :] = ones.astype(BF)
        dkt_ref[...] = jnp.zeros_like(dkt_ref)
        dvt_ref[...] = jnp.zeros_like(dvt_ref)

    tile = q_ref.shape[0]
    first = step < half // tile
    lane = lax.broadcasted_iota(jnp.int32, (tile, 128), 1)
    q = q_ref[...] * jnp.asarray(0.125, BF)
    do = jnp.where(first, mine_ref[...], got_ref[...])
    o = jnp.where(first, o_mine_ref[...], o_sent_ref[...])
    product = do.astype(F32) * o.astype(F32)
    lse = lse_ref[0].T
    qt, dot_t = q.T, do.T

    def extra(x, first):
        a, b, c = split3(-x)
        tail = jnp.where(lane == 2, b, jnp.where(lane == 3, c, 0.0))
        return jnp.where(lane == 0, first, jnp.where(lane == 1, a, tail)).astype(BF)

    def scores(h, at):
        return dot(left[h][0], kt_ref[:, at]), dot(left[h][1], vt_ref[:, at])

    left = []
    for h in range(2):
        mine = (lane < 64) if h == 0 else (lane >= 64)
        delta = jnp.sum(jnp.where(mine, product, 0.0), axis=1, keepdims=True)
        qx = jnp.concatenate(
            [jnp.where(mine, q, jnp.zeros_like(q)), extra(lse[:, h : h + 1], 1.0)], axis=1
        )
        dx = jnp.concatenate([jnp.where(mine, do, jnp.zeros_like(do)), extra(delta, 0.0)], axis=1)
        left.append((qx, dx))
    work = [(h, slice(k, k + 512)) for h in range(2) for k in range(0, rows, 512)]
    dq = [jnp.zeros((tile, 128), F32)] * 2
    ahead = scores(*work[0])
    for i, (h, at) in enumerate(work):
        s, dp = ahead
        if i + 1 < len(work):
            ahead = scores(*work[i + 1])
        p = jnp.exp(s)
        low = p.astype(BF)
        ds = (p * dp).astype(BF)
        dq[h] = dq[h] + dot(ds, k_ref[at, :])
        part = slice(64 * h, 64 * h + 64)
        dkt_ref[part, at] += dot(qt[part, :], ds)
        dvt_ref[part, at] += dot(dot_t[part, :], low)
    dq = (jnp.where(lane < 64, dq[0], dq[1]) * 0.125).astype(BF)
    d_ref[0, pl.ds(pl.multiple_of(step * tile, 128), tile), :] = dq

    @pl.when(step == pl.num_programs(1) - 1)
    def _():
        d_ref[1] = dkt_ref[...].T.astype(BF)
        d_ref[2] = dvt_ref[...].T.astype(BF)


def attention_backward(qkv, o_mine, o_sent, do_mine, do_got, lse, token, half, valid, start, count):
    rows, width = qkv.shape
    pairs = width // 3 // 128

    def whole(part):
        return pl.BlockSpec((rows, 128), lambda p, i: (0, part * pairs + start + p))

    tile = 384
    per_half = half // tile
    block = pl.BlockSpec((tile, 128), lambda p, i: (i, start + p))
    fixed = pl.BlockSpec((tile, 128), lambda p, i: (lax.rem(i, per_half), start + p))
    return pl.pallas_call(
        functools.partial(backward_kernel, half, valid),
        grid=(count, 2 * per_half),
        in_specs=[
            block, whole(1), whole(2), fixed, fixed, fixed, fixed,
            pl.BlockSpec((1, 8, tile), lambda p, i: (start + p, 0, i)),
            pl.BlockSpec(memory_space=pl.ANY),
        ],
        out_specs=pl.BlockSpec((3, rows, 128), lambda p, i: (0, 0, p)),
        out_shape=jax.ShapeDtypeStruct((3, rows, count * 128), BF),
        scratch_shapes=[
            pltpu.VMEM((256, rows), BF),
            pltpu.VMEM((256, rows), BF),
            pltpu.VMEM((128, rows), F32),
            pltpu.VMEM((128, rows), F32),
        ],
        cost_estimate=pl.CostEstimate(
            flops=count * 2 * 8 * rows * rows * 256,
            bytes_accessed=count * rows * 128 * 16,
            transcendentals=count * 2 * rows * rows,
        ),
        name="attention_backward",
    )(qkv, qkv, qkv, o_mine, o_sent, do_mine, do_got, lse, token)


def rows_below(x, start, valid):
    row = start + lax.broadcasted_iota(jnp.int32, x.shape, 0)
    return jnp.where(row < valid, x, jnp.zeros_like(x))


def prepare_kernel(valid, x_ref, *refs):
    normed_ref, flipped_ref, inverse_ref = refs[-3:]
    tile, wide = normed_ref.shape
    x = rows_below(x_ref[0].astype(F32), pl.program_id(0) * tile, valid)
    centered = x - jnp.mean(x, axis=-1, keepdims=True)
    inverse = lax.rsqrt(jnp.mean(centered * centered, axis=-1, keepdims=True) + EPSILON)
    normed = centered * inverse
    normed_ref[...] = normed
    inverse_ref[...] = jnp.broadcast_to(inverse, inverse_ref.shape)
    flipped_ref[:wide, :] = normed.T.astype(BF)
    flipped_ref[wide:, :] = jnp.ones((16, tile), BF)


def prepare(frames, half, block, filled=()):
    _, valid, wide = frames.shape
    tile = 384
    first = block * (half // tile)
    return pl.pallas_call(
        functools.partial(prepare_kernel, valid),
        grid=(half // tile,),
        in_specs=[pl.BlockSpec((1, tile, wide), lambda i: (0, i, 0))]
        + [pl.BlockSpec(memory_space=pl.ANY)] * len(filled),
        out_specs=[
            pl.BlockSpec((tile, wide), lambda i: (first + i, 0)),
            pl.BlockSpec((wide + 16, tile), lambda i: (0, first + i)),
            pl.BlockSpec((tile, 128), lambda i: (i, 0)),
        ],
        out_shape=[
            jax.ShapeDtypeStruct((2 * half, wide), F32),
            jax.ShapeDtypeStruct((wide + 16, 2 * half), BF),
            jax.ShapeDtypeStruct((half, 128), F32),
        ],
        input_output_aliases={1: 0, 2: 1} if filled else {},
        cost_estimate=pl.CostEstimate(
            flops=half * wide * 16, bytes_accessed=half * wide * 8, transcendentals=half
        ),
        name="prepare",
    )(frames, *filled)


def attend_kernel(valid, place_ref, x_ref, mine_ref, got_ref, w_ref, rows_ref, sum_ref, h_ref):
    tile = sum_ref.shape[0]
    group = mine_ref.shape[1]
    here = place_ref[0]
    first = w_ref[pl.ds(pl.multiple_of(here * group, 128), group), :]
    other = w_ref[pl.ds(pl.multiple_of(group - here * group, 128), group), :]
    total = dot(mine_ref[...], first) + dot(got_ref[...], other)
    x = rows_below(x_ref[0].astype(F32), pl.program_id(0) * tile, valid)
    total = x + total + rows_ref[4:5, :]
    sum_ref[...] = total
    centered = total - jnp.mean(total, axis=-1, keepdims=True)
    inverse = lax.rsqrt(jnp.mean(centered * centered, axis=-1, keepdims=True) + EPSILON)
    h_ref[...] = (centered * inverse * rows_ref[5:6, :] + rows_ref[6:7, :]).astype(BF)


def attend(here, frames, mine, got, w, column, table):
    _, valid, wide = frames.shape
    half, group = mine.shape
    tile = 256
    block = pl.BlockSpec((tile, group), lambda i, p: (i, 0))
    out = pl.BlockSpec((tile, wide), lambda i, p: (i, 0))
    return pl.pallas_call(
        functools.partial(attend_kernel, valid),
        grid_spec=pltpu.PrefetchScalarGridSpec(
            num_scalar_prefetch=1,
            grid=(half // tile,),
            in_specs=[
                pl.BlockSpec((1, tile, wide), lambda i, p: (0, i, 0)), block, block,
                pl.BlockSpec((wide, wide), lambda i, p: (0, column)),
                pl.BlockSpec((16, wide), lambda i, p: (0, 0)),
            ],
            out_specs=[out, out],
        ),
        out_shape=[
            jax.ShapeDtypeStruct((half, wide), F32),
            jax.ShapeDtypeStruct((half, wide), BF),
        ],
        cost_estimate=pl.CostEstimate(
            flops=4 * half * wide * group, bytes_accessed=half * wide * 10, transcendentals=half
        ),
        name="attend",
    )(here, frames, mine, got, w, table)


def projection_kernel(
    part, group, place_ref, held_ref, x_ref, qkv_ref, w_ref, wt_ref, rows_ref, scale_ref,
    gain_ref, bias_ref, columns_ref,
):
    wide, width = w_ref.shape

    @pl.when(pl.program_id(0) == 0)
    def _():
        blocks, extent, _ = held_ref.shape
        for d in range(blocks):
            block = held_ref[place_ref[d]]
            w_ref[d * extent : (d + 1) * extent, :] = block[:, :width]
            columns_ref[d * extent : (d + 1) * extent, :] = block[:, width:].astype(F32)
        wt_ref[...] = w_ref[...].T
        table = columns_ref[...].T[:16, :]
        rows_ref[...] = table
        scale_ref[:, :128] = jnp.broadcast_to(columns_ref[:, 0:1], (wide, 128))
        scale_ref[:, 128:] = jnp.broadcast_to(columns_ref[:, 1:2], (wide, 128))
        gain_ref[...] = table[:8]
        here = place_ref[blocks]
        few = group // 2
        row = lax.broadcasted_iota(jnp.int32, (few, group), 0)
        entry = lax.broadcasted_iota(jnp.int32, (few, group), 1)
        base = row + part * (row // part)
        for v in range(2):
            at = pl.multiple_of(v * (wide // 2) + here * few, 64)
            low = columns_ref[pl.ds(at, few), :].T[:16].astype(BF)
            total = jnp.zeros((16, group), F32)
            for j in range(2):
                chosen = entry == base + part * j
                picked = dot(low, jnp.where(chosen, 1.0, 0.0).astype(BF))
                total = total + picked[2 + j : 3 + j, :]
            bias_ref[:, 2 * v * group : (2 * v + 1) * group] = total[:8]
        bias_ref[:, group : 2 * group] = jnp.zeros((8, group), F32)

    h = (x_ref[...] * gain_ref[0:1, :] + gain_ref[1:2, :]).astype(BF)
    qkv_ref[...] = (dot(h, w_ref[...]) + bias_ref[0:1, :]).astype(BF)


def projection(held, place, normed, part):
    blocks, extent, across = held.shape
    width = across - 128
    rows, wide = normed.shape
    tile = 384

    def fixed(*shape):
        return pl.BlockSpec(shape, lambda i, p: tuple(0 for _ in shape))

    return pl.pallas_call(
        functools.partial(projection_kernel, part, width // 3),
        grid_spec=pltpu.PrefetchScalarGridSpec(
            num_scalar_prefetch=1,
            grid=(rows // tile,),
            in_specs=[fixed(blocks, extent, across), pl.BlockSpec((tile, wide), lambda i, p: (i, 0))],
            out_specs=[
                pl.BlockSpec((tile, width), lambda i, p: (i, 0)),
                fixed(wide, width), fixed(width, wide), fixed(16, wide), fixed(wide, 256),
            ],
            scratch_shapes=[
                pltpu.VMEM((8, wide), F32),
                pltpu.VMEM((8, width), F32),
                pltpu.VMEM((wide, 128), F32),
            ],
        ),
        out_shape=[
            jax.ShapeDtypeStruct((rows, width), BF),
            jax.ShapeDtypeStruct((wide, width), BF),
            jax.ShapeDtypeStruct((width, wide), BF),
            jax.ShapeDtypeStruct((16, wide), F32),
            jax.ShapeDtypeStruct((wide, 256), F32),
        ],
        cost_estimate=pl.CostEstimate(
            flops=2 * rows * wide * width, bytes_accessed=rows * wide * 8, transcendentals=0
        ),
        name="projection",
    )(place, held, normed)


def weight_kernel(pieces, xt_ref, w_ref, scale_ref, *refs):
    d_refs, (g_ref, c_ref, s_ref) = refs[:pieces], refs[pieces:]
    d = jnp.concatenate([r[0] for r in d_refs], axis=1)
    m = dot(xt_ref[...], d)
    s = m[w_ref.shape[0] :][:8]
    m = m[: w_ref.shape[0]]
    s_ref[...] = s
    gain, shift = scale_ref[:, 0:1], scale_ref[:, 128:129]
    total = s[0:1, :]
    g_ref[...] = (gain * m + shift * total).astype(BF)
    w = w_ref[...].astype(F32)
    lane = lax.broadcasted_iota(jnp.int32, c_ref.shape, 1)
    first = jnp.sum(w * m, axis=1, keepdims=True)
    second = jnp.sum(w * total, axis=1, keepdims=True)
    now = jnp.where(lane == 0, first, jnp.where(lane == 1, second, 0.0))
    before = jnp.where(pl.program_id(0) == 0, jnp.zeros_like(now), c_ref[...])
    c_ref[...] = before + now


def projection_weight_gradient(xt, w, scale, ds):
    tall, rows = xt.shape
    wide = w.shape[0]
    group = sum(d.shape[2] for d in ds)
    return pl.pallas_call(
        functools.partial(weight_kernel, len(ds)),
        grid=(3,),
        in_specs=[
            pl.BlockSpec((tall, rows), lambda j: (0, 0)),
            pl.BlockSpec((wide, group), lambda j: (0, j)),
            pl.BlockSpec((wide, 256), lambda j: (0, 0)),
        ]
        + [pl.BlockSpec((1, *d.shape[1:]), lambda j: (j, 0, 0)) for d in ds],
        out_specs=[
            pl.BlockSpec((wide, group), lambda j: (0, j)),
            pl.BlockSpec((wide, 128), lambda j: (0, 0)),
            pl.BlockSpec((8, group), lambda j: (0, j)),
        ],
        out_shape=[
            jax.ShapeDtypeStruct((wide, 3 * group), BF),
            jax.ShapeDtypeStruct((wide, 128), F32),
            jax.ShapeDtypeStruct((8, 3 * group), F32),
        ],
        cost_estimate=pl.CostEstimate(
            flops=2 * rows * wide * 3 * group, bytes_accessed=rows * wide * 4, transcendentals=0
        ),
        name="projection_weight_gradient",
    )(xt, w, scale, *ds)


def spread_kernel(
    part, pieces, per, place_ref, token_ref, xt_ref, w_ref, scale_ref, *refs
):
    d_refs, refs = refs[:pieces], refs[pieces:]
    b_ref, v_ref, keep_ref, give_ref, c_ref, s_ref, first_ref, second_ref = refs
    step = pl.program_id(0)
    wide, group = w_ref.shape
    d = jnp.concatenate([r[0] for r in d_refs], axis=1)
    m = dot(xt_ref[...], d)
    s = m[wide : wide + 8]
    s_ref[step] = s

    @pl.when(step == 0)
    def _():
        first_ref[...] = jnp.zeros_like(first_ref)
        second_ref[...] = jnp.zeros_like(second_ref)

    gain, shift = scale_ref[:, :128], scale_ref[:, 128:]
    one, two, gs = first_ref[...], second_ref[...], []
    for i in range(group // 128):
        columns = slice(128 * i, 128 * (i + 1))
        piece, w, total = m[:wide, columns], w_ref[:, columns].astype(F32), s[0:1, columns]
        one, two = one + w * piece, two + w * total
        gs.append((gain * piece + shift * total).astype(BF))
    first_ref[...], second_ref[...] = one, two
    at = pl.ds(pl.multiple_of(step * group, 128), group)
    spread_store(part, place_ref, keep_ref, give_ref, jnp.concatenate(gs, axis=1), at)

    @pl.when(step == 2)
    def _():
        lane = lax.broadcasted_iota(jnp.int32, c_ref.shape, 1)
        second = jnp.sum(second_ref[...], axis=1, keepdims=True)
        first = jnp.sum(first_ref[...], axis=1, keepdims=True)
        columns = jnp.where(lane == 0, first, jnp.where(lane == 1, second, 0.0))
        small = v_ref[...].T
        for i, name in enumerate((4, 5, 6, 7 + per)):
            columns = jnp.where(lane == name, small[:, i : i + 1], columns)
        v = jnp.broadcast_to(b_ref[...], (8, b_ref.shape[1])).T[:, 0:1]
        for j in range(per):
            column = jnp.concatenate(
                [v[(d * per + j) * part :][:part] for d in range(wide // part)], axis=0
            )
            columns = jnp.where(lane == 7 + j, column, columns)
        c_ref[...] = columns
        half = group // 2
        low = lane[:half]
        for side in (0, 2):
            v = s_ref[side].T[:, 0:1]
            at = pl.ds(pl.multiple_of(place_ref[1] * half + side * wide // 4, 64), half)
            block = c_ref[at, :]
            for j in range(2):
                column = jnp.concatenate(
                    [v[(2 * d + j) * part :][:part] for d in range(half // part)], axis=0
                )
                block = jnp.where(low == 2 + j, column, block)
            c_ref[at, :] = block
        g = c_ref[...].astype(BF)
        spread_store(part, place_ref, keep_ref, give_ref, g, pl.ds(3 * group, 128))


def spread_store(part, place_ref, keep_ref, give_ref, value, columns):
    value = value.reshape(keep_ref.shape[0], 2, part, value.shape[1])
    even, odd = value[:, 0], value[:, 1]
    low = place_ref[0] == 0
    keep_ref[:, :, columns] = jnp.where(low, even, odd)
    give_ref[:, :, columns] = jnp.where(low, odd, even)


def spread_weight_gradient(place, token, xt, w, scale, ds, bias, sums, part):
    _, rows = xt.shape
    wide = w.shape[0]
    group = sum(d.shape[2] for d in ds)
    size = wide // part
    out = pl.BlockSpec((size // 2, part, 3 * group + 128), lambda j, p: (0, 0, 0))

    def fixed(x):
        return pl.BlockSpec(x.shape, lambda j, p: (0, 0))

    return pl.pallas_call(
        functools.partial(spread_kernel, part, len(ds), bias.shape[1] // wide),
        grid_spec=pltpu.PrefetchScalarGridSpec(
            num_scalar_prefetch=1,
            grid=(3,),
            in_specs=[
                pl.BlockSpec(memory_space=pl.ANY),
                fixed(xt),
                pl.BlockSpec((wide, group), lambda j, p: (0, j)),
                fixed(scale),
            ]
            + [pl.BlockSpec((1, *d.shape[1:]), lambda j, p: (j, 0, 0)) for d in ds]
            + [fixed(bias), fixed(sums)],
            out_specs=[out, out],
            scratch_shapes=[
                pltpu.VMEM((wide, 128), F32),
                pltpu.VMEM((3, 8, group), F32),
                pltpu.VMEM((wide, 128), F32),
                pltpu.VMEM((wide, 128), F32),
            ],
        ),
        out_shape=[jax.ShapeDtypeStruct((size // 2, part, 3 * group + 128), BF)] * 2,
        cost_estimate=pl.CostEstimate(
            flops=2 * rows * wide * 3 * group, bytes_accessed=rows * wide * 4, transcendentals=0
        ),
        name="spread_weight_gradient",
    )(place, token, xt, w, scale, *ds, bias, sums)


def input_kernel(pieces, token_ref, wt_ref, *refs):
    d_refs, out_ref = refs[:pieces], refs[pieces]
    d = jnp.concatenate([r[j] for j in range(3) for r in d_refs], axis=1)
    out_ref[...] = dot(d, wt_ref[...]).astype(out_ref.dtype)


def projection_input_gradient(wt, ds, token, half, block, kind):
    wide = wt.shape[1]
    tile = 384
    start = block * (half // tile)
    return pl.pallas_call(
        functools.partial(input_kernel, len(ds)),
        grid=(half // tile,),
        in_specs=[pl.BlockSpec(memory_space=pl.ANY), pl.BlockSpec(wt.shape, lambda i: (0, 0))]
        + [pl.BlockSpec((3, tile, d.shape[2]), lambda i: (0, start + i, 0)) for d in ds],
        out_specs=pl.BlockSpec((tile, wide), lambda i: (i, 0)),
        out_shape=jax.ShapeDtypeStruct((half, wide), kind),
        cost_estimate=pl.CostEstimate(
            flops=2 * half * wt.size, bytes_accessed=half * wt.shape[0] * 4, transcendentals=0
        ),
        name="projection_input_gradient",
    )(token, wt, *ds)


def second_kernel(place_ref, token_ref, mine_ref, got_ref, drb_ref, h_ref, du_ref, out_ref, ht_ref):
    group = mine_ref.shape[1]
    step = pl.program_id(0)

    @pl.when(step == 0)
    def _():
        ht_ref[...] = h_ref[...].T
        here = place_ref[0]
        first = pl.multiple_of(here * group, 128)
        other = pl.multiple_of(group - here * group, 128)
        out_ref[pl.ds(first, group), :] = dot(mine_ref[...], drb_ref[...], 0, 0).astype(BF)
        out_ref[pl.ds(other, group), :] = dot(got_ref[...], drb_ref[...], 0, 0).astype(BF)

    @pl.when(step > 0)
    def _():
        out_ref[...] = dot(ht_ref[...], du_ref[...]).astype(BF)


def second_gradient(here, token, o_mine, o_got, drb, hidden, du):
    rows, wide = hidden.shape
    ff = du.shape[1]

    def fixed(x):
        return pl.BlockSpec(x.shape, lambda i, p: (0, 0))

    return pl.pallas_call(
        second_kernel,
        grid_spec=pltpu.PrefetchScalarGridSpec(
            num_scalar_prefetch=1,
            grid=(1 + ff // wide,),
            in_specs=[
                pl.BlockSpec(memory_space=pl.ANY), fixed(o_mine), fixed(o_got), fixed(drb), fixed(hidden),
                pl.BlockSpec((rows, wide), lambda i, p: (0, jnp.maximum(i - 1, 0))),
            ],
            out_specs=pl.BlockSpec((wide, wide), lambda i, p: (0, i)),
            scratch_shapes=[pltpu.VMEM((wide, rows), BF)],
        ),
        out_shape=jax.ShapeDtypeStruct((wide, wide + ff), BF),
        cost_estimate=pl.CostEstimate(
            flops=2 * rows * wide * (wide + ff), bytes_accessed=rows * ff * 4, transcendentals=0
        ),
        name="second_gradient",
    )(here, token, o_mine, o_got, drb, hidden, du)


def pack_kernel(fc2_ref, out_ref, fc1_ref, packed_ref):
    part, wide = out_ref.shape
    per = fc2_ref.shape[0] // part
    for j in range(per):
        packed_ref[:, j * wide : (j + 1) * wide] = fc2_ref[j * part : (j + 1) * part, :]
    packed_ref[:, per * wide : (per + 1) * wide] = out_ref[...]
    packed_ref[:, (per + 1) * wide :] = fc1_ref[...]


def pack(w_fc2, w_o, w_fc1):
    part, wide = w_o.shape
    across = wide + 2 * w_fc1.shape[1]
    return pl.pallas_call(
        pack_kernel, out_shape=jax.ShapeDtypeStruct((part, across), BF), name="pack"
    )(w_fc2, w_o, w_fc1)


def fill_rows(ref, x):
    valid = x.shape[0]
    start = valid // 16 * 16
    ref[start:, :] = jnp.zeros((ref.shape[0] - start, ref.shape[1]), ref.dtype)
    ref[:valid, :] = x


def third_kernel(place_ref, z_ref, cot_ref, token_ref, keep_ref, give_ref, padded_ref):
    @pl.when(pl.program_id(0) == 0)
    def _():
        fill_rows(padded_ref, cot_ref[0])

    value = dot(z_ref[...], padded_ref[...], 0, 0).astype(BF)
    owners, extent, wide = keep_ref.shape
    value = value.reshape(owners, 2, extent, wide)

    @pl.when(place_ref[0] == 0)
    def _():
        keep_ref[...] = value[:, 0]
        give_ref[...] = value[:, 1]

    @pl.when(place_ref[0] == 1)
    def _():
        keep_ref[...] = value[:, 1]
        give_ref[...] = value[:, 0]


def third_gradient(parity, activated, cotangent, size, token):
    _, valid, wide = cotangent.shape
    rows, ff = activated.shape
    extent = ff // size
    owners = wide // extent // 2
    out = pl.BlockSpec((owners, extent, wide), lambda i, p: (i, 0, 0))
    return pl.pallas_call(
        third_kernel,
        grid_spec=pltpu.PrefetchScalarGridSpec(
            num_scalar_prefetch=1,
            grid=(ff // wide,),
            in_specs=[
                pl.BlockSpec((rows, wide), lambda i, p: (0, i)),
                pl.BlockSpec((1, valid, wide), lambda i, p: (0, 0, 0)),
                pl.BlockSpec(memory_space=pl.ANY),
            ],
            out_specs=[out, out],
            scratch_shapes=[pltpu.VMEM((rows, wide), BF)],
        ),
        out_shape=[jax.ShapeDtypeStruct((size // 2, extent, wide), BF)] * 2,
        cost_estimate=pl.CostEstimate(
            flops=2 * rows * wide * ff, bytes_accessed=rows * ff * 4, transcendentals=0
        ),
        name="third_gradient",
    )(parity, activated, cotangent, token)


def feed_back_kernel(
    part, place_ref, fc2_ref, fc1_ref, late_out_ref, slope_ref, cot_ref, late_ref, gain_ref,
    du_ref, flat_ref, low_ref, mine_ref, sent_ref, bias_ref, sums_ref,
    total_ref, padded_ref, out_ref, residual_ref, sem_ref,
):
    step = pl.program_id(0)
    rows, wide = total_ref.shape
    group = mine_ref.shape[1]
    per = fc2_ref.shape[1] // wide

    first = per * wide if part else 0
    copies = (
        pltpu.make_async_copy(late_out_ref.at[:, first : first + wide], out_ref, sem_ref.at[0]),
        pltpu.make_async_copy(late_ref, residual_ref, sem_ref.at[1]),
    )

    @pl.when(step == 0)
    def _():
        for copy in copies:
            copy.start()
        fill_rows(padded_ref, cot_ref[0])
        total_ref[...] = jnp.zeros_like(total_ref)

    if part:
        for d in range(fc2_ref.shape[0] // part):
            for j in range(per):
                block = fc2_ref[d * part : (d + 1) * part, j * wide : (j + 1) * wide]
                flat_ref[(d * per + j) * part : (d * per + j + 1) * part, :] = block
    else:
        flat_ref[...] = fc2_ref[...]
    du = dot(padded_ref[...], flat_ref[...], 1, 1) * slope_ref[...].astype(F32)
    bias_ref[...] = jnp.sum(du, axis=0, keepdims=True)
    du = du.astype(BF)
    du_ref[...] = du
    total_ref[...] += dot(du, fc1_ref[...], 1, 1)

    @pl.when(step == pl.num_programs(0) - 1)
    def _():
        for copy in copies:
            copy.wait()
        tile = 64

        def body(i, sums):
            at = pl.ds(pl.multiple_of(i * tile, tile), tile)
            r = residual_ref[at, :]
            centered = r - jnp.mean(r, axis=-1, keepdims=True)
            inverse = lax.rsqrt(jnp.mean(centered * centered, axis=-1, keepdims=True) + EPSILON)
            normed = centered * inverse
            dh = total_ref[at, :]
            weighted = dh * gain_ref[...]
            first = jnp.mean(weighted, axis=-1, keepdims=True)
            second = jnp.mean(weighted * normed, axis=-1, keepdims=True)
            g = padded_ref[at, :].astype(F32)
            grad = g + inverse * (weighted - first - normed * second)
            low_ref[at, :] = grad.astype(BF)
            parts = (grad, dh * normed, dh, g)
            return tuple(s + jnp.sum(p, axis=0, keepdims=True) for s, p in zip(sums, parts, strict=True))

        zero = jnp.zeros((1, wide), F32)
        sums = lax.fori_loop(0, rows // tile, body, (zero,) * 4)
        sums_ref[...] = jnp.concatenate(sums + (jnp.zeros((4, wide), F32),), axis=0)
        here = place_ref[0]
        mine = out_ref[pl.ds(pl.multiple_of(here * group, 128), group), :]
        other = out_ref[pl.ds(pl.multiple_of(group - here * group, 128), group), :]
        sent_ref[...] = dot(low_ref[...], other, 1, 1).astype(BF)
        mine_ref[...] = dot(low_ref[...], mine, 1, 1).astype(BF)


def feed_back(here, weights, slope, cotangent, residual, gain, part):
    rows, ff = slope.shape
    _, valid, wide = cotangent.shape
    group = wide // 2
    per = ff // wide
    if part % 16:
        part = 0
        fc2, fc1, out = weights
        fc2_spec = pl.BlockSpec((wide, wide), lambda i, p: (i, 0))
        fc1_spec = pl.BlockSpec((wide, wide), lambda i, p: (0, i))
    else:
        fc2 = fc1 = out = weights
        fc2_spec = pl.BlockSpec((wide // per, ff), lambda i, p: (i, 0))
        fc1_spec = pl.BlockSpec((wide, wide), lambda i, p: (0, per + 1 + i))

    def fixed(*shape):
        return pl.BlockSpec(shape, lambda i, p: tuple(0 for _ in shape))

    block = pl.BlockSpec((rows, wide), lambda i, p: (0, i))
    return pl.pallas_call(
        functools.partial(feed_back_kernel, part),
        grid_spec=pltpu.PrefetchScalarGridSpec(
            num_scalar_prefetch=1,
            grid=(per,),
            in_specs=[
                fc2_spec, fc1_spec, pl.BlockSpec(memory_space=pl.ANY), block,
                fixed(1, valid, wide), pl.BlockSpec(memory_space=pl.ANY), fixed(1, wide),
            ],
            out_specs=[
                block, pl.BlockSpec((wide, wide), lambda i, p: (i, 0)),
                fixed(rows, wide), fixed(rows, group), fixed(rows, group),
                pl.BlockSpec((1, wide), lambda i, p: (0, i)), fixed(8, wide),
            ],
            scratch_shapes=[
                pltpu.VMEM((rows, wide), F32),
                pltpu.VMEM((rows, wide), BF),
                pltpu.VMEM((wide, wide), BF),
                pltpu.VMEM((rows, wide), F32),
                pltpu.SemaphoreType.DMA((2,)),
            ],
        ),
        out_shape=[
            jax.ShapeDtypeStruct((rows, ff), BF),
            jax.ShapeDtypeStruct((ff, wide), BF),
            jax.ShapeDtypeStruct((rows, wide), BF),
            jax.ShapeDtypeStruct((rows, group), BF),
            jax.ShapeDtypeStruct((rows, group), BF),
            jax.ShapeDtypeStruct((1, ff), F32),
            jax.ShapeDtypeStruct((8, wide), F32),
        ],
        cost_estimate=pl.CostEstimate(
            flops=4 * rows * wide * ff, bytes_accessed=ff * wide * 10, transcendentals=rows
        ),
        name="feed_back",
    )(here, fc2, fc1, out, slope, cotangent, residual, gain)


def finish_kernel(spans, place_ref, mine_ref, theirs_ref, w_ref, *refs):
    here = place_ref[0]
    group = w_ref.shape[1] // 6
    mine, theirs = mine_ref[...].astype(F32), theirs_ref[...].astype(F32)
    for j in range(3):
        part = slice(j * group, (j + 1) * group)
        at = (2 * j * group) + here * group
        w_ref[:, pl.ds(pl.multiple_of(at, 128), group)] = mine[:, part]
        at = (2 * j + 1) * group - here * group
        w_ref[:, pl.ds(pl.multiple_of(at, 128), group)] = theirs[:, part]
    rows = (mine[:, 3 * group :] + theirs[:, 3 * group :]).T
    for (start, stop), ref in zip(spans, refs, strict=True):
        ref[...] = jnp.concatenate([rows[i : i + 1] for i in range(start, stop)], axis=1)


def finish(here, mine, theirs, spans):
    part, across = mine.shape
    width = 2 * (across - 128)

    def fixed(*shape):
        return pl.BlockSpec(shape, lambda i, p: (0, 0))

    sizes = [(1, (stop - start) * part) for start, stop in spans]
    return pl.pallas_call(
        functools.partial(finish_kernel, spans),
        grid_spec=pltpu.PrefetchScalarGridSpec(
            num_scalar_prefetch=1,
            grid=(1,),
            in_specs=[fixed(part, across)] * 2,
            out_specs=[fixed(part, width)] + [fixed(*shape) for shape in sizes],
        ),
        out_shape=[jax.ShapeDtypeStruct((part, width), F32)]
        + [jax.ShapeDtypeStruct(shape, F32) for shape in sizes],
        name="finish",
    )(here, mine, theirs)


def output_kernel(
    token_ref, z_ref, w_ref, late_ref, rows_ref, out_ref, total_ref, residual_ref, sem_ref
):
    step = pl.program_id(0)
    copy = pltpu.make_async_copy(late_ref, residual_ref, sem_ref)

    @pl.when(step == 0)
    def _():
        copy.start()
        total_ref[...] = jnp.zeros_like(total_ref)

    total_ref[...] += dot(z_ref[...], w_ref[...])

    @pl.when(step == pl.num_programs(0) - 1)
    def _():
        copy.wait()
        total = total_ref[...] + residual_ref[...] + rows_ref[-1:, :]
        out_ref[0] = total[: out_ref.shape[1], :].astype(BF)


def output_end(token, activated, w, residual, bias, valid):
    rows, ff = activated.shape
    wide = w.shape[1]
    return pl.pallas_call(
        output_kernel,
        grid=(ff // wide,),
        in_specs=[
            pl.BlockSpec(memory_space=pl.ANY),
            pl.BlockSpec((rows, wide), lambda i: (0, i)),
            pl.BlockSpec((wide, wide), lambda i: (i, 0)),
            pl.BlockSpec(memory_space=pl.ANY),
            pl.BlockSpec((1, wide), lambda i: (0, 0)),
        ],
        out_specs=pl.BlockSpec((1, valid, wide), lambda i: (0, 0, 0)),
        out_shape=jax.ShapeDtypeStruct((1, valid, wide), BF),
        scratch_shapes=[
            pltpu.VMEM((rows, wide), F32),
            pltpu.VMEM((rows, wide), F32),
            pltpu.SemaphoreType.DMA,
        ],
        cost_estimate=pl.CostEstimate(
            flops=2 * rows * wide * ff, bytes_accessed=rows * ff * 4, transcendentals=0
        ),
        name="output_end",
    )(token, activated, w, residual, bias)


def join_kernel(mine_ref, theirs_ref, out_ref, first_ref):
    wide = out_ref.shape[1]
    mine, theirs = mine_ref[...].astype(F32), theirs_ref[...].astype(F32)
    out_ref[...] = mine[:, :wide] + theirs[:, :wide]
    first_ref[...] = mine[:, wide:] + theirs[:, wide:]


def join_second(mine, theirs, wide):
    part, across = mine.shape
    return pl.pallas_call(
        join_kernel,
        out_shape=[
            jax.ShapeDtypeStruct((part, wide), F32),
            jax.ShapeDtypeStruct((part, across - wide), F32),
        ],
        name="join_second",
    )(mine, theirs)


def input_end_kernel(mine_ref, got_ref, residual_ref, normed_ref, gain_ref, inverse_ref, out_ref):
    normed = normed_ref[...]
    weighted = (mine_ref[...].astype(F32) + got_ref[...].astype(F32)) * gain_ref[...]
    first = jnp.mean(weighted, axis=-1, keepdims=True)
    second = jnp.mean(weighted * normed, axis=-1, keepdims=True)
    out_ref[:, 0, :] = residual_ref[...].astype(F32) + inverse_ref[:, 0:1] * (weighted - first - normed * second)


def input_end(mine, got, residual, normed, gain, inverse, valid):
    half, wide = mine.shape
    tile = 384
    block = pl.BlockSpec((tile, wide), lambda i: (i, 0))
    return pl.pallas_call(
        input_end_kernel,
        grid=(half // tile,),
        in_specs=[
            block, block, block, block, pl.BlockSpec((1, wide), lambda i: (0, 0)),
            pl.BlockSpec((tile, 128), lambda i: (i, 0)),
        ],
        out_specs=pl.BlockSpec((tile, 1, wide), lambda i: (i, 0, 0)),
        out_shape=jax.ShapeDtypeStruct((valid, 1, wide), F32),
        cost_estimate=pl.CostEstimate(
            flops=half * wide * 10, bytes_accessed=half * wide * 18, transcendentals=0
        ),
        name="input_end",
    )(mine, got, residual, normed, gain, inverse)


def swap(x, axis, size, bit):
    return lax.ppermute(x, axis, [(i, i ^ bit) for i in range(size)])


def bits_of(size):
    top = size // 4
    return top, [1 << b for b in range(top.bit_length() - 2, -1, -1)]


def gather_blocks(x, size):
    me = lax.axis_index("dp")
    top, bits = bits_of(size)
    held = jnp.stack([x] + [swap(x, "dp", size, j * top) for j in (1, 2, 3)])
    where = [j * top for j in range(4)]
    for bit in bits:
        held = jnp.concatenate([held, swap(held, "dp", size, bit)])
        where = where + [w ^ bit for w in where]
    place = [0] * size
    for i, w in enumerate(where):
        place[w] = i
    return held, jnp.asarray(place, jnp.int32)[me ^ jnp.arange(size)]


def halve(x, axis, bit):
    mine = lax.rem(lax.axis_index("dp") // bit, 2)
    keep = lax.dynamic_index_in_dim(x, mine, axis, keepdims=False)
    give = lax.dynamic_index_in_dim(x, 1 - mine, axis, keepdims=False)
    return keep, give.astype(BF)


def scatter_split(x, size):
    top, _ = bits_of(size)
    mine = lax.axis_index("dp") // top
    gives = [
        lax.dynamic_index_in_dim(x, mine ^ j, 0, keepdims=False).astype(BF) for j in (1, 2, 3)
    ]
    return gives, lax.dynamic_index_in_dim(x, mine, 0, keepdims=False).astype(F32)


def scatter_join(total, gives, size):
    top, _ = bits_of(size)
    for j, give in zip((1, 2, 3), gives, strict=True):
        total = total + swap(give, "dp", size, j * top).astype(F32)
    return total


def after(x, *others):
    return lax.optimization_barrier((x, *others))[0]


def gelu_cdf(values):
    return 0.5 * (1.0 + lax.erf(values * (1.0 / math.sqrt(2.0))))


def layer(
    size, frames_in, ln1_gain, ln1_bias, w_qkv, b_qv, w_o, b_o,
    ln2_gain, ln2_bias, w_fc1, b_fc1, w_fc2, b_fc2, cotangent,
):
    clips, valid, wide = frames_in.shape
    assert clips == 1
    ff = w_fc1.shape[1]
    part = w_qkv.shape[0]
    group = wide // 2
    half = -(-valid // 256) * 256
    here = lax.axis_index("seq")

    def other(x):
        return swap(x, "seq", 2, 1)

    def pick(x, axis, index):
        return lax.dynamic_index_in_dim(x, index, axis, keepdims=False)

    per = ff // wide
    me = lax.axis_index("dp")
    _, bits = bits_of(size)

    vectors = jnp.concatenate([ln1_gain, ln1_bias, b_qv, b_o, ln2_gain, ln2_bias, b_fc1, b_fc2])
    count = vectors.shape[0] // part
    columns = lax.optimization_barrier(
        jnp.pad(vectors.reshape(count, part).T, ((0, 0), (0, 128 - count)))
    )
    w_mine = [
        lax.dynamic_slice_in_dim(w_qkv, j * wide + here * group, group, axis=1) for j in range(3)
    ]
    held, place = gather_blocks(jnp.concatenate(w_mine + [columns], axis=1), size)
    if part % 16:
        held = jnp.take(held, place, axis=0, mode="clip").reshape(1, wide, 3 * group + 128)
        place = jnp.zeros((1,), jnp.int32)
    place = jnp.concatenate([place, jnp.full((1,), here, jnp.int32)])
    if part % 16:
        fc2_local = w_fc2.reshape(per, part, wide).transpose(1, 0, 2).reshape(part, ff)
        packed = jnp.concatenate([fc2_local, w_o, w_fc1], axis=1)
    else:
        packed = pack(w_fc2, w_o, w_fc1)
    later = lax.all_gather(packed, "dp", axis=0, tiled=True)
    out_full, fc1_full = later[:, ff : ff + wide], later[:, ff + wide :]
    weights = later
    if part % 16:
        fc2_full = later[:, :ff].reshape(size, part, per, wide)
        weights = (fc2_full.transpose(0, 2, 1, 3).reshape(ff, wide), fc1_full, out_full)

    prepared = prepare(frames_in, half, 0)
    inverse_one = prepared[2]
    normed_both, normed_t, _ = prepare(other(frames_in), half, 1, prepared[:2])
    qkv, w_full, w_flipped, table, scale = projection(held, place, normed_both, part)

    def vector(start, stop):
        return table[start:stop].reshape(-1, size, part).transpose(1, 0, 2).reshape(-1)

    gain_one, gain_two = table[0], table[5]
    bias_fc1, bias_fc2 = vector(7, 7 + per), table[7 + per]
    o_mine, o_sent, lse = attention_forward(qkv, half, valid)
    o_got = other(o_sent)
    flag = jnp.full((1,), here, jnp.int32)
    if part % 16:
        residual, hidden_two = attend(flag, frames_in, o_mine, o_got, out_full, 0, table)
    else:
        residual, hidden_two = attend(flag, frames_in, o_mine, o_got, later, per, table)

    pre_act = dot(hidden_two, fc1_full) + bias_fc1
    cdf = gelu_cdf(pre_act)
    density = jnp.exp(-0.5 * pre_act * pre_act) * (1.0 / math.sqrt(2.0 * math.pi))
    activated, slope = lax.optimization_barrier(
        ((pre_act * cdf).astype(BF), (cdf + pre_act * density).astype(BF))
    )
    (
        grad_pre_low, fc2_full, grad_residual_low,
        do_mine, do_sent, grad_bias_fc1, grad_sums,
    ) = feed_back(flag, weights, slope, cotangent, residual, gain_two[None], part)
    do_got = other(do_sent)
    parity = jnp.full((1,), lax.rem(me, 2), jnp.int32)
    fc2_keep, fc2_give = third_gradient(parity, activated, cotangent, size, do_sent)
    second_part = second_gradient(
        flag, fc2_give, o_mine, o_got, grad_residual_low, hidden_two, grad_pre_low
    )
    grad_second = lax.psum_scatter(second_part, "dp", scatter_dimension=0, tiled=True)

    def backward(token, start, count):
        return attention_backward(
            qkv, o_mine, o_sent, do_mine, do_got, lse, token, half, valid, start, count
        )

    x = fc2_keep.astype(F32) + swap(fc2_give, "dp", size, 1).astype(F32)
    x = x.reshape(size // 2, 2, -1, wide)
    keep, give = pick(x, 1, here).astype(BF), pick(x, 1, 1 - here).astype(BF)
    got = other(give)
    ds = [backward(give, 0, group // 128)]
    grad_other = projection_input_gradient(w_flipped, ds, ds[0], half, 1, BF)
    grad_got = other(grad_other)
    for at in range(len(bits) - 2, -1, -1):
        x = after(keep, grad_other).astype(F32) + got.astype(F32)
        keep, give = halve(x.reshape(-1, 2, *x.shape[1:]), 1, bits[at])
        keep, got = keep.astype(BF), swap(give, "dp", size, bits[at])
    fc2_keep_x, fc2_got_x = keep, got

    vectors = [(7, grad_bias_fc1)]
    if part % 16:
        grad_qkv, norm_sums, sums = projection_weight_gradient(normed_t, w_full, scale, ds)
        grad_bias_mine = jnp.stack([sums[0, :group], sums[0, 2 * group :]])
        zero = jnp.zeros_like(grad_bias_mine)
        grad_bias_qv = jnp.where(
            here == 0,
            jnp.concatenate([grad_bias_mine, zero], axis=1),
            jnp.concatenate([zero, grad_bias_mine], axis=1),
        )

        def as_columns(start, v):
            v = v.reshape(size, -1, part).transpose(0, 2, 1)
            return jnp.pad(v, ((0, 0), (0, 0), (start, 128 - start - v.shape[2])))

        columns = norm_sums.reshape(size, part, 128) + as_columns(2, grad_bias_qv)
        vectors += [(p, grad_sums[i]) for i, p in enumerate((4, 5, 6, 7 + per))]
        columns = columns + sum(as_columns(start, v) for start, v in vectors)
        x = jnp.concatenate([grad_qkv.reshape(size, part, -1), columns.astype(BF)], axis=2)
        keep, give = halve(x.reshape(size // 2, 2, *x.shape[1:]), 1, 1)
    else:
        sides = jnp.concatenate([parity, jnp.full((1,), here, jnp.int32)])
        keep, give = spread_weight_gradient(
            sides, give, normed_t, w_full, scale, ds, grad_bias_fc1, grad_sums, part
        )
    got = swap(give, "dp", size, 1)
    for at in range(len(bits) - 2, -1, -1):
        x = keep.astype(F32) + got.astype(F32)
        keep, give = halve(x.reshape(-1, 2, *x.shape[1:]), 1, bits[at])
        got = swap(give, "dp", size, bits[at])
    fc2_keep, fc2_got = after((fc2_keep_x, fc2_got_x), give)
    fc2_gives, fc2_stay = scatter_split(fc2_keep.astype(F32) + fc2_got.astype(F32), size)
    grad_mine = projection_input_gradient(w_flipped, ds, fc2_gives[2], half, 0, BF)
    frames_out = output_end(
        fc2_gives[2], activated, fc2_full, residual, bias_fc2[None], valid
    )
    fc2_part = scatter_join(fc2_stay, fc2_gives, size).astype(BF)
    gives, stay = scatter_split(keep.astype(F32) + got.astype(F32), size)
    grad_input = input_end(
        grad_mine, grad_got, grad_residual_low, normed_both, gain_one[None], inverse_one, valid
    ).transpose(1, 0, 2)
    mine = scatter_join(stay, gives, size).astype(BF)
    theirs = other(mine)
    spans = ((0, 1), (1, 2), (2, 4), (4, 5), (5, 6), (6, 7), (7, 7 + per), (7 + per, 8 + per))
    grad_w_qkv, *small = finish(flag, mine, theirs, spans)
    small = [v[0] for v in small]
    fc2_got = other(fc2_part)
    fc2_sum = jnp.where(
        here == 0,
        jnp.concatenate([fc2_part, fc2_got], axis=0),
        jnp.concatenate([fc2_got, fc2_part], axis=0),
    ).astype(F32)
    out_sum, first_sum = join_second(grad_second, other(grad_second), wide)
    return (
        frames_out, grad_input, small[0], small[1], grad_w_qkv, small[2], out_sum, small[3],
        small[4], small[5], first_sum, small[6], fc2_sum, small[7],
    )


def solution(mesh):
    frames, rows, vector = P("dp", "seq", None), P("dp", None), P("dp")
    in_specs = (
        frames, vector, vector, rows, vector, rows, vector,
        vector, vector, rows, vector, rows, vector, frames,
    )
    out_specs = (
        frames, frames, vector, vector, rows, vector, rows, vector,
        vector, vector, rows, vector, rows, vector,
    )
    return jax.shard_map(
        functools.partial(layer, mesh.shape["dp"]),
        mesh=mesh, in_specs=in_specs, out_specs=out_specs, check_vma=False,
    )
```
